32 devices in a mesh: sensor: 2 (over y), tm: 16 (over z, x, core).
Axes of the slice: x: 2, y: 2, z: 4, core: 2. Of those that a mesh axis runs over, the one named last changes fastest.
Arguments:
- recording: bfloat16 [256, 16384], P('sensor', 'tm'), may hold values from -6 to 6
- spatial_w: bfloat16 [512, 256], P(None, 'sensor'), may hold values from -0.375 to 0.375
- conv_w: bfloat16 [3, 3, 512, 512], P(None, None, 'sensor'), may hold values from -0.15625 to 0.15625
- conv_b: float32 [3, 512], P(None, 'sensor'), may hold values from -3 to 3
- dilations: int32 [3], replicated, may hold values from 1 to 16, as said below
- valid_frames: int32 [16], P('tm'), may hold values from 512 to 1024, as said below
- key_w: bfloat16 [512, 512], P('sensor'), may hold values from -0.25 to 0.25
- value_w: bfloat16 [512, 512], P('sensor'), may hold values from -0.25 to 0.25
- queries: bfloat16 [512, 2048], P('sensor'), may hold values from -60 to 60
Outputs:
- features: bfloat16 [512, 16384], P('sensor', 'tm')
- attended: bfloat16 [512, 2048], P('sensor')
The draws below stay inside these ranges and needn't reach their ends.
Inputs may be any that keep to these rules, and one draw needn't show every extreme that they name: `dilations`: one layer has dilation exactly 16 and another exactly 1. `valid_frames`: one block is full and one holds exactly half of its 1024 frames.
All inputs are finite; a program needn't handle non-finite values.
Results may differ from the reference program's by a relative error of at most 0.015.
The reference program's roundings to bfloat16 on the way count: a program that leaves them out, or rounds other values in their place, can miss the bound.
Values may be sent and summed in bfloat16 or wider, within the bound.
No kernel may reach another device: no remote copies, remote signals or barrier semaphores. Data moves between devices by JAX's collectives and lax.ppermute only.
A program may use at most 64 MiB of HBM per device.

```python
import math
import jax
import jax.numpy as jnp
from jax import lax

SENSORS = 256
CH = 512
LATW = 512
HD = 64
LATENTS = 2048
LAYERS = 3
DMAX = 16
F_DEV = 1024
FRAMES = 16384
BLOCKS = 16
HEADS = 8


def draw_dilations(key, part):
    ranking = jax.random.permutation(jax.random.fold_in(key, 11), LAYERS)
    baseline = jax.random.randint(jax.random.fold_in(key, 12), (LAYERS,), 1, DMAX + 1)
    return baseline.at[ranking[0]].set(DMAX).at[ranking[1]].set(1).astype(jnp.int32)


def draw_valid_frames(key, part):
    ranking = jax.random.permutation(jax.random.fold_in(key, 21), BLOCKS)
    baseline = jax.random.randint(jax.random.fold_in(key, 22), (BLOCKS,), F_DEV // 2, F_DEV + 1)
    return baseline.at[ranking[0]].set(F_DEV).at[ranking[1]].set(F_DEV // 2).astype(jnp.int32)


def draw_queries(key, part):
    values = jnp.clip(3.0 * jax.random.normal(jax.random.fold_in(key, 34), (LATW, LATENTS)), -12.0, 12.0)
    return values.astype(jnp.bfloat16)


def steps_of(rng, extent, split, low, largest):
    level = 1.0
    for position, parts in split:
        heights = jax.random.uniform(jax.random.fold_in(jax.random.fold_in(rng, 6), position), (parts,), jnp.float32, low / len(split), largest / len(split))
        level = level * jnp.repeat(jnp.exp(heights), extent[position] // parts).reshape((-1,) + (1,) * (len(extent) - 1 - position))
    return level


def scatter_about(key, extent, spread, bound, shards=(), kind=jnp.bfloat16):
    drawn = spread * jax.random.normal(key, extent, jnp.float32)
    if shards:
        drawn = drawn * steps_of(key, extent, shards, -0.22, 0.18)
    return jnp.clip(drawn, -bound, bound).astype(kind)


def setup_inputs(seed: int = 0) -> dict:
    keys = jax.random.split(jax.random.key(seed), 10)
    return {
        "recording": scatter_about(keys[0], (SENSORS, FRAMES), 1.0, 6.0, ((0, 2), (1, 16))),
        "spatial_w": scatter_about(keys[1], (CH, SENSORS), SENSORS ** -0.5, 0.375, ((1, 2),)),
        "conv_w": scatter_about(keys[2], (LAYERS, 3, CH, CH), (3 * CH) ** -0.5, 0.15625, ((2, 2),)),
        "conv_b": scatter_about(keys[3], (LAYERS, CH), 0.5, 3.0, ((1, 2),), jnp.float32),
        "dilations": draw_dilations(jax.random.fold_in(keys[9], 71), 0),
        "valid_frames": draw_valid_frames(jax.random.fold_in(keys[9], 71), 0),
        "key_w": scatter_about(keys[6], (LATW, CH), CH ** -0.5, 0.25, ((0, 2),)),
        "value_w": scatter_about(keys[7], (LATW, CH), CH ** -0.5, 0.25, ((0, 2),)),
        "queries": draw_queries(jax.random.fold_in(keys[9], 71), 0),
    }


def reference(recording, spatial_w, conv_w, conv_b, dilations, valid_frames, key_w, value_w, queries):
    hidden = jnp.dot(spatial_w, recording, preferred_element_type=jnp.float32).astype(jnp.bfloat16)
    for layer in range(LAYERS):
        dilation = dilations[layer]
        padded = jnp.pad(hidden, ((0, 0), (DMAX, DMAX)))
        preact = jnp.broadcast_to(conv_b[layer][:, None], (CH, FRAMES)).astype(jnp.float32)
        for tap_index in range(3):
            offset = (DMAX + (tap_index - 1) * dilation).astype(jnp.int32)
            shifted = lax.dynamic_slice_in_dim(padded, offset, FRAMES, 1)
            preact = preact + jnp.dot(conv_w[layer, tap_index], shifted, preferred_element_type=jnp.float32)
        hidden = (hidden.astype(jnp.float32) + jax.nn.gelu(preact, approximate=False)).astype(jnp.bfloat16)
    features = hidden
    key_rows = jnp.dot(key_w, features, preferred_element_type=jnp.float32).astype(jnp.bfloat16)
    value_rows = jnp.dot(value_w, features, preferred_element_type=jnp.float32).astype(jnp.bfloat16)
    frame_mask = jnp.arange(FRAMES) % F_DEV < jnp.repeat(valid_frames, F_DEV)
    block_rows = min(LATENTS, 512)
    block_count = LATENTS // block_rows
    key_heads = key_rows.reshape(HEADS, HD, FRAMES)
    value_heads = value_rows.reshape(HEADS, HD, FRAMES)
    query_blocks = queries.reshape(HEADS, HD, block_count, block_rows).transpose(0, 2, 1, 3)
    query_blocks = query_blocks.reshape(HEADS * block_count, HD, block_rows)
    scale = 1.0 / math.sqrt(HD)

    def attend(index):
        head = index // block_count
        query_block = query_blocks[index]
        key_head = lax.dynamic_index_in_dim(key_heads, head, 0, keepdims=False)
        value_head = lax.dynamic_index_in_dim(value_heads, head, 0, keepdims=False)
        scores = jnp.dot(query_block.T, key_head, preferred_element_type=jnp.float32) * scale
        scores = jnp.where(frame_mask[None, :], scores, -jnp.inf)
        peaks = lax.optimization_barrier(jnp.max(scores, axis=1))
        probs = jnp.where(frame_mask[None, :], jnp.exp(scores - peaks[:, None]), 0.0)
        totals = lax.optimization_barrier(jnp.sum(probs, axis=1))
        weighted = jnp.dot(value_head, probs.astype(jnp.bfloat16).T, preferred_element_type=jnp.float32)
        return weighted / totals[None, :]
    outputs = lax.map(attend, jnp.arange(HEADS * block_count, dtype=jnp.int32))
    attended = outputs.reshape(HEADS, block_count, HD, block_rows).transpose(0, 2, 1, 3)
    attended = attended.reshape(LATW, LATENTS).astype(jnp.bfloat16)
    return (features, attended)
```

```python
import functools
import math

import jax
import jax.numpy as jnp
from jax import lax
from jax.experimental import pallas as pl
from jax.experimental.pallas import tpu as pltpu
from jax.sharding import PartitionSpec as P

HD = 64
LATENTS = 2048
LAYERS = 3
DMAX = 16


def padded(cells, sides, width):
    for axis, dim in sides:
        count = lax.axis_size(axis)
        ends = count - 1
        head = lax.slice_in_dim(cells, 0, width, axis=dim)
        tail = lax.slice_in_dim(cells, cells.shape[dim] - width, cells.shape[dim], axis=dim)
        cells = jnp.concatenate(
            [
                lax.ppermute(tail, axis, [(i, (i + 1) % count) for i in range(ends)]),
                cells,
                lax.ppermute(head, axis, [((i + 1) % count, i) for i in range(ends)]),
            ],
            axis=dim,
        )
    return cells


def tap_folder(kernels, dilation, frames, margin):

    def add_taps(running, portion, first_row):
        portion = jnp.pad(portion, ((0, 0), (margin, margin)))
        for tap_index in range(3):
            kernel = kernels[tap_index]
            offset = DMAX + (tap_index - 1) * dilation
            shifted = lax.dynamic_slice_in_dim(portion, offset, frames, 1)
            running = running + jnp.dot(kernel, shifted, preferred_element_type=jnp.float32)
        return running

    return add_taps


def generic_device(
    recording, spatial_w, conv_w, conv_b, dilations, valid_frames, key_w, value_w, queries
):
    frames = recording.shape[1]
    ch_loc = conv_w.shape[2]
    hidden = lax.psum_scatter(
        jnp.dot(spatial_w, recording, preferred_element_type=jnp.float32),
        "sensor",
        scatter_dimension=0,
        tiled=True,
    ).astype(jnp.bfloat16)
    reach = 3 * DMAX
    extended = padded(hidden, (("tm", 1),), reach)
    span = frames + 2 * reach
    position = lax.axis_index("tm") * frames - reach + jnp.arange(span, dtype=jnp.int32)
    inside = (position >= 0) & (position < frames * lax.axis_size("tm"))
    for layer in range(LAYERS):
        initial = jnp.broadcast_to(conv_b[layer][:, None], (ch_loc, span))
        folder = tap_folder(conv_w[layer], dilations[layer], span, DMAX)
        preact = folder(
            initial, lax.all_gather(extended, "sensor", axis=0, tiled=True), jnp.int32(0)
        )
        updated = extended.astype(jnp.float32) + jax.nn.gelu(preact, approximate=False)
        extended = jnp.where(inside[None, :], updated, 0.0).astype(jnp.bfloat16)
    hidden = extended[:, reach : reach + frames]
    portion = lax.all_gather(hidden, "sensor", axis=0, tiled=True)
    key_rows = jnp.dot(key_w, portion, preferred_element_type=jnp.float32)
    value_rows = jnp.dot(value_w, portion, preferred_element_type=jnp.float32)
    head_count = key_w.shape[0] // HD
    key_heads = key_rows.astype(jnp.bfloat16).reshape(head_count, HD, frames)
    value_heads = value_rows.astype(jnp.bfloat16).reshape(head_count, HD, frames)
    frame_mask = jnp.arange(frames, dtype=jnp.int32) < valid_frames[0]
    block_rows = min(LATENTS, 512)
    block_count = LATENTS // block_rows
    query_blocks = queries.reshape(head_count, HD, block_count, block_rows).transpose(2, 0, 1, 3)
    scale = 1.0 / math.sqrt(HD)

    def attend(query_block):
        scores = (
            jnp.einsum("hdq,hdt->hqt", query_block, key_heads, preferred_element_type=jnp.float32)
            * scale
        )
        scores = jnp.where(frame_mask[None, None, :], scores, -jnp.inf)
        peaks = jnp.max(scores, axis=2)
        probs = jnp.where(frame_mask[None, None, :], jnp.exp(scores - peaks[:, :, None]), 0.0)
        totals = jnp.sum(probs, axis=2)
        weighted = jnp.einsum(
            "hqt,hdt->hdq",
            probs.astype(jnp.bfloat16),
            value_heads,
            preferred_element_type=jnp.float32,
        )
        return (peaks, totals, weighted)

    peaks, totals, weighted = lax.map(attend, query_blocks)
    peaks = peaks.transpose(1, 0, 2).reshape(head_count, LATENTS)
    totals = totals.transpose(1, 0, 2).reshape(head_count, LATENTS)
    weighted = weighted.transpose(1, 2, 0, 3).reshape(head_count, HD, LATENTS)
    global_peaks = lax.pmax(peaks, "tm")
    rescale = jnp.exp(peaks - global_peaks)
    totals, weighted = lax.psum((totals * rescale, weighted * rescale[:, None, :]), "tm")
    attended = (
        (weighted / totals[:, None, :]).reshape(head_count * HD, LATENTS).astype(jnp.bfloat16)
    )
    return (hidden, attended)


VMEM = pltpu.VMEM
EDGE = 128
HALF = EDGE // 2
LOG2E = 1.4426950408889634
MASKED = -1e30


def whole(count):
    return [pl.BlockSpec(memory_space=pltpu.VMEM)] * count


def smem(count):
    return [pl.BlockSpec(memory_space=pltpu.SMEM)] * count


def params():
    return pltpu.CompilerParams(vmem_limit_bytes=56 * 1024 * 1024)


def dot(left, right):
    return jnp.dot(left, right, preferred_element_type=jnp.float32)


def first_kernel(own_w, other_w, own, other, own_edge, other_edge, out):
    frames = own.shape[1]
    out[:, :frames] = (dot(own_w[...], own[...]) + dot(other_w[...], other[...])).astype(out.dtype)
    out[:, frames:] = (
        dot(own_w[...], own_edge[...]) + dot(other_w[...], other_edge[...])
    ).astype(out.dtype)


def gelu(value):
    return 0.5 * value * (1.0 + lax.erf(value * (1.0 / math.sqrt(2.0))))


def conv_rows(shifted, hidden, kernel, bias, row, keep, store, cols, step):
    rows = kernel.shape[1]
    row = pl.multiple_of(row, rows)
    for start in range(0, cols, step):
        width = min(step, cols - start)
        here = pl.ds(start, width)
        total = dot(kernel[0], shifted[0, :, here])
        total = total + dot(kernel[1], hidden[:, here])
        total = total + dot(kernel[2], shifted[1, :, here])
        old = hidden[pl.ds(row, rows), here].astype(jnp.float32)
        new = old + gelu(total + bias[...])
        if keep is not None and start + width > cols - EDGE:
            new = jnp.where(keep(start, width), new, 0.0)
        store(row, rows, here, new.astype(jnp.bfloat16))


def spread(info, hidden, shifted):
    span = hidden.shape[1]
    wide = hidden[...].astype(jnp.float32)
    shifted[0] = pltpu.roll(wide, info[0], 1).astype(jnp.bfloat16)
    shifted[1] = pltpu.roll(wide, span - info[0], 1).astype(jnp.bfloat16)


def middle_kernel(info, hidden, own_w, near_w, far_w, own_b, near_b, far_b, out, shifted):
    span = hidden.shape[1]
    spread(info, hidden, shifted)

    def keep(start, width):
        lane = lax.broadcasted_iota(jnp.int32, (1, width), 1) + start
        frame = jnp.where(lane < span - HALF, lane, lane - span) + info[4]
        return (frame >= 0) & (frame < info[5])

    def store(row, rows, here, value):
        out[pl.ds(row, rows), here] = value

    for kernel, bias, row in ((own_w, own_b, info[1]), (near_w, near_b, info[2]), (far_w, far_b, info[3])):
        conv_rows(shifted, hidden, kernel, bias, row, keep, store, span, 384)


def last_kernel(
    info, hidden, own_w, near_w, far_w, own_b, near_b, far_b, key_w, value_w,
    features, key_keep, key_send, value_keep, value_send, shifted, full,
):
    frames = features.shape[1]
    spread(info, hidden, shifted)

    def store(row, rows, here, value):
        full[pl.ds(row, rows), here] = value

    for kernel, bias, row in ((own_w, own_b, info[1]), (near_w, near_b, info[2]), (far_w, far_b, info[3])):
        conv_rows(shifted, hidden, kernel, bias, row, None, store, frames, 256)
    rows = features.shape[0]
    features[...] = full[pl.ds(pl.multiple_of(info[1], rows), rows), :]
    half = rows // 2
    for key_out, value_out, row in ((key_keep, value_keep, info[6]), (key_send, value_send, info[7])):
        here = pl.ds(pl.multiple_of(row, half), half)
        key_out[...] = dot(key_w[here, :], full[...]).T.astype(jnp.bfloat16)
        value_out[...] = dot(value_w[here, :], full[...]).astype(jnp.bfloat16)


def thirds(value):
    first = value.astype(jnp.bfloat16)
    rest = value - first.astype(jnp.float32)
    second = rest.astype(jnp.bfloat16)
    third = (rest - second.astype(jnp.float32)).astype(jnp.bfloat16)
    return first, second, third


def pack(out, peak, total, weighted):
    out[0:HD, :] = weighted.astype(jnp.bfloat16)
    lines = [line.astype(jnp.float32) for line in thirds(peak) + thirds(total)]
    lines.append(jnp.zeros_like(lines[0]))
    lines.append(jnp.zeros_like(lines[0]))
    out[HD : HD + 8, :] = jnp.concatenate(lines, axis=0).astype(jnp.bfloat16)


def unpack(packed):
    lines = packed[HD : HD + 8, :].astype(jnp.float32)
    peak = lines[0:1] + (lines[1:2] + lines[2:3])
    total = lines[3:4] + (lines[4:5] + lines[5:6])
    return peak, total, packed[0:HD, :].astype(jnp.float32)


SCALE = LOG2E / math.sqrt(HD)


def join(one, two):
    peak = jnp.maximum(one[0], two[0])
    left = jnp.exp2((one[0] - peak) * SCALE)
    right = jnp.exp2((two[0] - peak) * SCALE)
    return peak, one[1] * left + two[1] * right, one[2] * left + two[2] * right


def ordered(info, mine, theirs):
    swap = info[0] == 1
    one = tuple(jnp.where(swap, t, m) for m, t in zip(mine, theirs))
    two = tuple(jnp.where(swap, m, t) for m, t in zip(mine, theirs))
    return one, two


def meet_kernel(peak, total, weighted, theirs, out):
    pack(out, *join((peak[...], total[...], weighted[...]), unpack(theirs)))


def merge_kernel(info, mine, theirs, out):
    pack(out, *join(*ordered(info, unpack(mine), unpack(theirs))))


def finish_kernel(info, mine, theirs, out):
    peak, total, weighted = join(*ordered(info, unpack(mine), unpack(theirs)))
    out[...] = (weighted / total).astype(out.dtype)


def divide_kernel(mine, out):
    peak, total, weighted = unpack(mine)
    out[...] = (weighted / total).astype(out.dtype)


def attend_kernel(
    packed, info, key_own, key_rec, value_own, value_rec, queries, *refs
):
    outs = refs[:-6]
    keyed, asked, score_a, score_b, peak_a, peak_b = refs[-6:]
    frames = key_own.shape[0]
    latents = queries.shape[1]
    tile = score_a.shape[1]
    chunk = 256
    slot = info[0]
    lane = lax.broadcasted_iota(jnp.int32, (frames, 2 * HD), 1)
    frame = lax.broadcasted_iota(jnp.int32, (frames, 2 * HD), 0)
    spare = (1 - slot) * HD
    for part, source in enumerate((key_own, key_rec)):
        bias = jnp.where(frame < info[1 + part], 0.0, MASKED)
        keyed[pl.ds(part * frames, frames), :] = jnp.where(
            lane == spare, bias, source[...].astype(jnp.float32)
        ).astype(jnp.bfloat16)
    row = lax.broadcasted_iota(jnp.int32, (2 * HD, latents), 0)
    wide = queries[...].astype(jnp.float32)
    wide = jnp.where(row // HD == slot, wide, jnp.where(row == spare, 1.0, 0.0))
    asked[...] = wide.astype(jnp.bfloat16)
    value_rows = pl.ds(pl.multiple_of(slot * HD, HD), HD)

    def score(index, scores, peaks):
        cols = pl.ds(pl.multiple_of(index * tile, tile), tile)
        peak = None
        for start in range(0, 2 * frames, chunk):
            here = pl.ds(start, chunk)
            value = dot(keyed[here, :], asked[:, cols])
            scores[here, :] = value
            top = jnp.max(value.reshape(chunk // 8, 8, tile), axis=0)
            peak = top if peak is None else jnp.maximum(peak, top)
        peaks[...] = jnp.max(peak, axis=0, keepdims=True)

    def weigh(index, scores, peaks):
        cols = pl.ds(pl.multiple_of(index * tile, tile), tile)
        peak = peaks[...]
        total = None
        weighted = None
        for start in range(0, 2 * frames, chunk):
            probs = jnp.exp2((scores[pl.ds(start, chunk), :] - peak) * SCALE)
            part = jnp.sum(probs.reshape(chunk // 8, 8, tile), axis=0)
            total = part if total is None else total + part
            source, offset = (value_own, start) if start < frames else (value_rec, start - frames)
            values = source[value_rows, pl.ds(offset, chunk)]
            term = dot(values, probs.astype(jnp.bfloat16))
            weighted = term if weighted is None else weighted + term
        total = jnp.sum(total, axis=0, keepdims=True)
        if packed:
            pack(outs[0].at[:, cols], peak, total, weighted)
        else:
            outs[0][:, cols] = peak
            outs[1][:, cols] = total
            outs[2][:, cols] = weighted

    count = latents // tile
    score(0, score_a, peak_a)

    @pl.loop(0, count // 2)
    def _(step):
        score(2 * step + 1, score_b, peak_b)
        weigh(2 * step, score_a, peak_a)
        score(jnp.minimum(2 * step + 2, count - 1), score_a, peak_a)
        weigh(2 * step + 1, score_b, peak_b)


def attend(packed, info, keys, values, queries):
    latents = queries.shape[1]
    frames = keys[0].shape[0]
    tile = min(256, latents // 2)
    if packed:
        out_shape = jax.ShapeDtypeStruct((HD + 8, latents), jnp.bfloat16)
        out_specs = pl.BlockSpec(memory_space=pltpu.VMEM)
    else:
        out_shape = [
            jax.ShapeDtypeStruct((1, latents), jnp.float32),
            jax.ShapeDtypeStruct((1, latents), jnp.float32),
            jax.ShapeDtypeStruct((HD, latents), jnp.float32),
        ]
        out_specs = whole(3)
    return pl.pallas_call(
        functools.partial(attend_kernel, packed),
        out_shape=out_shape,
        in_specs=smem(1) + whole(5),
        out_specs=out_specs,
        scratch_shapes=[
            VMEM((2 * frames, 2 * HD), jnp.bfloat16),
            VMEM((2 * HD, latents), jnp.bfloat16),
            VMEM((2 * frames, tile), jnp.float32),
            VMEM((2 * frames, tile), jnp.float32),
            VMEM((1, tile), jnp.float32),
            VMEM((1, tile), jnp.float32),
        ],
        compiler_params=params(),
        name="attend_send" if packed else "attend_keep",
    )(info, *keys, *values, queries)


def assemble_kernel(info, own, across, core_own, core_across, out):
    for piece, index in ((own, 0), (across, 1), (core_own, 2), (core_across, 3)):
        out[pl.ds(pl.multiple_of(info[index] * HD, HD), HD), :] = piece[...]


def swap(value, axis, bit):
    return lax.ppermute(value, axis, [(i, i ^ bit) for i in range(lax.axis_size(axis))])


def simple(kernel, out_shape, scalars, arrays, scratch=(), name=None):
    many = isinstance(out_shape, (list, tuple))
    return pl.pallas_call(
        kernel,
        out_shape=out_shape,
        in_specs=smem(len(scalars)) + whole(len(arrays)),
        out_specs=whole(len(out_shape)) if many else pl.BlockSpec(memory_space=pltpu.VMEM),
        scratch_shapes=list(scratch),
        compiler_params=params(),
        name=name,
    )(*scalars, *arrays)


def pair_device(
    recording, spatial_w, conv_w, conv_b, dilations, valid_frames, key_w, value_w, queries
):
    frames = recording.shape[1]
    ch_loc = conv_w.shape[2]
    ch = conv_w.shape[3]
    half = ch_loc // 2
    latents = queries.shape[1]
    blocks = lax.axis_size("tm")
    side = lax.axis_index("sensor")
    place = lax.axis_index("tm")
    core = place & 1
    cross = (place >> 1) & 1
    span = frames + EDGE
    bf16 = jnp.bfloat16

    other_rec = swap(recording, "sensor", 1)
    other_w = swap(spatial_w, "sensor", 1)
    tail = lax.ppermute(
        recording[:, frames - EDGE :], "tm", [(i, i + 1) for i in range(blocks - 1)]
    )
    head = lax.ppermute(recording[:, :EDGE], "tm", [(i + 1, i) for i in range(blocks - 1)])
    lane = jnp.arange(EDGE, dtype=jnp.int32)[None, :]
    edge = jnp.where(lane < HALF, head, tail)
    other_edge = swap(edge, "sensor", 1)
    mine = lax.dynamic_slice_in_dim(conv_w, core * half, half, axis=2)
    near = [swap(mine[layer], "sensor", 1) for layer in range(LAYERS)]
    far = [swap(near[layer], "tm", 1) for layer in range(LAYERS)]
    other_b = swap(conv_b, "sensor", 1)
    near_b = lax.dynamic_slice_in_dim(other_b, core * half, half, axis=1)
    far_b = lax.dynamic_slice_in_dim(other_b, (1 - core) * half, half, axis=1)
    other_valid = swap(valid_frames, "tm", 1)

    hidden = simple(
        first_kernel,
        jax.ShapeDtypeStruct((ch, span), bf16),
        (),
        (spatial_w, other_w, recording, other_rec, edge, other_edge),
        name="first",
    )
    row_own = side * ch_loc
    row_near = (1 - side) * ch_loc + core * half
    row_far = (1 - side) * ch_loc + (1 - core) * half
    for layer in range(LAYERS):
        info = jnp.stack(
            [
                dilations[layer], row_own, row_near, row_far, place * frames, blocks * frames,
                core * half, (1 - core) * half,
            ]
        ).astype(jnp.int32)
        arrays = (
            hidden, conv_w[layer], near[layer], far[layer],
            conv_b[layer][:, None], near_b[layer][:, None], far_b[layer][:, None],
        )
        scratch = [VMEM((2, ch, span), bf16)]
        if layer < LAYERS - 1:
            hidden = simple(
                middle_kernel, jax.ShapeDtypeStruct((ch, span), bf16), (info,), arrays, scratch,
                name="conv",
            )
        else:
            shapes = [
                jax.ShapeDtypeStruct((ch_loc, frames), bf16),
                jax.ShapeDtypeStruct((frames, half), bf16),
                jax.ShapeDtypeStruct((frames, half), bf16),
                jax.ShapeDtypeStruct((half, frames), bf16),
                jax.ShapeDtypeStruct((half, frames), bf16),
            ]
            features, key_keep, key_send, value_keep, value_send = simple(
                last_kernel, shapes, (info,), arrays + (key_w, value_w),
                scratch + [VMEM((ch, frames), bf16)], name="conv_last",
            )
    keys = (key_keep, swap(key_send, "tm", 1))
    values = (value_keep, swap(value_send, "tm", 1))
    asked = lax.dynamic_slice_in_dim(queries, core * half, half, axis=0)

    def facts(slot):
        return jnp.stack([slot, valid_frames[0], other_valid[0]]).astype(jnp.int32)

    sent = attend(True, facts(1 - cross), keys, values, asked)
    arrived = swap(sent, "tm", 2)
    peak, total, weighted = attend(False, facts(cross), keys, values, asked)
    packed_shape = jax.ShapeDtypeStruct((HD + 8, latents), bf16)
    final_shape = jax.ShapeDtypeStruct((HD, latents), bf16)
    packed = simple(meet_kernel, packed_shape, (), (peak, total, weighted, arrived), name="meet")
    if blocks == 4:
        done = simple(divide_kernel, final_shape, (), (packed,), name="divide")
    bit = 4
    while bit < blocks:
        theirs = swap(packed, "tm", bit)
        which = ((place & bit) != 0).astype(jnp.int32)[None]
        if bit * 2 < blocks:
            packed = simple(merge_kernel, packed_shape, (which,), (packed, theirs), name="merge")
        else:
            done = simple(finish_kernel, final_shape, (which,), (packed, theirs), name="finish")
        bit *= 2
    across = swap(done, "tm", 2)
    core_done = swap(done, "tm", 1)
    core_across = swap(across, "tm", 1)
    spots = jnp.stack(
        [
            2 * core + cross, 2 * core + 1 - cross, 2 * (1 - core) + cross,
            2 * (1 - core) + 1 - cross,
        ]
    ).astype(jnp.int32)
    attended = simple(
        assemble_kernel, jax.ShapeDtypeStruct((ch_loc, latents), bf16), (spots,),
        (done, across, core_done, core_across), name="assemble",
    )
    return (features, attended)


def fits(mesh):
    sensors, blocks = mesh.shape["sensor"], mesh.shape["tm"]
    return sensors == 2 and blocks >= 4 and blocks & (blocks - 1) == 0


def on_device(*arrays):
    heads = arrays[6].shape[0] // HD
    if lax.axis_size("sensor") == 2 and heads == 4:
        return pair_device(*arrays)
    return generic_device(*arrays)


def solution(mesh):
    return jax.shard_map(
        on_device if fits(mesh) else generic_device,
        mesh=mesh,
        in_specs=(
            P("sensor", "tm"),
            P(None, "sensor"),
            P(None, None, "sensor", None),
            P(None, "sensor"),
            P(),
            P("tm"),
            P("sensor", None),
            P("sensor", None),
            P("sensor", None),
        ),
        out_specs=(P("sensor", "tm"), P("sensor", None)),
        check_vma=False,
    )
```

```python
import functools
import math

import jax
import jax.numpy as jnp
from jax import lax
from jax.experimental import pallas as pl
from jax.experimental.pallas import tpu as pltpu
from jax.sharding import PartitionSpec as P


HD = 64
LATENTS = 2048
LAYERS = 3
DMAX = 16


def padded(cells, sides, width):
    for axis, dim in sides:
        count = lax.axis_size(axis)
        ends = count - 1
        head = lax.slice_in_dim(cells, 0, width, axis=dim)
        tail = lax.slice_in_dim(cells, cells.shape[dim] - width, cells.shape[dim], axis=dim)
        cells = jnp.concatenate(
            [
                lax.ppermute(tail, axis, [(i, (i + 1) % count) for i in range(ends)]),
                cells,
                lax.ppermute(head, axis, [((i + 1) % count, i) for i in range(ends)]),
            ],
            axis=dim,
        )
    return cells


def tap_folder(kernels, dilation, frames, margin):

    def add_taps(running, portion, first_row):
        portion = jnp.pad(portion, ((0, 0), (margin, margin)))
        for tap_index in range(3):
            kernel = kernels[tap_index]
            offset = DMAX + (tap_index - 1) * dilation
            shifted = lax.dynamic_slice_in_dim(portion, offset, frames, 1)
            running = running + jnp.dot(kernel, shifted, preferred_element_type=jnp.float32)
        return running

    return add_taps


def generic_device(
    recording, spatial_w, conv_w, conv_b, dilations, valid_frames, key_w, value_w, queries
):
    frames = recording.shape[1]
    ch_loc = conv_w.shape[2]
    hidden = lax.psum_scatter(
        jnp.dot(spatial_w, recording, preferred_element_type=jnp.float32),
        "sensor",
        scatter_dimension=0,
        tiled=True,
    ).astype(jnp.bfloat16)
    reach = 3 * DMAX
    extended = padded(hidden, (("tm", 1),), reach)
    span = frames + 2 * reach
    position = lax.axis_index("tm") * frames - reach + jnp.arange(span, dtype=jnp.int32)
    inside = (position >= 0) & (position < frames * lax.axis_size("tm"))
    for layer in range(LAYERS):
        initial = jnp.broadcast_to(conv_b[layer][:, None], (ch_loc, span))
        folder = tap_folder(conv_w[layer], dilations[layer], span, DMAX)
        preact = folder(
            initial, lax.all_gather(extended, "sensor", axis=0, tiled=True), jnp.int32(0)
        )
        updated = extended.astype(jnp.float32) + jax.nn.gelu(preact, approximate=False)
        extended = jnp.where(inside[None, :], updated, 0.0).astype(jnp.bfloat16)
    hidden = extended[:, reach : reach + frames]
    portion = lax.all_gather(hidden, "sensor", axis=0, tiled=True)
    key_rows = jnp.dot(key_w, portion, preferred_element_type=jnp.float32)
    value_rows = jnp.dot(value_w, portion, preferred_element_type=jnp.float32)
    head_count = key_w.shape[0] // HD
    key_heads = key_rows.astype(jnp.bfloat16).reshape(head_count, HD, frames)
    value_heads = value_rows.astype(jnp.bfloat16).reshape(head_count, HD, frames)
    frame_mask = jnp.arange(frames, dtype=jnp.int32) < valid_frames[0]
    block_rows = min(LATENTS, 512)
    block_count = LATENTS // block_rows
    query_blocks = queries.reshape(head_count, HD, block_count, block_rows).transpose(2, 0, 1, 3)
    scale = 1.0 / math.sqrt(HD)

    def attend(query_block):
        scores = (
            jnp.einsum("hdq,hdt->hqt", query_block, key_heads, preferred_element_type=jnp.float32)
            * scale
        )
        scores = jnp.where(frame_mask[None, None, :], scores, -jnp.inf)
        peaks = jnp.max(scores, axis=2)
        probs = jnp.where(frame_mask[None, None, :], jnp.exp(scores - peaks[:, :, None]), 0.0)
        totals = jnp.sum(probs, axis=2)
        weighted = jnp.einsum(
            "hqt,hdt->hdq",
            probs.astype(jnp.bfloat16),
            value_heads,
            preferred_element_type=jnp.float32,
        )
        return (peaks, totals, weighted)

    peaks, totals, weighted = lax.map(attend, query_blocks)
    peaks = peaks.transpose(1, 0, 2).reshape(head_count, LATENTS)
    totals = totals.transpose(1, 0, 2).reshape(head_count, LATENTS)
    weighted = weighted.transpose(1, 2, 0, 3).reshape(head_count, HD, LATENTS)
    global_peaks = lax.pmax(peaks, "tm")
    rescale = jnp.exp(peaks - global_peaks)
    totals, weighted = lax.psum((totals * rescale, weighted * rescale[:, None, :]), "tm")
    attended = (
        (weighted / totals[:, None, :]).reshape(head_count * HD, LATENTS).astype(jnp.bfloat16)
    )
    return (hidden, attended)


VMEM = pltpu.VMEM
EDGE = 128
HALF = EDGE // 2
LOG2E = 1.4426950408889634
MASKED = -1e30


def whole(count):
    return [pl.BlockSpec(memory_space=pltpu.VMEM)] * count


def smem(count):
    return [pl.BlockSpec(memory_space=pltpu.SMEM)] * count


def params(mib):
    return pltpu.CompilerParams(vmem_limit_bytes=mib * 1024 * 1024)


def dot(left, right):
    return jnp.dot(left, right, preferred_element_type=jnp.float32)


def first_kernel(own_w, other_w, own, other, own_edge, other_edge, out):
    frames = own.shape[1]
    out[:, :frames] = (dot(own_w[...], own[...]) + dot(other_w[...], other[...])).astype(out.dtype)
    out[:, frames:] = (
        dot(own_w[...], own_edge[...]) + dot(other_w[...], other_edge[...])
    ).astype(out.dtype)


def gelu(value):
    return 0.5 * value * (1.0 + lax.erf(value * (1.0 / math.sqrt(2.0))))


def conv_rows(shifted, hidden, kernel, bias, row, keep, store, cols, step):
    rows = kernel.shape[1]
    row = pl.multiple_of(row, rows)
    for start in range(0, cols, step):
        width = min(step, cols - start)
        here = pl.ds(start, width)
        total = dot(kernel[0], shifted[0, :, here])
        total = total + dot(kernel[1], hidden[:, here])
        total = total + dot(kernel[2], shifted[1, :, here])
        old = hidden[pl.ds(row, rows), here].astype(jnp.float32)
        new = old + gelu(total + bias[...])
        if keep is not None and start + width > cols - EDGE:
            new = jnp.where(keep(start, width), new, 0.0)
        store(row, rows, here, new.astype(jnp.bfloat16))


def spread(shift, hidden, shifted):
    span = hidden.shape[1]
    wide = hidden[...].astype(jnp.float32)
    shifted[0] = pltpu.roll(wide, shift, 1).astype(jnp.bfloat16)
    shifted[1] = pltpu.roll(wide, span - shift, 1).astype(jnp.bfloat16)


def column(row, out):
    out[...] = jnp.broadcast_to(row, (EDGE, row.shape[1])).T


def pieces(layer, side, core, own_w, near_w, far_w, own_b, other_b, own_col, other_col):
    rows = own_w.shape[1]
    half = rows // 2
    column(own_b[layer : layer + 1, :], own_col)
    column(other_b[layer : layer + 1, :], other_col)
    near = pl.multiple_of(core[0] * half, half)
    far = pl.multiple_of((1 - core[0]) * half, half)
    base = (1 - side[0]) * rows
    return (
        (own_w, own_col[:, 0:1], side[0] * rows),
        (near_w, other_col[pl.ds(near, half), 0:1], base + near),
        (far_w, other_col[pl.ds(far, half), 0:1], base + far),
    )


def middle_kernel(
    layer, blocks, dilations, side, core, place, hidden, own_w, near_w, far_w, own_b, other_b,
    out, shifted, own_col, other_col,
):
    span = hidden.shape[1]
    frames = span - EDGE
    spread(dilations[layer], hidden, shifted)

    def keep(start, width):
        lane = lax.broadcasted_iota(jnp.int32, (1, width), 1) + start
        frame = jnp.where(lane < span - HALF, lane, lane - span) + place[0] * frames
        return (frame >= 0) & (frame < blocks * frames)

    def store(row, rows, here, value):
        out[pl.ds(row, rows), here] = value

    for kernel, bias, row in pieces(
        layer, side, core, own_w, near_w, far_w, own_b, other_b, own_col, other_col
    ):
        conv_rows(shifted, hidden, kernel, bias, row, keep, store, span, 384)


def last_kernel(
    layer, dilations, side, core, hidden, own_w, near_w, far_w, own_b, other_b, key_w, value_w,
    features, key_keep, key_send, value_keep, value_send, shifted, own_col, other_col, full,
):
    frames = features.shape[1]
    spread(dilations[layer], hidden, shifted)

    def store(row, rows, here, value):
        full[pl.ds(row, rows), here] = value

    for kernel, bias, row in pieces(
        layer, side, core, own_w, near_w, far_w, own_b, other_b, own_col, other_col
    ):
        conv_rows(shifted, hidden, kernel, bias, row, None, store, frames, 256)
    rows = features.shape[0]
    features[...] = full[pl.ds(pl.multiple_of(side[0] * rows, rows), rows), :]
    half = rows // 2
    for key_out, value_out, part in (
        (key_send, value_send, 1 - core[0]), (key_keep, value_keep, core[0])
    ):
        here = pl.ds(pl.multiple_of(part * half, half), half)
        key_out[...] = dot(key_w[here, :], full[...]).T.astype(jnp.bfloat16)
        value_out[...] = dot(value_w[here, :], full[...]).astype(jnp.bfloat16)


def thirds(value):
    first = value.astype(jnp.bfloat16)
    rest = value - first.astype(jnp.float32)
    second = rest.astype(jnp.bfloat16)
    third = (rest - second.astype(jnp.float32)).astype(jnp.bfloat16)
    return first, second, third


def pack(out, peak, total, weighted):
    out[0:HD, :] = weighted.astype(jnp.bfloat16)
    lines = [line.astype(jnp.float32) for line in thirds(peak) + thirds(total)]
    lines.append(jnp.zeros_like(lines[0]))
    lines.append(jnp.zeros_like(lines[0]))
    out[HD : HD + 8, :] = jnp.concatenate(lines, axis=0).astype(jnp.bfloat16)


def unpack(packed):
    lines = packed[HD : HD + 8, :].astype(jnp.float32)
    peak = lines[0:1] + (lines[1:2] + lines[2:3])
    total = lines[3:4] + (lines[4:5] + lines[5:6])
    return peak, total, packed[0:HD, :].astype(jnp.float32)


SCALE = LOG2E / math.sqrt(HD)


def join(one, two):
    peak = jnp.maximum(one[0], two[0])
    left = jnp.exp2((one[0] - peak) * SCALE)
    right = jnp.exp2((two[0] - peak) * SCALE)
    return peak, one[1] * left + two[1] * right, one[2] * left + two[2] * right


def ordered(info, mine, theirs):
    swap = info[0] == 1
    one = tuple(jnp.where(swap, t, m) for m, t in zip(mine, theirs))
    two = tuple(jnp.where(swap, m, t) for m, t in zip(mine, theirs))
    return one, two


def meet_kernel(peak, total, weighted, theirs, out):
    pack(out, *join((peak[...], total[...], weighted[...]), unpack(theirs)))


def merge_kernel(info, mine, theirs, out):
    pack(out, *join(*ordered(info, unpack(mine), unpack(theirs))))


def finish_kernel(info, mine, theirs, out):
    _, total, weighted = join(*ordered(info, unpack(mine), unpack(theirs)))
    out[...] = (weighted / total).astype(out.dtype)


def divide_kernel(mine, out):
    _, total, weighted = unpack(mine)
    out[...] = (weighted / total).astype(out.dtype)


def attend_kernel(
    packed, core, which, valid_own, valid_rec, key_own, key_rec, value_own, value_rec, queries,
    *refs
):
    outs = refs[:-6]
    keyed, asked, score_a, score_b, peak_a, peak_b = refs[-6:]
    frames = key_own.shape[0]
    latents = queries.shape[1]
    tile = score_a.shape[1]
    chunk = 256
    slot = which[0]
    lane = lax.broadcasted_iota(jnp.int32, (frames, 2 * HD), 1)
    frame = lax.broadcasted_iota(jnp.int32, (frames, 2 * HD), 0)
    spare = (1 - slot) * HD
    for part, (source, valid) in enumerate(((key_own, valid_own), (key_rec, valid_rec))):
        bias = jnp.where(frame < valid[0], 0.0, MASKED)
        keyed[pl.ds(part * frames, frames), :] = jnp.where(
            lane == spare, bias, source[...].astype(jnp.float32)
        ).astype(jnp.bfloat16)
    row = lax.broadcasted_iota(jnp.int32, (2 * HD, latents), 0)
    wide = queries[pl.ds(pl.multiple_of(core[0] * 2 * HD, 2 * HD), 2 * HD), :].astype(jnp.float32)
    wide = jnp.where(row // HD == slot, wide, jnp.where(row == spare, 1.0, 0.0))
    asked[...] = wide.astype(jnp.bfloat16)
    value_rows = pl.ds(pl.multiple_of(slot * HD, HD), HD)

    def score(index, scores, peaks):
        cols = pl.ds(pl.multiple_of(index * tile, tile), tile)
        peak = None
        for start in range(0, 2 * frames, chunk):
            here = pl.ds(start, chunk)
            value = dot(keyed[here, :], asked[:, cols])
            scores[here, :] = value
            top = jnp.max(value.reshape(chunk // 8, 8, tile), axis=0)
            peak = top if peak is None else jnp.maximum(peak, top)
        peaks[...] = jnp.max(peak, axis=0, keepdims=True)

    def weigh(index, scores, peaks):
        cols = pl.ds(pl.multiple_of(index * tile, tile), tile)
        peak = peaks[...]
        total = None
        weighted = None
        for start in range(0, 2 * frames, chunk):
            probs = jnp.exp2((scores[pl.ds(start, chunk), :] - peak) * SCALE)
            part = jnp.sum(probs.reshape(chunk // 8, 8, tile), axis=0)
            total = part if total is None else total + part
            source, offset = (value_own, start) if start < frames else (value_rec, start - frames)
            values = source[value_rows, pl.ds(offset, chunk)]
            term = dot(values, probs.astype(jnp.bfloat16))
            weighted = term if weighted is None else weighted + term
        total = jnp.sum(total, axis=0, keepdims=True)
        if packed:
            pack(outs[0].at[:, cols], peak, total, weighted)
        else:
            outs[0][:, cols] = peak
            outs[1][:, cols] = total
            outs[2][:, cols] = weighted

    count = latents // tile
    score(0, score_a, peak_a)

    @pl.loop(0, count // 2)
    def _(step):
        score(2 * step + 1, score_b, peak_b)
        weigh(2 * step, score_a, peak_a)
        score(jnp.minimum(2 * step + 2, count - 1), score_a, peak_a)
        weigh(2 * step + 1, score_b, peak_b)


def attend(packed, scalars, keys, values, queries):
    latents = queries.shape[1]
    frames = keys[0].shape[0]
    tile = min(256, latents // 2)
    if packed:
        out_shape = jax.ShapeDtypeStruct((HD + 8, latents), jnp.bfloat16)
        out_specs = pl.BlockSpec(memory_space=pltpu.VMEM)
    else:
        out_shape = [
            jax.ShapeDtypeStruct((1, latents), jnp.float32),
            jax.ShapeDtypeStruct((1, latents), jnp.float32),
            jax.ShapeDtypeStruct((HD, latents), jnp.float32),
        ]
        out_specs = whole(3)
    return pl.pallas_call(
        functools.partial(attend_kernel, packed),
        out_shape=out_shape,
        in_specs=smem(4) + whole(5),
        out_specs=out_specs,
        scratch_shapes=[
            VMEM((2 * frames, 2 * HD), jnp.bfloat16),
            VMEM((2 * HD, latents), jnp.bfloat16),
            VMEM((2 * frames, tile), jnp.float32),
            VMEM((2 * frames, tile), jnp.float32),
            VMEM((1, tile), jnp.float32),
            VMEM((1, tile), jnp.float32),
        ],
        compiler_params=params(20),
        name="attend_send" if packed else "attend_keep",
    )(*scalars, *keys, *values, queries)


def assemble_kernel(core, cross, own, across, core_own, core_across, out):
    mine, theirs = 2 * core[0], 2 - 2 * core[0]
    for piece, head in (
        (own, mine + cross[0]), (across, mine + 1 - cross[0]),
        (core_own, theirs + cross[0]), (core_across, theirs + 1 - cross[0]),
    ):
        out[pl.ds(pl.multiple_of(head * HD, HD), HD), :] = piece[...]


def swap(value, axis, bit):
    return lax.ppermute(value, axis, [(i, i ^ bit) for i in range(lax.axis_size(axis))])


def simple(kernel, out_shape, scalars, arrays, scratch=(), mib=16, specs=None):
    many = isinstance(out_shape, (list, tuple))
    return pl.pallas_call(
        kernel,
        grid=(1,),
        out_shape=out_shape,
        in_specs=smem(len(scalars)) + (specs or whole(len(arrays))),
        out_specs=whole(len(out_shape)) if many else pl.BlockSpec(memory_space=pltpu.VMEM),
        scratch_shapes=list(scratch),
        compiler_params=params(mib),
    )(*scalars, *arrays)


def pair_device(
    recording, spatial_w, conv_w, conv_b, dilations, valid_frames, key_w, value_w, queries
):
    frames = recording.shape[1]
    ch_loc = conv_w.shape[2]
    ch = conv_w.shape[3]
    half = ch_loc // 2
    latents = queries.shape[1]
    blocks = lax.axis_size("tm")
    side = lax.axis_index("sensor").astype(jnp.int32).reshape(1)
    place = lax.axis_index("tm").astype(jnp.int32).reshape(1)
    core = place & 1
    cross = (place >> 1) & 1
    span = frames + EDGE
    bf16 = jnp.bfloat16
    across = [(0, 1), (1, 0)]
    twins = [(i, i ^ 1) for i in range(blocks)]

    other_rec = lax.ppermute(recording, "sensor", across)
    tail = lax.ppermute(
        recording[:, frames - EDGE :], "tm", [(i, i + 1) for i in range(blocks - 1)]
    )
    head = lax.ppermute(recording[:, :EDGE], "tm", [(i + 1, i) for i in range(blocks - 1)])
    other_w = lax.ppermute(spatial_w, "sensor", across)
    lane = jnp.arange(EDGE, dtype=jnp.int32)[None, :]
    edge = jnp.where(lane < HALF, head, tail)
    other_edge = lax.ppermute(edge, "sensor", across)
    other_b = lax.ppermute(conv_b, "sensor", across)
    mine = [
        lax.dynamic_slice(conv_w, (layer, 0, core[0] * half, 0), (1, 3, half, ch))[0]
        for layer in range(LAYERS)
    ]
    near = [lax.ppermute(mine[n], "sensor", across) for n in range(LAYERS)]
    far = [lax.ppermute(near[n], "tm", twins) for n in range(LAYERS)]
    other_valid = lax.ppermute(valid_frames, "tm", twins)

    hidden = simple(
        first_kernel,
        jax.ShapeDtypeStruct((ch, span), bf16),
        (),
        (spatial_w, other_w, recording, other_rec, edge, other_edge),
    )
    columns = [VMEM((ch_loc, EDGE), jnp.float32)] * 2
    for layer in range(LAYERS):
        arrays = (hidden, conv_w, near[layer], far[layer], conv_b, other_b)
        specs = whole(len(arrays))
        specs[1] = pl.BlockSpec((None, 3, ch_loc, ch), lambda _, layer=layer: (layer, 0, 0, 0))
        scratch = [VMEM((2, ch, span), bf16)] + columns
        if layer < LAYERS - 1:
            hidden = simple(
                functools.partial(middle_kernel, layer, blocks),
                jax.ShapeDtypeStruct((ch, span), bf16),
                (dilations, side, core, place), arrays, scratch,
                mib=28, specs=specs,
            )
        else:
            shapes = [
                jax.ShapeDtypeStruct((ch_loc, frames), bf16),
                jax.ShapeDtypeStruct((frames, half), bf16),
                jax.ShapeDtypeStruct((frames, half), bf16),
                jax.ShapeDtypeStruct((half, frames), bf16),
                jax.ShapeDtypeStruct((half, frames), bf16),
            ]
            features, key_keep, key_send, value_keep, value_send = simple(
                functools.partial(last_kernel, layer), shapes, (dilations, side, core),
                arrays + (key_w, value_w),
                scratch + [VMEM((ch, frames), bf16)],
                mib=28, specs=specs + whole(2),
            )
    keys = (key_keep, lax.ppermute(key_send, "tm", twins))
    values = (value_keep, lax.ppermute(value_send, "tm", twins))
    facts = (valid_frames, other_valid)
    sent = attend(True, (core, 1 - cross) + facts, keys, values, queries)
    arrived = swap(sent, "tm", 2)
    peak, total, weighted = attend(False, (core, cross) + facts, keys, values, queries)
    packed_shape = jax.ShapeDtypeStruct((HD + 8, latents), bf16)
    final_shape = jax.ShapeDtypeStruct((HD, latents), bf16)
    packed = simple(meet_kernel, packed_shape, (), (peak, total, weighted, arrived))
    if blocks == 4:
        done = simple(divide_kernel, final_shape, (), (packed,))
    bit = 4
    while bit < blocks:
        theirs = swap(packed, "tm", bit)
        which = ((place & bit) != 0).astype(jnp.int32)
        if bit * 2 < blocks:
            packed = simple(merge_kernel, packed_shape, (which,), (packed, theirs))
        else:
            done = simple(finish_kernel, final_shape, (which,), (packed, theirs))
        bit *= 2
    crossed = swap(done, "tm", 2)
    core_done = swap(done, "tm", 1)
    core_crossed = swap(crossed, "tm", 1)
    attended = simple(
        assemble_kernel, jax.ShapeDtypeStruct((ch_loc, latents), bf16), (core, cross),
        (done, crossed, core_done, core_crossed),
    )
    return (features, attended)


def fits(mesh):
    sensors, blocks = mesh.shape["sensor"], mesh.shape["tm"]
    return sensors == 2 and blocks >= 4 and blocks & (blocks - 1) == 0


def on_device(*arrays):
    if arrays[6].shape[0] // HD != 4:
        return generic_device(*arrays)
    return pair_device(*arrays)


def solution(mesh):
    quick = fits(mesh)
    return jax.shard_map(
        on_device if quick else generic_device,
        mesh=mesh,
        in_specs=(
            P("sensor", "tm"),
            P(None, "sensor"),
            P(None, None, "sensor", None),
            P(None, "sensor"),
            P(),
            P("tm"),
            P("sensor", None),
            P("sensor", None),
            P("sensor", None),
        ),
        out_specs=(P("sensor", "tm"), P("sensor", None)),
        check_vma=False,
    )
```

```python
import functools
import math

import jax
import jax.numpy as jnp
from jax import lax
from jax.experimental import pallas as pl
from jax.experimental.pallas import tpu as pltpu
from jax.sharding import PartitionSpec as P


HD = 64
LATENTS = 2048
LAYERS = 3
DMAX = 16


def padded(cells, sides, width):
    for axis, dim in sides:
        count = lax.axis_size(axis)
        ends = count - 1
        head = lax.slice_in_dim(cells, 0, width, axis=dim)
        tail = lax.slice_in_dim(cells, cells.shape[dim] - width, cells.shape[dim], axis=dim)
        cells = jnp.concatenate(
            [
                lax.ppermute(tail, axis, [(i, (i + 1) % count) for i in range(ends)]),
                cells,
                lax.ppermute(head, axis, [((i + 1) % count, i) for i in range(ends)]),
            ],
            axis=dim,
        )
    return cells


def tap_folder(kernels, dilation, frames, margin):

    def add_taps(running, portion, first_row):
        portion = jnp.pad(portion, ((0, 0), (margin, margin)))
        for tap_index in range(3):
            kernel = kernels[tap_index]
            offset = DMAX + (tap_index - 1) * dilation
            shifted = lax.dynamic_slice_in_dim(portion, offset, frames, 1)
            running = running + jnp.dot(kernel, shifted, preferred_element_type=jnp.float32)
        return running

    return add_taps


def generic_device(
    recording, spatial_w, conv_w, conv_b, dilations, valid_frames, key_w, value_w, queries
):
    frames = recording.shape[1]
    ch_loc = conv_w.shape[2]
    hidden = lax.psum_scatter(
        jnp.dot(spatial_w, recording, preferred_element_type=jnp.float32),
        "sensor",
        scatter_dimension=0,
        tiled=True,
    ).astype(jnp.bfloat16)
    reach = 3 * DMAX
    extended = padded(hidden, (("tm", 1),), reach)
    span = frames + 2 * reach
    position = lax.axis_index("tm") * frames - reach + jnp.arange(span, dtype=jnp.int32)
    inside = (position >= 0) & (position < frames * lax.axis_size("tm"))
    for layer in range(LAYERS):
        initial = jnp.broadcast_to(conv_b[layer][:, None], (ch_loc, span))
        folder = tap_folder(conv_w[layer], dilations[layer], span, DMAX)
        preact = folder(
            initial, lax.all_gather(extended, "sensor", axis=0, tiled=True), jnp.int32(0)
        )
        updated = extended.astype(jnp.float32) + jax.nn.gelu(preact, approximate=False)
        extended = jnp.where(inside[None, :], updated, 0.0).astype(jnp.bfloat16)
    hidden = extended[:, reach : reach + frames]
    portion = lax.all_gather(hidden, "sensor", axis=0, tiled=True)
    key_rows = jnp.dot(key_w, portion, preferred_element_type=jnp.float32)
    value_rows = jnp.dot(value_w, portion, preferred_element_type=jnp.float32)
    head_count = key_w.shape[0] // HD
    key_heads = key_rows.astype(jnp.bfloat16).reshape(head_count, HD, frames)
    value_heads = value_rows.astype(jnp.bfloat16).reshape(head_count, HD, frames)
    frame_mask = jnp.arange(frames, dtype=jnp.int32) < valid_frames[0]
    block_rows = min(LATENTS, 512)
    block_count = LATENTS // block_rows
    query_blocks = queries.reshape(head_count, HD, block_count, block_rows).transpose(2, 0, 1, 3)
    scale = 1.0 / math.sqrt(HD)

    def attend(query_block):
        scores = (
            jnp.einsum("hdq,hdt->hqt", query_block, key_heads, preferred_element_type=jnp.float32)
            * scale
        )
        scores = jnp.where(frame_mask[None, None, :], scores, -jnp.inf)
        peaks = jnp.max(scores, axis=2)
        probs = jnp.where(frame_mask[None, None, :], jnp.exp(scores - peaks[:, :, None]), 0.0)
        totals = jnp.sum(probs, axis=2)
        weighted = jnp.einsum(
            "hqt,hdt->hdq",
            probs.astype(jnp.bfloat16),
            value_heads,
            preferred_element_type=jnp.float32,
        )
        return (peaks, totals, weighted)

    peaks, totals, weighted = lax.map(attend, query_blocks)
    peaks = peaks.transpose(1, 0, 2).reshape(head_count, LATENTS)
    totals = totals.transpose(1, 0, 2).reshape(head_count, LATENTS)
    weighted = weighted.transpose(1, 2, 0, 3).reshape(head_count, HD, LATENTS)
    global_peaks = lax.pmax(peaks, "tm")
    rescale = jnp.exp(peaks - global_peaks)
    totals, weighted = lax.psum((totals * rescale, weighted * rescale[:, None, :]), "tm")
    attended = (
        (weighted / totals[:, None, :]).reshape(head_count * HD, LATENTS).astype(jnp.bfloat16)
    )
    return (hidden, attended)


VMEM = pltpu.VMEM
EDGE = 128
HALF = EDGE // 2
LOG2E = 1.4426950408889634
MASKED = -1e30


def whole(count):
    return [pl.BlockSpec(memory_space=pltpu.VMEM)] * count


def smem(count):
    return [pl.BlockSpec(memory_space=pltpu.SMEM)] * count


def params(mib):
    return pltpu.CompilerParams(vmem_limit_bytes=mib * 1024 * 1024)


def dot(left, right):
    return jnp.dot(left, right, preferred_element_type=jnp.float32)


def first_kernel(
    side, core, own_w, near_w, far_w, own, other, own_edge, other_edge, mine, theirs, weights
):
    frames = own.shape[1]
    rows = mine.shape[0]
    weights[core[0]] = near_w[...]
    weights[1 - core[0]] = far_w[...]
    for out, part in ((mine, side[0]), (theirs, 1 - side[0])):
        left = own_w[pl.ds(pl.multiple_of(part * rows, rows), rows), :]
        right = weights[part]
        out[:, :frames] = (dot(left, own[...]) + dot(right, other[...])).astype(out.dtype)
        out[:, frames:] = (dot(left, own_edge[...]) + dot(right, other_edge[...])).astype(out.dtype)


def gelu(value):
    return 0.5 * value * (1.0 + lax.erf(value * (1.0 / math.sqrt(2.0))))


def conv_rows(taps, old, kernel, bias, keep, store, cols, step):
    for start in range(0, cols, step):
        width = min(step, cols - start)
        here = pl.ds(start, width)
        total = dot(kernel[0], taps[0, :, here])
        total = total + dot(kernel[1], taps[1, :, here])
        total = total + dot(kernel[2], taps[2, :, here])
        new = old(here).astype(jnp.float32) + gelu(total + bias)
        if keep is not None and start + width > cols - EDGE:
            new = jnp.where(keep(start, width), new, 0.0)
        store(here, new.astype(jnp.bfloat16))


def column(row, out):
    out[...] = jnp.broadcast_to(row, (EDGE, row.shape[1])).T


def keeper(place, blocks, span):
    frames = span - EDGE

    def keep(start, width):
        lane = lax.broadcasted_iota(jnp.int32, (1, width), 1) + start
        frame = jnp.where(lane < span - HALF, lane, lane - span) + place[0] * frames
        return (frame >= 0) & (frame < blocks * frames)

    return keep


def own_kernel(
    layer, blocks, last, dilations, side, place, mine, theirs, weights, biases, out, taps, col
):
    rows, span = mine.shape
    shift = dilations[layer]
    for part, source in ((side[0], mine), (1 - side[0], theirs)):
        here = pl.ds(pl.multiple_of(part * rows, rows), rows)
        wide = source[...].astype(jnp.float32)
        taps[1, here, :] = source[...]
        taps[0, here, :] = pltpu.roll(wide, shift, 1).astype(jnp.bfloat16)
        taps[2, here, :] = pltpu.roll(wide, span - shift, 1).astype(jnp.bfloat16)
    column(biases[layer : layer + 1, :], col)

    def store(here, value):
        out[:, here] = value

    conv_rows(
        taps, lambda here: mine[:, here], weights, col[:, 0:1],
        None if last else keeper(place, blocks, span), store, out.shape[1], 256 if last else 384,
    )


def other_rows(layer, core, theirs, taps, near_w, far_w, biases, col, keep, target, cols, step):
    half = near_w.shape[1]
    column(biases[layer : layer + 1, :], col)
    for weights, part in ((near_w, core[0]), (far_w, 1 - core[0])):
        rows = pl.ds(pl.multiple_of(part * half, half), half)

        def store(here, value, rows=rows):
            target(rows, here, value)

        conv_rows(
            taps, lambda here, rows=rows: theirs[rows, here], weights, col[rows, 0:1], keep,
            store, cols, step,
        )


def other_kernel(layer, blocks, core, place, theirs, taps, near_w, far_w, biases, out, col):
    span = theirs.shape[1]

    def target(rows, here, value):
        out[rows, here] = value

    other_rows(
        layer, core, theirs, taps, near_w, far_w, biases, col, keeper(place, blocks, span), target,
        span, 384,
    )


def last_kernel(
    layer, side, core, features, theirs, taps, near_w, far_w, biases, key_w, value_w,
    key_keep, key_send, value_keep, value_send, col, full,
):
    rows, frames = features.shape
    base = (1 - side[0]) * rows
    full[pl.ds(pl.multiple_of(side[0] * rows, rows), rows), :] = features[...]
    half = rows // 2

    def target(part, here, value):
        full[pl.ds(pl.multiple_of(base + part.start, half), half), here] = value

    other_rows(
        layer, core, theirs, taps, near_w, far_w, biases, col, None, target, frames, 256
    )
    for key_out, value_out, part in (
        (key_send, value_send, 1 - core[0]), (key_keep, value_keep, core[0])
    ):
        here = pl.ds(pl.multiple_of(part * half, half), half)
        key_out[...] = dot(key_w[here, :], full[...]).T.astype(jnp.bfloat16)
        value_out[...] = dot(value_w[here, :], full[...]).astype(jnp.bfloat16)


def thirds(value):
    first = value.astype(jnp.bfloat16)
    rest = value - first.astype(jnp.float32)
    second = rest.astype(jnp.bfloat16)
    third = (rest - second.astype(jnp.float32)).astype(jnp.bfloat16)
    return first, second, third


def pack(out, peak, total, weighted):
    out[0:HD, :] = weighted.astype(jnp.bfloat16)
    lines = [line.astype(jnp.float32) for line in thirds(peak) + thirds(total)]
    lines.append(jnp.zeros_like(lines[0]))
    lines.append(jnp.zeros_like(lines[0]))
    out[HD : HD + 8, :] = jnp.concatenate(lines, axis=0).astype(jnp.bfloat16)


def unpack(packed):
    lines = packed[HD : HD + 8, :].astype(jnp.float32)
    peak = lines[0:1] + (lines[1:2] + lines[2:3])
    total = lines[3:4] + (lines[4:5] + lines[5:6])
    return peak, total, packed[0:HD, :].astype(jnp.float32)


SCALE = LOG2E / math.sqrt(HD)


def join(one, two):
    peak = jnp.maximum(one[0], two[0])
    left = jnp.exp2((one[0] - peak) * SCALE)
    right = jnp.exp2((two[0] - peak) * SCALE)
    return peak, one[1] * left + two[1] * right, one[2] * left + two[2] * right


def ordered(info, mine, theirs):
    swap = info[0] == 1
    one = tuple(jnp.where(swap, t, m) for m, t in zip(mine, theirs))
    two = tuple(jnp.where(swap, m, t) for m, t in zip(mine, theirs))
    return one, two


def meet_kernel(peak, total, weighted, *refs):
    state = (peak[...], total[...], weighted[...])
    for theirs in refs[:-1]:
        state = join(state, unpack(theirs))
    pack(refs[-1], *state)


def merge_kernel(info, mine, theirs, out):
    pack(out, *join(*ordered(info, unpack(mine), unpack(theirs))))


def finish_kernel(info, mine, theirs, out):
    _, total, weighted = join(*ordered(info, unpack(mine), unpack(theirs)))
    out[...] = (weighted / total).astype(out.dtype)


def attend_kernel(
    packed, core, which, half, valid_own, valid_rec, key_own, key_rec, value_own, value_rec,
    queries, *refs
):
    outs = refs[:-5]
    keyed, asked, valued, score_a, score_b = refs[-5:]
    frames = key_own.shape[0]
    latents = asked.shape[1]
    tile = score_a.shape[1]
    chunk = 256
    slot = which[0]
    lane = lax.broadcasted_iota(jnp.int32, (frames, 2 * HD), 1)
    frame = lax.broadcasted_iota(jnp.int32, (frames, 2 * HD), 0)
    spare = (1 - slot) * HD
    value_rows = pl.ds(pl.multiple_of(slot * HD, HD), HD)
    for part, (source, valid) in enumerate(((key_own, valid_own), (key_rec, valid_rec))):
        bias = jnp.where(frame < valid[0], 0.0, MASKED)
        keyed[pl.ds(part * frames, frames), :] = jnp.where(
            lane == spare, bias, source[...].astype(jnp.float32)
        ).astype(jnp.bfloat16)
    valued[0:HD, 0:frames] = value_own[value_rows, :]
    valued[0:HD, frames:] = value_rec[value_rows, :]
    valued[HD:, :] = jnp.ones((valued.shape[0] - HD, 2 * frames), jnp.bfloat16)
    row = lax.broadcasted_iota(jnp.int32, (2 * HD, latents), 0)
    wide = queries[
        pl.ds(pl.multiple_of(core[0] * 2 * HD, 2 * HD), 2 * HD),
        pl.ds(pl.multiple_of(half[0] * latents, latents), latents),
    ].astype(jnp.float32)
    wide = jnp.where(row // HD == slot, wide, jnp.where(row == spare, 1.0, 0.0))
    asked[...] = wide.astype(jnp.bfloat16)

    buffers = (score_a, score_b)
    count = latents // tile
    peak = None
    for step in range(count + 1):
        cols = slice(step * tile, (step + 1) * tile)
        done = slice((step - 1) * tile, step * tile)
        top = None
        weighted = None
        for start in range(0, 2 * frames, chunk):
            here = pl.ds(start, chunk)
            if step < count:
                value = dot(keyed[here, :], asked[:, cols])
                buffers[step % 2][here, :] = value
                high = jnp.max(value.reshape(chunk // 8, 8, tile), axis=0)
                top = high if top is None else jnp.maximum(top, high)
            if step > 0:
                probs = jnp.exp2((buffers[(step - 1) % 2][here, :] - peak) * SCALE)
                term = dot(valued[:, here], probs.astype(jnp.bfloat16))
                weighted = term if weighted is None else weighted + term
        if step > 0:
            total = weighted[HD : HD + 1, :]
            if packed:
                pack(outs[0].at[:, done], peak, total, weighted[0:HD, :])
            else:
                outs[0][:, done] = peak
                outs[1][:, done] = total
                outs[2][:, done] = weighted[0:HD, :]
        if step < count:
            peak = jnp.max(top, axis=0, keepdims=True)


def attend(packed, scalars, keys, values, queries):
    latents = queries.shape[1] // 2
    frames = keys[0].shape[0]
    tile = min(256, latents)
    if packed:
        out_shape = jax.ShapeDtypeStruct((HD + 8, latents), jnp.bfloat16)
        out_specs = pl.BlockSpec(memory_space=pltpu.VMEM)
    else:
        out_shape = [
            jax.ShapeDtypeStruct((1, latents), jnp.float32),
            jax.ShapeDtypeStruct((1, latents), jnp.float32),
            jax.ShapeDtypeStruct((HD, latents), jnp.float32),
        ]
        out_specs = whole(3)
    return pl.pallas_call(
        functools.partial(attend_kernel, packed),
        out_shape=out_shape,
        in_specs=smem(5) + whole(5),
        out_specs=out_specs,
        scratch_shapes=[
            VMEM((2 * frames, 2 * HD), jnp.bfloat16),
            VMEM((2 * HD, latents), jnp.bfloat16),
            VMEM((HD + 16, 2 * frames), jnp.bfloat16),
            VMEM((2 * frames, tile), jnp.float32),
            VMEM((2 * frames, tile), jnp.float32),
        ],
        compiler_params=params(20),
        name="attend_send" if packed else "attend_keep",
    )(*scalars, *keys, *values, queries)


def assemble_kernel(core, cross, lower, *refs):
    out = refs[-1]
    latents = refs[0].shape[1]
    mine, theirs = 2 * core[0], 2 - 2 * core[0]
    heads = (mine + cross[0], mine + 1 - cross[0], theirs + cross[0], theirs + 1 - cross[0])
    for index, piece in enumerate(refs[:-1]):
        part = lower[0] if index % 2 == 0 else 1 - lower[0]
        out[
            pl.ds(pl.multiple_of(heads[index // 2] * HD, HD), HD),
            pl.ds(pl.multiple_of(part * latents, latents), latents),
        ] = piece[...]


def simple(kernel, out_shape, scalars, arrays, scratch=(), mib=16, specs=None):
    many = isinstance(out_shape, (list, tuple))
    return pl.pallas_call(
        kernel,
        grid=(1,),
        out_shape=out_shape,
        in_specs=smem(len(scalars)) + (specs or whole(len(arrays))),
        out_specs=whole(len(out_shape)) if many else pl.BlockSpec(memory_space=pltpu.VMEM),
        scratch_shapes=list(scratch),
        compiler_params=params(mib),
    )(*scalars, *arrays)


def pair_device(
    recording, spatial_w, conv_w, conv_b, dilations, valid_frames, key_w, value_w, queries
):
    frames = recording.shape[1]
    ch_loc = conv_w.shape[2]
    ch = conv_w.shape[3]
    half = ch_loc // 2
    latents = queries.shape[1]
    blocks = lax.axis_size("tm")
    side = lax.axis_index("sensor").astype(jnp.int32).reshape(1)
    place = lax.axis_index("tm").astype(jnp.int32).reshape(1)
    core = place & 1
    cross = (place >> 1) & 1
    span = frames + EDGE
    bf16 = jnp.bfloat16
    across = [(0, 1), (1, 0)]
    twins = [(i, i ^ 1) for i in range(blocks)]

    other_rec = lax.ppermute(recording, "sensor", across)
    slab = ch // 2
    near_sp = lax.ppermute(
        lax.dynamic_slice_in_dim(spatial_w, core[0] * slab, slab, axis=0),
        "sensor", across,
    )
    far_sp = lax.ppermute(near_sp, "tm", twins)
    tail = lax.ppermute(
        recording[:, frames - EDGE :], "tm", [(i, i + 1) for i in range(blocks - 1)]
    )
    head = lax.ppermute(recording[:, :EDGE], "tm", [(i + 1, i) for i in range(blocks - 1)])
    lane = jnp.arange(EDGE, dtype=jnp.int32)[None, :]
    edge = jnp.where(lane < HALF, head, tail)
    other_edge = lax.ppermute(edge, "sensor", across)
    other_b = lax.ppermute(conv_b, "sensor", across)
    mine = [
        lax.dynamic_slice(conv_w, (layer, 0, core[0] * half, 0), (1, 3, half, ch))[0]
        for layer in range(LAYERS)
    ]
    near = [lax.ppermute(mine[n], "sensor", across) for n in range(LAYERS)]
    far = [lax.ppermute(near[n], "tm", twins) for n in range(LAYERS)]
    other_valid = lax.ppermute(valid_frames, "tm", twins)

    half_shape = jax.ShapeDtypeStruct((ch_loc, span), bf16)
    own_h, other_h = simple(
        first_kernel,
        [half_shape, half_shape],
        (side, core),
        (spatial_w, near_sp, far_sp, recording, other_rec, edge, other_edge),
        [VMEM((2, slab, recording.shape[0]), bf16)],
        mib=48,
    )
    taps_shape = jax.ShapeDtypeStruct((3, ch, span), bf16)
    col = [VMEM((ch_loc, EDGE), jnp.float32)]
    for layer in range(LAYERS):
        last = layer == LAYERS - 1
        specs = whole(4)
        specs[2] = pl.BlockSpec((None, 3, ch_loc, ch), lambda _, layer=layer: (layer, 0, 0, 0))
        own_next, taps = simple(
            functools.partial(own_kernel, layer, blocks, last),
            [jax.ShapeDtypeStruct((ch_loc, frames), bf16) if last else half_shape, taps_shape],
            (dilations, side, place), (own_h, other_h, conv_w, conv_b), col,
            mib=24, specs=specs,
        )
        arrays = (other_h, taps, near[layer], far[layer], other_b)
        if last:
            features = own_next
            shapes = [
                jax.ShapeDtypeStruct((frames, half), bf16),
                jax.ShapeDtypeStruct((frames, half), bf16),
                jax.ShapeDtypeStruct((half, frames), bf16),
                jax.ShapeDtypeStruct((half, frames), bf16),
            ]
            key_keep, key_send, value_keep, value_send = simple(
                functools.partial(last_kernel, layer), shapes, (side, core),
                (features,) + arrays + (key_w, value_w), col + [VMEM((ch, frames), bf16)],
                mib=24,
            )
        else:
            other_h = simple(
                functools.partial(other_kernel, layer, blocks), half_shape, (core, place), arrays,
                col, mib=24,
            )
            own_h = own_next
    keys = (key_keep, lax.ppermute(key_send, "tm", twins))
    values = (value_keep, lax.ppermute(value_send, "tm", twins))

    def flip(value, bit):
        return lax.ppermute(value, "tm", [(i, i ^ bit) for i in range(blocks)])

    lower = (place >> 2) & 1

    def run(packed, slot, part):
        scalars = (core, slot, part, valid_frames, other_valid)
        return attend(packed, scalars, keys, values, queries)

    sent = flip(run(True, 1 - cross, 1 - lower), 2)
    kept = flip(run(True, 1 - cross, lower), 2)
    packed_shape = jax.ShapeDtypeStruct((HD + 8, latents // 2), bf16)
    final_shape = jax.ShapeDtypeStruct((HD, latents // 2), bf16)
    given = run(False, cross, 1 - lower)
    given = simple(meet_kernel, packed_shape, (), (*given, sent))
    given = flip(given, 4)
    held = run(False, cross, lower)
    packed = simple(meet_kernel, packed_shape, (), (*held, kept, given))
    bit = 8
    while bit < blocks:
        theirs = flip(packed, bit)
        which = ((place & bit) != 0).astype(jnp.int32)
        if bit * 2 < blocks:
            packed = simple(merge_kernel, packed_shape, (which,), (packed, theirs))
        else:
            done = simple(finish_kernel, final_shape, (which,), (packed, theirs))
        bit *= 2
    above = flip(done, 4)
    beside = flip(done, 2)
    corner = flip(above, 2)
    pieces = [done, above, beside, corner]
    pieces += [flip(piece, 1) for piece in pieces]
    attended = simple(
        assemble_kernel, jax.ShapeDtypeStruct((ch_loc, latents), bf16), (core, cross, lower),
        pieces,
    )
    return (features, attended)


def fits(mesh):
    sensors, blocks = mesh.shape["sensor"], mesh.shape["tm"]
    return sensors == 2 and blocks >= 16 and blocks & (blocks - 1) == 0


def on_device(*arrays):
    if arrays[6].shape[0] // HD != 4:
        return generic_device(*arrays)
    return pair_device(*arrays)


def solution(mesh):
    quick = fits(mesh)
    return jax.shard_map(
        on_device if quick else generic_device,
        mesh=mesh,
        in_specs=(
            P("sensor", "tm"),
            P(None, "sensor"),
            P(None, None, "sensor", None),
            P(None, "sensor"),
            P(),
            P("tm"),
            P("sensor", None),
            P("sensor", None),
            P("sensor", None),
        ),
        out_specs=(P("sensor", "tm"), P("sensor", None)),
        check_vma=False,
    )
```

```python
import functools
import math

import jax
import jax.numpy as jnp
from jax import lax
from jax.experimental import pallas as pl
from jax.experimental.pallas import tpu as pltpu
from jax.sharding import PartitionSpec as P


HD = 64
LATENTS = 2048
LAYERS = 3
DMAX = 16


def padded(cells, sides, width):
    for axis, dim in sides:
        count = lax.axis_size(axis)
        ends = count - 1
        head = lax.slice_in_dim(cells, 0, width, axis=dim)
        tail = lax.slice_in_dim(cells, cells.shape[dim] - width, cells.shape[dim], axis=dim)
        cells = jnp.concatenate(
            [
                lax.ppermute(tail, axis, [(i, (i + 1) % count) for i in range(ends)]),
                cells,
                lax.ppermute(head, axis, [((i + 1) % count, i) for i in range(ends)]),
            ],
            axis=dim,
        )
    return cells


def tap_folder(kernels, dilation, frames, margin):

    def add_taps(running, portion, first_row):
        portion = jnp.pad(portion, ((0, 0), (margin, margin)))
        for tap_index in range(3):
            kernel = kernels[tap_index]
            offset = DMAX + (tap_index - 1) * dilation
            shifted = lax.dynamic_slice_in_dim(portion, offset, frames, 1)
            running = running + jnp.dot(kernel, shifted, preferred_element_type=jnp.float32)
        return running

    return add_taps


def generic_device(
    recording, spatial_w, conv_w, conv_b, dilations, valid_frames, key_w, value_w, queries
):
    frames = recording.shape[1]
    ch_loc = conv_w.shape[2]
    hidden = lax.psum_scatter(
        jnp.dot(spatial_w, recording, preferred_element_type=jnp.float32),
        "sensor",
        scatter_dimension=0,
        tiled=True,
    ).astype(jnp.bfloat16)
    reach = 3 * DMAX
    extended = padded(hidden, (("tm", 1),), reach)
    span = frames + 2 * reach
    position = lax.axis_index("tm") * frames - reach + jnp.arange(span, dtype=jnp.int32)
    inside = (position >= 0) & (position < frames * lax.axis_size("tm"))
    for layer in range(LAYERS):
        initial = jnp.broadcast_to(conv_b[layer][:, None], (ch_loc, span))
        folder = tap_folder(conv_w[layer], dilations[layer], span, DMAX)
        preact = folder(
            initial, lax.all_gather(extended, "sensor", axis=0, tiled=True), jnp.int32(0)
        )
        updated = extended.astype(jnp.float32) + jax.nn.gelu(preact, approximate=False)
        extended = jnp.where(inside[None, :], updated, 0.0).astype(jnp.bfloat16)
    hidden = extended[:, reach : reach + frames]
    portion = lax.all_gather(hidden, "sensor", axis=0, tiled=True)
    key_rows = jnp.dot(key_w, portion, preferred_element_type=jnp.float32)
    value_rows = jnp.dot(value_w, portion, preferred_element_type=jnp.float32)
    head_count = key_w.shape[0] // HD
    key_heads = key_rows.astype(jnp.bfloat16).reshape(head_count, HD, frames)
    value_heads = value_rows.astype(jnp.bfloat16).reshape(head_count, HD, frames)
    frame_mask = jnp.arange(frames, dtype=jnp.int32) < valid_frames[0]
    block_rows = min(LATENTS, 512)
    block_count = LATENTS // block_rows
    query_blocks = queries.reshape(head_count, HD, block_count, block_rows).transpose(2, 0, 1, 3)
    scale = 1.0 / math.sqrt(HD)

    def attend(query_block):
        scores = (
            jnp.einsum("hdq,hdt->hqt", query_block, key_heads, preferred_element_type=jnp.float32)
            * scale
        )
        scores = jnp.where(frame_mask[None, None, :], scores, -jnp.inf)
        peaks = jnp.max(scores, axis=2)
        probs = jnp.where(frame_mask[None, None, :], jnp.exp(scores - peaks[:, :, None]), 0.0)
        totals = jnp.sum(probs, axis=2)
        weighted = jnp.einsum(
            "hqt,hdt->hdq",
            probs.astype(jnp.bfloat16),
            value_heads,
            preferred_element_type=jnp.float32,
        )
        return (peaks, totals, weighted)

    peaks, totals, weighted = lax.map(attend, query_blocks)
    peaks = peaks.transpose(1, 0, 2).reshape(head_count, LATENTS)
    totals = totals.transpose(1, 0, 2).reshape(head_count, LATENTS)
    weighted = weighted.transpose(1, 2, 0, 3).reshape(head_count, HD, LATENTS)
    global_peaks = lax.pmax(peaks, "tm")
    rescale = jnp.exp(peaks - global_peaks)
    totals, weighted = lax.psum((totals * rescale, weighted * rescale[:, None, :]), "tm")
    attended = (
        (weighted / totals[:, None, :]).reshape(head_count * HD, LATENTS).astype(jnp.bfloat16)
    )
    return (hidden, attended)


VMEM = pltpu.VMEM
EDGE = 128
HALF = EDGE // 2
LOG2E = 1.4426950408889634
MASKED = -1e30


def whole(count):
    return [pl.BlockSpec(memory_space=pltpu.VMEM)] * count


def smem(count):
    return [pl.BlockSpec(memory_space=pltpu.SMEM)] * count


def params(mib):
    return pltpu.CompilerParams(vmem_limit_bytes=mib * 1024 * 1024)


def dot(left, right):
    return jnp.dot(left, right, preferred_element_type=jnp.float32)


def first_kernel(side, *refs):
    sources, (mine, theirs), held, done = refs[:6], refs[6:8], refs[8:14], refs[14]
    copies = [
        pltpu.make_async_copy(source, target, done.at[n])
        for n, (source, target) in enumerate(zip(sources, held))
    ]
    for copy in copies:
        copy.start()
    for copy in copies:
        copy.wait()
    own_w, other_w, own, other, own_edge, other_edge = held
    frames = own.shape[1]
    rows = mine.shape[0]
    for out, part in ((mine, side[0]), (theirs, 1 - side[0])):
        here = pl.ds(pl.multiple_of(part * rows, rows), rows)
        left, right = own_w[here, :], other_w[here, :]
        out[:, :frames] = (dot(left, own[...]) + dot(right, other[...])).astype(out.dtype)
        out[:, frames:] = (dot(left, own_edge[...]) + dot(right, other_edge[...])).astype(out.dtype)


def gelu(value):
    return 0.5 * value * (1.0 + lax.erf(value * (1.0 / math.sqrt(2.0))))


def conv_rows(taps, old, kernel, bias, keep, store, cols, step):
    for start in range(0, cols, step):
        width = min(step, cols - start)
        here = pl.ds(start, width)
        total = dot(kernel[0], taps[0, :, here])
        total = total + dot(kernel[1], taps[1, :, here])
        total = total + dot(kernel[2], taps[2, :, here])
        new = old(here).astype(jnp.float32) + gelu(total + bias)
        if keep is not None and start + width > cols - EDGE:
            new = jnp.where(keep(start, width), new, 0.0)
        store(here, new.astype(jnp.bfloat16))


def column(row, out):
    out[...] = jnp.broadcast_to(row, (EDGE, row.shape[1])).T


def keeper(place, blocks, span):
    frames = span - EDGE

    def keep(start, width):
        lane = lax.broadcasted_iota(jnp.int32, (1, width), 1) + start
        frame = jnp.where(lane < span - HALF, lane, lane - span) + place[0] * frames
        return (frame >= 0) & (frame < blocks * frames)

    return keep


def own_kernel(
    layer, blocks, last, dilations, side, place, mine, theirs, weights, biases, *refs
):
    outs, taps, col = refs[:-2], refs[-2], refs[-1]
    out = outs[0]
    rows, span = mine.shape
    shift = dilations[layer]
    lane = lax.broadcasted_iota(jnp.int32, (rows, EDGE), 1)
    count = span // EDGE
    for part, source in ((side[0], mine), (1 - side[0], theirs)):
        here = pl.ds(pl.multiple_of(part * rows, rows), rows)
        tiles = [source[:, n * EDGE : (n + 1) * EDGE] for n in range(count)]
        later = [pltpu.roll(tile, shift, 1) for tile in tiles]
        sooner = [pltpu.roll(tile, EDGE - shift, 1) for tile in tiles]
        for n in range(count):
            cols = slice(n * EDGE, (n + 1) * EDGE)
            taps[1, here, cols] = tiles[n]
            taps[0, here, cols] = jnp.where(lane < shift, later[n - 1], later[n])
            taps[2, here, cols] = jnp.where(
                lane < EDGE - shift, sooner[n], sooner[(n + 1) % count]
            )
    column(biases[layer : layer + 1, :], col)

    def store(here, value):
        for target in outs:
            target[:, here] = value

    conv_rows(
        taps, lambda here: mine[:, here], weights, col[:, 0:1],
        None if last else keeper(place, blocks, span), store, out.shape[1], 256 if last else 384,
    )


def other_rows(layer, core, theirs, taps, near_w, far_w, biases, col, keep, target, cols, step):
    half = near_w.shape[1]
    column(biases[layer : layer + 1, :], col)
    for weights, part in ((near_w, core[0]), (far_w, 1 - core[0])):
        rows = pl.ds(pl.multiple_of(part * half, half), half)

        def store(here, value, rows=rows):
            target(rows, here, value)

        conv_rows(
            taps, lambda here, rows=rows: theirs[rows, here], weights, col[rows, 0:1], keep,
            store, cols, step,
        )


def other_kernel(layer, blocks, core, place, theirs, taps, near_w, far_w, biases, out, col):
    span = theirs.shape[1]

    def target(rows, here, value):
        out[rows, here] = value

    other_rows(
        layer, core, theirs, taps, near_w, far_w, biases, col, keeper(place, blocks, span), target,
        span, 384,
    )


def last_kernel(
    layer, side, core, features, theirs, taps, near_w, far_w, biases, key_w, value_w,
    key_keep, key_send, value_keep, value_send, col, full,
):
    rows, frames = features.shape
    base = (1 - side[0]) * rows
    full[pl.ds(pl.multiple_of(side[0] * rows, rows), rows), :] = features[...]
    half = rows // 2

    def target(part, here, value):
        full[pl.ds(pl.multiple_of(base + part.start, half), half), here] = value

    other_rows(
        layer, core, theirs, taps, near_w, far_w, biases, col, None, target, frames, 256
    )
    for key_out, value_out, part in (
        (key_send, value_send, 1 - core[0]), (key_keep, value_keep, core[0])
    ):
        here = pl.ds(pl.multiple_of(part * half, half), half)
        key_out[...] = dot(key_w[here, :], full[...]).T.astype(jnp.bfloat16)
        value_out[...] = dot(value_w[here, :], full[...]).astype(jnp.bfloat16)


def thirds(value):
    first = value.astype(jnp.bfloat16)
    rest = value - first.astype(jnp.float32)
    second = rest.astype(jnp.bfloat16)
    third = (rest - second.astype(jnp.float32)).astype(jnp.bfloat16)
    return first, second, third


def pack(out, peak, total, weighted):
    out[0:HD, :] = weighted.astype(jnp.bfloat16)
    lines = [line.astype(jnp.float32) for line in thirds(peak) + thirds(total)]
    lines.append(jnp.zeros_like(lines[0]))
    lines.append(jnp.zeros_like(lines[0]))
    out[HD : HD + 8, :] = jnp.concatenate(lines, axis=0).astype(jnp.bfloat16)


def unpack(packed):
    lines = packed[HD : HD + 8, :].astype(jnp.float32)
    peak = lines[0:1] + (lines[1:2] + lines[2:3])
    total = lines[3:4] + (lines[4:5] + lines[5:6])
    return peak, total, packed[0:HD, :].astype(jnp.float32)


SCALE = LOG2E / math.sqrt(HD)


def join(one, two):
    peak = jnp.maximum(one[0], two[0])
    left = jnp.exp2((one[0] - peak) * SCALE)
    right = jnp.exp2((two[0] - peak) * SCALE)
    return peak, one[1] * left + two[1] * right, one[2] * left + two[2] * right


def ordered(info, mine, theirs):
    swap = info[0] == 1
    one = tuple(jnp.where(swap, t, m) for m, t in zip(mine, theirs))
    two = tuple(jnp.where(swap, m, t) for m, t in zip(mine, theirs))
    return one, two


def meet_kernel(peak, total, weighted, *refs):
    state = (peak[...], total[...], weighted[...])
    for theirs in refs[:-1]:
        state = join(state, unpack(theirs))
    pack(refs[-1], *state)


def merge_kernel(info, mine, theirs, out):
    pack(out, *join(*ordered(info, unpack(mine), unpack(theirs))))


def finish_kernel(info, mine, theirs, out):
    _, total, weighted = join(*ordered(info, unpack(mine), unpack(theirs)))
    out[...] = (weighted / total).astype(out.dtype)


def attend_kernel(
    packed, core, which, half, valid_own, valid_rec, key_own, key_rec, value_own, value_rec,
    queries, *refs
):
    outs = refs[:-5]
    keyed, asked, valued, score_a, score_b = refs[-5:]
    frames = key_own.shape[0]
    latents = asked.shape[1]
    tile = score_a.shape[1]
    chunk = frames
    slot = which[0]
    lane = lax.broadcasted_iota(jnp.int32, (frames, 2 * HD), 1)
    frame = lax.broadcasted_iota(jnp.int32, (frames, 2 * HD), 0)
    spare = (1 - slot) * HD
    value_rows = pl.ds(pl.multiple_of(slot * HD, HD), HD)
    for part, (source, valid) in enumerate(((key_own, valid_own), (key_rec, valid_rec))):
        bias = jnp.where(frame < valid[0], 0.0, MASKED)
        keyed[pl.ds(part * frames, frames), :] = jnp.where(
            lane == spare, bias, source[...].astype(jnp.float32)
        ).astype(jnp.bfloat16)
    valued[:, 0:frames] = value_own[value_rows, :]
    valued[:, frames:] = value_rec[value_rows, :]
    row = lax.broadcasted_iota(jnp.int32, (2 * HD, latents), 0)
    wide = queries[
        pl.ds(pl.multiple_of(core[0] * 2 * HD, 2 * HD), 2 * HD),
        pl.ds(pl.multiple_of(half[0] * latents, latents), latents),
    ].astype(jnp.float32)
    wide = jnp.where(row // HD == slot, wide, jnp.where(row == spare, 1.0, 0.0))
    asked[...] = wide.astype(jnp.bfloat16)

    count = latents // tile
    peak = None
    for step in range(count + 1):
        cols = slice(step * tile, (step + 1) * tile)
        done = slice((step - 1) * tile, step * tile)
        now, before = ((score_a, score_b), (score_b, score_a))[step % 2]

        def body(index, carry, step=step, cols=cols, now=now, before=before, peak=peak):
            top, total, weighted = carry
            here = pl.ds(pl.multiple_of(index * chunk, chunk), chunk)
            if step < count:
                value = dot(keyed[here, :], asked[:, cols])
                now[here, :] = value
                top = jnp.maximum(top, jnp.max(value.reshape(chunk // 8, 8, tile), axis=0))
            if step > 0:
                probs = jnp.exp2((before[here, :] - peak) * SCALE)
                total = total + jnp.sum(probs.reshape(chunk // 8, 8, tile), axis=0)
                weighted = weighted + dot(valued[:, here], probs.astype(jnp.bfloat16))
            return top, total, weighted

        top, total, weighted = lax.fori_loop(
            0, 2 * frames // chunk, body,
            (
                jnp.full((8, tile), -jnp.inf, jnp.float32), jnp.zeros((8, tile), jnp.float32),
                jnp.zeros((HD, tile), jnp.float32),
            ),
        )
        if step > 0:
            total = jnp.sum(total, axis=0, keepdims=True)
            if packed:
                pack(outs[0].at[:, done], peak, total, weighted)
            else:
                outs[0][:, done] = peak
                outs[1][:, done] = total
                outs[2][:, done] = weighted
        if step < count:
            peak = jnp.max(top, axis=0, keepdims=True)


def attend(packed, scalars, keys, values, queries):
    latents = queries.shape[1] // 2
    frames = keys[0].shape[0]
    tile = min(256, latents)
    if packed:
        out_shape = jax.ShapeDtypeStruct((HD + 8, latents), jnp.bfloat16)
        out_specs = pl.BlockSpec(memory_space=pltpu.VMEM)
    else:
        out_shape = [
            jax.ShapeDtypeStruct((1, latents), jnp.float32),
            jax.ShapeDtypeStruct((1, latents), jnp.float32),
            jax.ShapeDtypeStruct((HD, latents), jnp.float32),
        ]
        out_specs = whole(3)
    return pl.pallas_call(
        functools.partial(attend_kernel, packed),
        out_shape=out_shape,
        in_specs=smem(5) + whole(5),
        out_specs=out_specs,
        scratch_shapes=[
            VMEM((2 * frames, 2 * HD), jnp.bfloat16),
            VMEM((2 * HD, latents), jnp.bfloat16),
            VMEM((HD, 2 * frames), jnp.bfloat16),
            VMEM((2 * frames, tile), jnp.float32),
            VMEM((2 * frames, tile), jnp.float32),
        ],
        compiler_params=params(20),
        name="attend_send" if packed else "attend_keep",
    )(*scalars, *keys, *values, queries)


def assemble_kernel(core, cross, lower, *refs):
    out = refs[-1]
    latents = refs[0].shape[1]
    mine, theirs = 2 * core[0], 2 - 2 * core[0]
    heads = (mine + cross[0], mine + 1 - cross[0], theirs + cross[0], theirs + 1 - cross[0])
    for index, piece in enumerate(refs[:-1]):
        part = lower[0] if index % 2 == 0 else 1 - lower[0]
        out[
            pl.ds(pl.multiple_of(heads[index // 2] * HD, HD), HD),
            pl.ds(pl.multiple_of(part * latents, latents), latents),
        ] = piece[...]


def simple(kernel, out_shape, scalars, arrays, scratch=(), mib=16, specs=None):
    many = isinstance(out_shape, (list, tuple))
    return pl.pallas_call(
        kernel,
        grid=(1,),
        out_shape=out_shape,
        in_specs=smem(len(scalars)) + (specs or whole(len(arrays))),
        out_specs=whole(len(out_shape)) if many else pl.BlockSpec(memory_space=pltpu.VMEM),
        scratch_shapes=list(scratch),
        compiler_params=params(mib),
    )(*scalars, *arrays)


def pair_device(
    recording, spatial_w, conv_w, conv_b, dilations, valid_frames, key_w, value_w, queries
):
    frames = recording.shape[1]
    ch_loc = conv_w.shape[2]
    ch = conv_w.shape[3]
    half = ch_loc // 2
    latents = queries.shape[1]
    blocks = lax.axis_size("tm")
    side = lax.axis_index("sensor").astype(jnp.int32).reshape(1)
    place = lax.axis_index("tm").astype(jnp.int32).reshape(1)
    core = place & 1
    cross = (place >> 1) & 1
    span = frames + EDGE
    bf16 = jnp.bfloat16
    across = [(0, 1), (1, 0)]
    twins = [(i, i ^ 1) for i in range(blocks)]

    other_rec = lax.ppermute(recording, "sensor", across)
    other_w = lax.ppermute(spatial_w, "sensor", across)
    tail = lax.ppermute(
        recording[:, frames - EDGE :], "tm", [(i, i + 1) for i in range(blocks - 1)]
    )
    head = lax.ppermute(recording[:, :EDGE], "tm", [(i + 1, i) for i in range(blocks - 1)])
    lane = jnp.arange(EDGE, dtype=jnp.int32)[None, :]
    edge = jnp.where(lane < HALF, head, tail)
    other_edge = lax.ppermute(edge, "sensor", across)
    other_b = lax.ppermute(conv_b, "sensor", across)
    later_w = lax.optimization_barrier((conv_w, head))[0]
    mine = [
        lax.dynamic_slice(
            later_w if layer else conv_w, (layer, 0, core[0] * half, 0), (1, 3, half, ch)
        )[0]
        for layer in range(LAYERS)
    ]
    near = [lax.ppermute(mine[n], "sensor", across) for n in range(LAYERS)]
    far = [lax.ppermute(near[n], "tm", twins) for n in range(LAYERS)]
    half_shape = jax.ShapeDtypeStruct((ch_loc, span), bf16)
    parts = (spatial_w, other_w, recording, other_rec, edge, other_edge)
    own_h, other_h = simple(
        first_kernel, [half_shape, half_shape], (side,), parts,
        [VMEM(part.shape, bf16) for part in parts] + [pltpu.SemaphoreType.DMA((len(parts),))],
        specs=[pl.BlockSpec(memory_space=pltpu.HBM)] * len(parts),
    )
    taps_shape = jax.ShapeDtypeStruct((3, ch, span), bf16)
    col = [VMEM((ch_loc, EDGE), jnp.float32)]
    for layer in range(LAYERS):
        last = layer == LAYERS - 1
        specs = whole(4)
        specs[2] = pl.BlockSpec((None, 3, ch_loc, ch), lambda _, layer=layer: (layer, 0, 0, 0))
        made = [jax.ShapeDtypeStruct((ch_loc, frames), bf16)] * 2 if last else [half_shape]
        *own_next, taps = simple(
            functools.partial(own_kernel, layer, blocks, last), made + [taps_shape],
            (dilations, side, place), (own_h, other_h, conv_w, conv_b), col,
            mib=24, specs=specs,
        )
        arrays = (other_h, taps, near[layer], far[layer], other_b)
        if last:
            features, kept_features = own_next
            shapes = [
                jax.ShapeDtypeStruct((frames, half), bf16),
                jax.ShapeDtypeStruct((frames, half), bf16),
                jax.ShapeDtypeStruct((half, frames), bf16),
                jax.ShapeDtypeStruct((half, frames), bf16),
            ]
            key_keep, key_send, value_keep, value_send = simple(
                functools.partial(last_kernel, layer), shapes, (side, core),
                (kept_features,) + arrays + (key_w, value_w), col + [VMEM((ch, frames), bf16)],
                mib=24,
            )
        else:
            other_h = simple(
                functools.partial(other_kernel, layer, blocks), half_shape, (core, place), arrays,
                col, mib=24,
            )
            own_h = own_next[0]
    keys = (key_keep, lax.ppermute(key_send, "tm", twins))
    values = (value_keep, lax.ppermute(value_send, "tm", twins))
    other_valid = lax.ppermute(valid_frames, "tm", twins)

    def flip(value, bit):
        return lax.ppermute(value, "tm", [(i, i ^ bit) for i in range(blocks)])

    lower = (place >> 2) & 1

    def run(packed, slot, part):
        scalars = (core, slot, part, valid_frames, other_valid)
        return attend(packed, scalars, keys, values, queries)

    sent = flip(run(True, 1 - cross, 1 - lower), 2)
    kept = flip(run(True, 1 - cross, lower), 2)
    packed_shape = jax.ShapeDtypeStruct((HD + 8, latents // 2), bf16)
    final_shape = jax.ShapeDtypeStruct((HD, latents // 2), bf16)
    given = run(False, cross, 1 - lower)
    given = simple(meet_kernel, packed_shape, (), (*given, sent))
    given = flip(given, 4)
    held = run(False, cross, lower)
    packed = simple(meet_kernel, packed_shape, (), (*held, kept, given))
    bit = 8
    while bit < blocks:
        theirs = flip(packed, bit)
        which = ((place & bit) != 0).astype(jnp.int32)
        if bit * 2 < blocks:
            packed = simple(merge_kernel, packed_shape, (which,), (packed, theirs))
        else:
            done = simple(finish_kernel, final_shape, (which,), (packed, theirs))
        bit *= 2
    above = flip(done, 4)
    beside = flip(done, 2)
    corner = flip(above, 2)
    pieces = [done, above, beside, corner]
    pieces += [flip(piece, 1) for piece in pieces]
    attended = simple(
        assemble_kernel, jax.ShapeDtypeStruct((ch_loc, latents), bf16), (core, cross, lower),
        pieces,
    )
    return (features, attended)


def fits(mesh):
    sensors, blocks = mesh.shape["sensor"], mesh.shape["tm"]
    return sensors == 2 and blocks >= 16 and blocks & (blocks - 1) == 0


def on_device(*arrays):
    if arrays[6].shape[0] // HD != 4:
        return generic_device(*arrays)
    return pair_device(*arrays)


def solution(mesh):
    quick = fits(mesh)
    return jax.shard_map(
        on_device if quick else generic_device,
        mesh=mesh,
        in_specs=(
            P("sensor", "tm"),
            P(None, "sensor"),
            P(None, None, "sensor", None),
            P(None, "sensor"),
            P(),
            P("tm"),
            P("sensor", None),
            P("sensor", None),
            P("sensor", None),
        ),
        out_specs=(P("sensor", "tm"), P("sensor", None)),
        check_vma=False,
    )
```

```python
import functools
import math

import jax
import jax.numpy as jnp
from jax import lax
from jax.experimental import pallas as pl
from jax.experimental.pallas import tpu as pltpu
from jax.sharding import PartitionSpec as P


HD = 64
LATENTS = 2048
LAYERS = 3
DMAX = 16


def padded(cells, sides, width):
    for axis, dim in sides:
        count = lax.axis_size(axis)
        ends = count - 1
        head = lax.slice_in_dim(cells, 0, width, axis=dim)
        tail = lax.slice_in_dim(cells, cells.shape[dim] - width, cells.shape[dim], axis=dim)
        cells = jnp.concatenate(
            [
                lax.ppermute(tail, axis, [(i, (i + 1) % count) for i in range(ends)]),
                cells,
                lax.ppermute(head, axis, [((i + 1) % count, i) for i in range(ends)]),
            ],
            axis=dim,
        )
    return cells


def tap_folder(kernels, dilation, frames, margin):

    def add_taps(running, portion, first_row):
        portion = jnp.pad(portion, ((0, 0), (margin, margin)))
        for tap_index in range(3):
            kernel = kernels[tap_index]
            offset = DMAX + (tap_index - 1) * dilation
            shifted = lax.dynamic_slice_in_dim(portion, offset, frames, 1)
            running = running + jnp.dot(kernel, shifted, preferred_element_type=jnp.float32)
        return running

    return add_taps


def generic_device(
    recording, spatial_w, conv_w, conv_b, dilations, valid_frames, key_w, value_w, queries
):
    frames = recording.shape[1]
    ch_loc = conv_w.shape[2]
    hidden = lax.psum_scatter(
        jnp.dot(spatial_w, recording, preferred_element_type=jnp.float32),
        "sensor",
        scatter_dimension=0,
        tiled=True,
    ).astype(jnp.bfloat16)
    reach = 3 * DMAX
    extended = padded(hidden, (("tm", 1),), reach)
    span = frames + 2 * reach
    position = lax.axis_index("tm") * frames - reach + jnp.arange(span, dtype=jnp.int32)
    inside = (position >= 0) & (position < frames * lax.axis_size("tm"))
    for layer in range(LAYERS):
        initial = jnp.broadcast_to(conv_b[layer][:, None], (ch_loc, span))
        folder = tap_folder(conv_w[layer], dilations[layer], span, DMAX)
        preact = folder(
            initial, lax.all_gather(extended, "sensor", axis=0, tiled=True), jnp.int32(0)
        )
        updated = extended.astype(jnp.float32) + jax.nn.gelu(preact, approximate=False)
        extended = jnp.where(inside[None, :], updated, 0.0).astype(jnp.bfloat16)
    hidden = extended[:, reach : reach + frames]
    portion = lax.all_gather(hidden, "sensor", axis=0, tiled=True)
    key_rows = jnp.dot(key_w, portion, preferred_element_type=jnp.float32)
    value_rows = jnp.dot(value_w, portion, preferred_element_type=jnp.float32)
    head_count = key_w.shape[0] // HD
    key_heads = key_rows.astype(jnp.bfloat16).reshape(head_count, HD, frames)
    value_heads = value_rows.astype(jnp.bfloat16).reshape(head_count, HD, frames)
    frame_mask = jnp.arange(frames, dtype=jnp.int32) < valid_frames[0]
    block_rows = min(LATENTS, 512)
    block_count = LATENTS // block_rows
    query_blocks = queries.reshape(head_count, HD, block_count, block_rows).transpose(2, 0, 1, 3)
    scale = 1.0 / math.sqrt(HD)

    def attend(query_block):
        scores = (
            jnp.einsum("hdq,hdt->hqt", query_block, key_heads, preferred_element_type=jnp.float32)
            * scale
        )
        scores = jnp.where(frame_mask[None, None, :], scores, -jnp.inf)
        peaks = jnp.max(scores, axis=2)
        probs = jnp.where(frame_mask[None, None, :], jnp.exp(scores - peaks[:, :, None]), 0.0)
        totals = jnp.sum(probs, axis=2)
        weighted = jnp.einsum(
            "hqt,hdt->hdq",
            probs.astype(jnp.bfloat16),
            value_heads,
            preferred_element_type=jnp.float32,
        )
        return (peaks, totals, weighted)

    peaks, totals, weighted = lax.map(attend, query_blocks)
    peaks = peaks.transpose(1, 0, 2).reshape(head_count, LATENTS)
    totals = totals.transpose(1, 0, 2).reshape(head_count, LATENTS)
    weighted = weighted.transpose(1, 2, 0, 3).reshape(head_count, HD, LATENTS)
    global_peaks = lax.pmax(peaks, "tm")
    rescale = jnp.exp(peaks - global_peaks)
    totals, weighted = lax.psum((totals * rescale, weighted * rescale[:, None, :]), "tm")
    attended = (
        (weighted / totals[:, None, :]).reshape(head_count * HD, LATENTS).astype(jnp.bfloat16)
    )
    return (hidden, attended)


VMEM = pltpu.VMEM
EDGE = 128
HALF = EDGE // 2
LOG2E = 1.4426950408889634
MASKED = -1e30


def whole(count):
    return [pl.BlockSpec(memory_space=pltpu.VMEM)] * count


def smem(count):
    return [pl.BlockSpec(memory_space=pltpu.SMEM)] * count


def params(mib):
    return pltpu.CompilerParams(vmem_limit_bytes=mib * 1024 * 1024)


def dot(left, right):
    return jnp.dot(left, right, preferred_element_type=jnp.float32)


def first_kernel(side, *refs):
    sources, (mine, theirs), held, done = refs[:6], refs[6:8], refs[8:14], refs[14]
    copies = [
        pltpu.make_async_copy(source, target, done.at[n])
        for n, (source, target) in enumerate(zip(sources, held))
    ]
    for copy in copies:
        copy.start()
    for copy in copies:
        copy.wait()
    own_w, other_w, own, other, own_edge, other_edge = held
    frames = own.shape[1]
    rows = mine.shape[0]
    for out, part in ((mine, side[0]), (theirs, 1 - side[0])):
        here = pl.ds(pl.multiple_of(part * rows, rows), rows)
        left, right = own_w[here, :], other_w[here, :]
        out[:, :frames] = (dot(left, own[...]) + dot(right, other[...])).astype(out.dtype)
        out[:, frames:] = (dot(left, own_edge[...]) + dot(right, other_edge[...])).astype(out.dtype)


def gelu(value):
    return 0.5 * value * (1.0 + lax.erf(value * (1.0 / math.sqrt(2.0))))


def conv_rows(taps, old, kernel, bias, keep, store, cols, step):
    for start in range(0, cols, step):
        width = min(step, cols - start)
        here = pl.ds(start, width)
        total = dot(kernel[0], taps[0, :, here])
        total = total + dot(kernel[1], taps[1, :, here])
        total = total + dot(kernel[2], taps[2, :, here])
        new = old(here).astype(jnp.float32) + gelu(total + bias)
        if keep is not None and start + width > cols - EDGE:
            new = jnp.where(keep(start, width), new, 0.0)
        store(here, new.astype(jnp.bfloat16))


def column(row, out):
    out[...] = jnp.broadcast_to(row, (EDGE, row.shape[1])).T


def keeper(place, blocks, span):
    frames = span - EDGE

    def keep(start, width):
        lane = lax.broadcasted_iota(jnp.int32, (1, width), 1) + start
        frame = jnp.where(lane < span - HALF, lane, lane - span) + place[0] * frames
        return (frame >= 0) & (frame < blocks * frames)

    return keep


def own_kernel(
    layer, blocks, last, dilations, side, place, mine, theirs, weights, biases, *refs
):
    outs, taps, col = refs[:-2], refs[-2], refs[-1]
    out = outs[0]
    rows, span = mine.shape
    shift = dilations[layer]
    lane = lax.broadcasted_iota(jnp.int32, (rows, EDGE), 1)
    count = span // EDGE
    for part, source in ((side[0], mine), (1 - side[0], theirs)):
        here = pl.ds(pl.multiple_of(part * rows, rows), rows)
        tiles = [source[:, n * EDGE : (n + 1) * EDGE] for n in range(count)]
        later = [pltpu.roll(tile, shift, 1) for tile in tiles]
        sooner = [pltpu.roll(tile, EDGE - shift, 1) for tile in tiles]
        for n in range(count):
            cols = slice(n * EDGE, (n + 1) * EDGE)
            taps[1, here, cols] = tiles[n]
            taps[0, here, cols] = jnp.where(lane < shift, later[n - 1], later[n])
            taps[2, here, cols] = jnp.where(
                lane < EDGE - shift, sooner[n], sooner[(n + 1) % count]
            )
    column(biases[layer : layer + 1, :], col)

    def store(here, value):
        for target in outs:
            target[:, here] = value

    conv_rows(
        taps, lambda here: mine[:, here], weights, col[:, 0:1],
        None if last else keeper(place, blocks, span), store, out.shape[1], 256 if last else 384,
    )


def other_rows(layer, core, theirs, taps, near_w, far_w, biases, col, keep, target, cols, step):
    half = near_w.shape[1]
    column(biases[layer : layer + 1, :], col)
    for weights, part in ((near_w, core[0]), (far_w, 1 - core[0])):
        rows = pl.ds(pl.multiple_of(part * half, half), half)

        def store(here, value, rows=rows):
            target(rows, here, value)

        conv_rows(
            taps, lambda here, rows=rows: theirs[rows, here], weights, col[rows, 0:1], keep,
            store, cols, step,
        )


def other_kernel(layer, blocks, core, place, theirs, taps, near_w, far_w, biases, out, col):
    span = theirs.shape[1]

    def target(rows, here, value):
        out[rows, here] = value

    other_rows(
        layer, core, theirs, taps, near_w, far_w, biases, col, keeper(place, blocks, span), target,
        span, 384,
    )


def last_kernel(
    layer, side, core, features, theirs, taps, near_w, far_w, biases, key_w, value_w,
    key_keep, key_send, value_keep, value_send, col, full,
):
    rows, frames = features.shape
    base = (1 - side[0]) * rows
    full[pl.ds(pl.multiple_of(side[0] * rows, rows), rows), :] = features[...]
    half = rows // 2

    def target(part, here, value):
        full[pl.ds(pl.multiple_of(base + part.start, half), half), here] = value

    other_rows(
        layer, core, theirs, taps, near_w, far_w, biases, col, None, target, frames, 256
    )
    for key_out, value_out, part in (
        (key_send, value_send, 1 - core[0]), (key_keep, value_keep, core[0])
    ):
        here = pl.ds(pl.multiple_of(part * half, half), half)
        key_out[...] = dot(key_w[here, :], full[...]).astype(jnp.bfloat16)
        value_out[...] = dot(value_w[here, :], full[...]).T.astype(jnp.bfloat16)


def thirds(value):
    first = value.astype(jnp.bfloat16)
    rest = value - first.astype(jnp.float32)
    second = rest.astype(jnp.bfloat16)
    third = (rest - second.astype(jnp.float32)).astype(jnp.bfloat16)
    return first, second, third


def pack(out, peak, total, weighted):
    out[0:HD, :] = weighted.astype(jnp.bfloat16)
    lines = [line.astype(jnp.float32) for line in thirds(peak) + thirds(total)]
    lines.append(jnp.zeros_like(lines[0]))
    lines.append(jnp.zeros_like(lines[0]))
    out[HD : HD + 8, :] = jnp.concatenate(lines, axis=0).astype(jnp.bfloat16)


def unpack(packed):
    lines = packed[HD : HD + 8, :].astype(jnp.float32)
    peak = lines[0:1] + (lines[1:2] + lines[2:3])
    total = lines[3:4] + (lines[4:5] + lines[5:6])
    return peak, total, packed[0:HD, :].astype(jnp.float32)


SCALE = LOG2E / math.sqrt(HD)


def join(one, two):
    peak = jnp.maximum(one[0], two[0])
    left = jnp.exp2((one[0] - peak) * SCALE)
    right = jnp.exp2((two[0] - peak) * SCALE)
    return peak, one[1] * left + two[1] * right, one[2] * left + two[2] * right


def ordered(info, mine, theirs):
    swap = info[0] == 1
    one = tuple(jnp.where(swap, t, m) for m, t in zip(mine, theirs))
    two = tuple(jnp.where(swap, m, t) for m, t in zip(mine, theirs))
    return one, two


def meet_kernel(peak, total, weighted, *refs):
    state = (peak[...], total[...], weighted[...])
    for theirs in refs[:-1]:
        state = join(state, unpack(theirs))
    pack(refs[-1], *state)


def merge_kernel(info, mine, theirs, out):
    pack(out, *join(*ordered(info, unpack(mine), unpack(theirs))))


def finish_kernel(info, mine, theirs, out):
    _, total, weighted = join(*ordered(info, unpack(mine), unpack(theirs)))
    out[...] = (weighted / total).astype(out.dtype)


def ask_kernel(core, queries, out):
    rows = 2 * HD
    wide = queries[pl.ds(pl.multiple_of(core[0] * rows, rows), rows), :].astype(jnp.float32)
    out[...] = wide.T.astype(out.dtype)


def attend_kernel(
    packed, which, half, valid_own, valid_rec, key_own, key_rec, value_own, value_rec, queries,
    *refs
):
    outs = refs[:-6]
    asked, keyed, values, score_a, score_b, probs_ref = refs[-6:]
    frames = key_own.shape[1]
    latents = asked.shape[0]
    rows = score_a.shape[0]
    chunk = frames // 2
    slot = which[0]
    spare = (1 - slot) * HD
    row = lax.broadcasted_iota(jnp.int32, (2 * HD, frames), 0)
    frame = lax.broadcasted_iota(jnp.int32, (2 * HD, frames), 1)
    for part, (source, valid) in enumerate(((key_own, valid_own), (key_rec, valid_rec))):
        bias = jnp.where(frame < valid[0], 0.0, MASKED).astype(jnp.bfloat16)
        keyed[:, part * frames : (part + 1) * frames] = jnp.where(row == spare, bias, source[...])
    values[0:frames, :] = value_own[...]
    values[frames:, :] = value_rec[...]
    lane = lax.broadcasted_iota(jnp.int32, (latents, 2 * HD), 1)
    fill = jnp.where(lane == spare, 1.0, 0.0).astype(jnp.bfloat16)
    mine = queries[pl.ds(pl.multiple_of(half[0] * latents, latents), latents), :]
    asked[...] = jnp.where(lane // HD == slot, mine, fill)
    lane = lax.broadcasted_iota(jnp.int32, (rows, 2 * HD), 1)
    count = latents // rows
    peak = None
    for step in range(count + 1):
        now, before = ((score_a, score_b), (score_b, score_a))[step % 2]
        top = None
        total = None
        for start in range(0, 2 * frames, chunk):
            here = slice(start, start + chunk)
            if step < count:
                value = dot(asked[step * rows : (step + 1) * rows, :], keyed[:, here])
                now[:, here] = value
                for n in range(0, chunk, EDGE):
                    part = value[:, n : n + EDGE]
                    top = part if top is None else jnp.maximum(top, part)
            if step > 0:
                probs = jnp.exp2((before[:, here] - peak) * SCALE)
                for n in range(0, chunk, EDGE):
                    part = probs[:, n : n + EDGE]
                    total = part if total is None else total + part
                probs_ref[:, here] = probs.astype(jnp.bfloat16)
        if step > 0:
            weighted = dot(probs_ref[...], values[...])
            total = jnp.sum(total, axis=1, keepdims=True)
            both = jnp.where(
                lane == spare, peak, jnp.where(lane == spare + 1, total, weighted)
            ).T
            kept = jnp.where(slot == 0, both[0:HD, :], both[HD:, :])
            rest = jnp.where(slot == 0, both[HD : HD + 8, :], both[0:8, :])
            done = slice((step - 1) * rows, step * rows)
            if packed:
                pack(outs[0].at[:, done], rest[0:1], rest[1:2], kept)
            else:
                outs[0][:, done] = rest[0:1]
                outs[1][:, done] = rest[1:2]
                outs[2][:, done] = kept
        if step < count:
            peak = jnp.max(top, axis=1, keepdims=True)


def attend(packed, scalars, keys, values, queries):
    latents = queries.shape[0] // 2
    frames = keys[0].shape[1]
    rows = min(EDGE, latents)
    if packed:
        out_shape = jax.ShapeDtypeStruct((HD + 8, latents), jnp.bfloat16)
        out_specs = pl.BlockSpec(memory_space=pltpu.VMEM)
    else:
        out_shape = [
            jax.ShapeDtypeStruct((1, latents), jnp.float32),
            jax.ShapeDtypeStruct((1, latents), jnp.float32),
            jax.ShapeDtypeStruct((HD, latents), jnp.float32),
        ]
        out_specs = whole(3)
    return pl.pallas_call(
        functools.partial(attend_kernel, packed),
        out_shape=out_shape,
        in_specs=smem(4) + whole(5),
        out_specs=out_specs,
        scratch_shapes=[
            VMEM((latents, 2 * HD), jnp.bfloat16),
            VMEM((2 * HD, 2 * frames), jnp.bfloat16),
            VMEM((2 * frames, 2 * HD), jnp.bfloat16),
            VMEM((rows, 2 * frames), jnp.float32),
            VMEM((rows, 2 * frames), jnp.float32),
            VMEM((rows, 2 * frames), jnp.bfloat16),
        ],
        compiler_params=params(20),
        name="attend_send" if packed else "attend_keep",
    )(*scalars, *keys, *values, queries)


def assemble_kernel(core, cross, lower, *refs):
    out = refs[-1]
    latents = refs[0].shape[1]
    mine, theirs = 2 * core[0], 2 - 2 * core[0]
    heads = (mine + cross[0], mine + 1 - cross[0], theirs + cross[0], theirs + 1 - cross[0])
    for index, piece in enumerate(refs[:-1]):
        part = lower[0] if index % 2 == 0 else 1 - lower[0]
        out[
            pl.ds(pl.multiple_of(heads[index // 2] * HD, HD), HD),
            pl.ds(pl.multiple_of(part * latents, latents), latents),
        ] = piece[...]


def simple(kernel, out_shape, scalars, arrays, scratch=(), mib=16, specs=None):
    many = isinstance(out_shape, (list, tuple))
    return pl.pallas_call(
        kernel,
        grid=(1,),
        out_shape=out_shape,
        in_specs=smem(len(scalars)) + (specs or whole(len(arrays))),
        out_specs=whole(len(out_shape)) if many else pl.BlockSpec(memory_space=pltpu.VMEM),
        scratch_shapes=list(scratch),
        compiler_params=params(mib),
    )(*scalars, *arrays)


def pair_device(
    recording, spatial_w, conv_w, conv_b, dilations, valid_frames, key_w, value_w, queries
):
    frames = recording.shape[1]
    ch_loc = conv_w.shape[2]
    ch = conv_w.shape[3]
    half = ch_loc // 2
    latents = queries.shape[1]
    blocks = lax.axis_size("tm")
    side = lax.axis_index("sensor").astype(jnp.int32).reshape(1)
    place = lax.axis_index("tm").astype(jnp.int32).reshape(1)
    core = place & 1
    cross = (place >> 1) & 1
    span = frames + EDGE
    bf16 = jnp.bfloat16
    across = [(0, 1), (1, 0)]
    twins = [(i, i ^ 1) for i in range(blocks)]

    other_rec = lax.ppermute(recording, "sensor", across)
    other_w = lax.ppermute(spatial_w, "sensor", across)
    tail = lax.ppermute(
        recording[:, frames - EDGE :], "tm", [(i, i + 1) for i in range(blocks - 1)]
    )
    head = lax.ppermute(recording[:, :EDGE], "tm", [(i + 1, i) for i in range(blocks - 1)])
    lane = jnp.arange(EDGE, dtype=jnp.int32)[None, :]
    edge = jnp.where(lane < HALF, head, tail)
    other_edge = lax.ppermute(edge, "sensor", across)
    other_b = lax.ppermute(conv_b, "sensor", across)
    later_w = lax.optimization_barrier((conv_w, head))[0]
    mine = [
        lax.dynamic_slice(
            later_w if layer else conv_w, (layer, 0, core[0] * half, 0), (1, 3, half, ch)
        )[0]
        for layer in range(LAYERS)
    ]
    near = [lax.ppermute(mine[n], "sensor", across) for n in range(LAYERS)]
    far = [lax.ppermute(near[n], "tm", twins) for n in range(LAYERS)]
    asked = simple(ask_kernel, jax.ShapeDtypeStruct((latents, half), bf16), (core,), (queries,))
    half_shape = jax.ShapeDtypeStruct((ch_loc, span), bf16)
    parts = (spatial_w, other_w, recording, other_rec, edge, other_edge)
    own_h, other_h = simple(
        first_kernel, [half_shape, half_shape], (side,), parts,
        [VMEM(part.shape, bf16) for part in parts] + [pltpu.SemaphoreType.DMA((len(parts),))],
        specs=[pl.BlockSpec(memory_space=pltpu.HBM)] * len(parts),
    )
    taps_shape = jax.ShapeDtypeStruct((3, ch, span), bf16)
    col = [VMEM((ch_loc, EDGE), jnp.float32)]
    for layer in range(LAYERS):
        last = layer == LAYERS - 1
        specs = whole(4)
        specs[2] = pl.BlockSpec((None, 3, ch_loc, ch), lambda _, layer=layer: (layer, 0, 0, 0))
        made = [jax.ShapeDtypeStruct((ch_loc, frames), bf16)] * 2 if last else [half_shape]
        *own_next, taps = simple(
            functools.partial(own_kernel, layer, blocks, last), made + [taps_shape],
            (dilations, side, place), (own_h, other_h, conv_w, conv_b), col,
            mib=24, specs=specs,
        )
        arrays = (other_h, taps, near[layer], far[layer], other_b)
        if last:
            features, kept_features = own_next
            shapes = [
                jax.ShapeDtypeStruct((half, frames), bf16),
                jax.ShapeDtypeStruct((half, frames), bf16),
                jax.ShapeDtypeStruct((frames, half), bf16),
                jax.ShapeDtypeStruct((frames, half), bf16),
            ]
            key_keep, key_send, value_keep, value_send = simple(
                functools.partial(last_kernel, layer), shapes, (side, core),
                (kept_features,) + arrays + (key_w, value_w), col + [VMEM((ch, frames), bf16)],
                mib=24,
            )
        else:
            other_h = simple(
                functools.partial(other_kernel, layer, blocks), half_shape, (core, place), arrays,
                col, mib=24,
            )
            own_h = own_next[0]
    keys = (key_keep, lax.ppermute(key_send, "tm", twins))
    values = (value_keep, lax.ppermute(value_send, "tm", twins))
    other_valid = lax.ppermute(valid_frames, "tm", twins)

    def flip(value, bit):
        return lax.ppermute(value, "tm", [(i, i ^ bit) for i in range(blocks)])

    lower = (place >> 2) & 1

    def run(packed, slot, part):
        scalars = (slot, part, valid_frames, other_valid)
        return attend(packed, scalars, keys, values, asked)

    sent = flip(run(True, 1 - cross, 1 - lower), 2)
    kept = flip(run(True, 1 - cross, lower), 2)
    packed_shape = jax.ShapeDtypeStruct((HD + 8, latents // 2), bf16)
    final_shape = jax.ShapeDtypeStruct((HD, latents // 2), bf16)
    given = run(False, cross, 1 - lower)
    given = simple(meet_kernel, packed_shape, (), (*given, sent))
    given = flip(given, 4)
    held = run(False, cross, lower)
    packed = simple(meet_kernel, packed_shape, (), (*held, kept, given))
    bit = 8
    while bit < blocks:
        theirs = flip(packed, bit)
        which = ((place & bit) != 0).astype(jnp.int32)
        if bit * 2 < blocks:
            packed = simple(merge_kernel, packed_shape, (which,), (packed, theirs))
        else:
            done = simple(finish_kernel, final_shape, (which,), (packed, theirs))
        bit *= 2
    above = flip(done, 4)
    beside = flip(done, 2)
    corner = flip(above, 2)
    pieces = [done, above, beside, corner]
    pieces += [flip(piece, 1) for piece in pieces]
    attended = simple(
        assemble_kernel, jax.ShapeDtypeStruct((ch_loc, latents), bf16), (core, cross, lower),
        pieces,
    )
    return (features, attended)


def fits(mesh):
    sensors, blocks = mesh.shape["sensor"], mesh.shape["tm"]
    return sensors == 2 and blocks >= 16 and blocks & (blocks - 1) == 0


def on_device(*arrays):
    if arrays[6].shape[0] // HD != 4:
        return generic_device(*arrays)
    return pair_device(*arrays)


def solution(mesh):
    quick = fits(mesh)
    return jax.shard_map(
        on_device if quick else generic_device,
        mesh=mesh,
        in_specs=(
            P("sensor", "tm"),
            P(None, "sensor"),
            P(None, None, "sensor", None),
            P(None, "sensor"),
            P(),
            P("tm"),
            P("sensor", None),
            P("sensor", None),
            P("sensor", None),
        ),
        out_specs=(P("sensor", "tm"), P("sensor", None)),
        check_vma=False,
    )
```

```python
import functools
import math

import jax
import jax.numpy as jnp
from jax import lax
from jax.experimental import pallas as pl
from jax.experimental.pallas import tpu as pltpu
from jax.sharding import PartitionSpec as P


HD = 64
LATENTS = 2048
LAYERS = 3
DMAX = 16


def padded(cells, sides, width):
    for axis, dim in sides:
        count = lax.axis_size(axis)
        ends = count - 1
        head = lax.slice_in_dim(cells, 0, width, axis=dim)
        tail = lax.slice_in_dim(cells, cells.shape[dim] - width, cells.shape[dim], axis=dim)
        cells = jnp.concatenate(
            [
                lax.ppermute(tail, axis, [(i, (i + 1) % count) for i in range(ends)]),
                cells,
                lax.ppermute(head, axis, [((i + 1) % count, i) for i in range(ends)]),
            ],
            axis=dim,
        )
    return cells


def tap_folder(kernels, dilation, frames, margin):

    def add_taps(running, portion, first_row):
        portion = jnp.pad(portion, ((0, 0), (margin, margin)))
        for tap_index in range(3):
            kernel = kernels[tap_index]
            offset = DMAX + (tap_index - 1) * dilation
            shifted = lax.dynamic_slice_in_dim(portion, offset, frames, 1)
            running = running + jnp.dot(kernel, shifted, preferred_element_type=jnp.float32)
        return running

    return add_taps


def generic_device(
    recording, spatial_w, conv_w, conv_b, dilations, valid_frames, key_w, value_w, queries
):
    frames = recording.shape[1]
    ch_loc = conv_w.shape[2]
    hidden = lax.psum_scatter(
        jnp.dot(spatial_w, recording, preferred_element_type=jnp.float32),
        "sensor",
        scatter_dimension=0,
        tiled=True,
    ).astype(jnp.bfloat16)
    reach = 3 * DMAX
    extended = padded(hidden, (("tm", 1),), reach)
    span = frames + 2 * reach
    position = lax.axis_index("tm") * frames - reach + jnp.arange(span, dtype=jnp.int32)
    inside = (position >= 0) & (position < frames * lax.axis_size("tm"))
    for layer in range(LAYERS):
        initial = jnp.broadcast_to(conv_b[layer][:, None], (ch_loc, span))
        folder = tap_folder(conv_w[layer], dilations[layer], span, DMAX)
        preact = folder(
            initial, lax.all_gather(extended, "sensor", axis=0, tiled=True), jnp.int32(0)
        )
        updated = extended.astype(jnp.float32) + jax.nn.gelu(preact, approximate=False)
        extended = jnp.where(inside[None, :], updated, 0.0).astype(jnp.bfloat16)
    hidden = extended[:, reach : reach + frames]
    portion = lax.all_gather(hidden, "sensor", axis=0, tiled=True)
    key_rows = jnp.dot(key_w, portion, preferred_element_type=jnp.float32)
    value_rows = jnp.dot(value_w, portion, preferred_element_type=jnp.float32)
    head_count = key_w.shape[0] // HD
    key_heads = key_rows.astype(jnp.bfloat16).reshape(head_count, HD, frames)
    value_heads = value_rows.astype(jnp.bfloat16).reshape(head_count, HD, frames)
    frame_mask = jnp.arange(frames, dtype=jnp.int32) < valid_frames[0]
    block_rows = min(LATENTS, 512)
    block_count = LATENTS // block_rows
    query_blocks = queries.reshape(head_count, HD, block_count, block_rows).transpose(2, 0, 1, 3)
    scale = 1.0 / math.sqrt(HD)

    def attend(query_block):
        scores = (
            jnp.einsum("hdq,hdt->hqt", query_block, key_heads, preferred_element_type=jnp.float32)
            * scale
        )
        scores = jnp.where(frame_mask[None, None, :], scores, -jnp.inf)
        peaks = jnp.max(scores, axis=2)
        probs = jnp.where(frame_mask[None, None, :], jnp.exp(scores - peaks[:, :, None]), 0.0)
        totals = jnp.sum(probs, axis=2)
        weighted = jnp.einsum(
            "hqt,hdt->hdq",
            probs.astype(jnp.bfloat16),
            value_heads,
            preferred_element_type=jnp.float32,
        )
        return (peaks, totals, weighted)

    peaks, totals, weighted = lax.map(attend, query_blocks)
    peaks = peaks.transpose(1, 0, 2).reshape(head_count, LATENTS)
    totals = totals.transpose(1, 0, 2).reshape(head_count, LATENTS)
    weighted = weighted.transpose(1, 2, 0, 3).reshape(head_count, HD, LATENTS)
    global_peaks = lax.pmax(peaks, "tm")
    rescale = jnp.exp(peaks - global_peaks)
    totals, weighted = lax.psum((totals * rescale, weighted * rescale[:, None, :]), "tm")
    attended = (
        (weighted / totals[:, None, :]).reshape(head_count * HD, LATENTS).astype(jnp.bfloat16)
    )
    return (hidden, attended)


VMEM = pltpu.VMEM
EDGE = 128
HALF = EDGE // 2
LOG2E = 1.4426950408889634
MASKED = -1e30


def whole(count):
    return [pl.BlockSpec(memory_space=pltpu.VMEM)] * count


def smem(count):
    return [pl.BlockSpec(memory_space=pltpu.SMEM)] * count


def params(mib):
    return pltpu.CompilerParams(vmem_limit_bytes=mib * 1024 * 1024)


def dot(left, right):
    return jnp.dot(left, right, preferred_element_type=jnp.float32)


def first_kernel(side, *refs):
    sources, (mine, theirs), held, done = refs[:8], refs[8:10], refs[10:18], refs[18]
    copies = [
        pltpu.make_async_copy(source, target, done.at[n])
        for n, (source, target) in enumerate(zip(sources, held))
    ]
    for copy in copies:
        copy.start()
    for copy in copies:
        copy.wait()
    own_w, other_w, own, other, own_head, own_tail, other_head, other_tail = held
    frames = own.shape[1]
    rows = mine.shape[0]
    lane = lax.broadcasted_iota(jnp.int32, own_head.shape, 1)
    own_edge = jnp.where(lane < HALF, own_head[...], own_tail[...])
    other_edge = jnp.where(lane < HALF, other_head[...], other_tail[...])
    for out, part in ((mine, side[0]), (theirs, 1 - side[0])):
        here = pl.ds(pl.multiple_of(part * rows, rows), rows)
        left, right = own_w[here, :], other_w[here, :]
        out[:, :frames] = (dot(left, own[...]) + dot(right, other[...])).astype(out.dtype)
        out[:, frames:] = (dot(left, own_edge) + dot(right, other_edge)).astype(out.dtype)


def gelu(value):
    return 0.5 * value * (1.0 + lax.erf(value * (1.0 / math.sqrt(2.0))))


def conv_rows(taps, old, kernel, bias, keep, store, cols, step):
    for start in range(0, cols, step):
        width = min(step, cols - start)
        here = pl.ds(start, width)
        total = dot(kernel[0], taps[0, :, here])
        total = total + dot(kernel[1], taps[1, :, here])
        total = total + dot(kernel[2], taps[2, :, here])
        new = old(here).astype(jnp.float32) + gelu(total + bias)
        if keep is not None and start + width > cols - EDGE:
            new = jnp.where(keep(start, width), new, 0.0)
        store(here, new.astype(jnp.bfloat16))


def column(row, out):
    out[...] = jnp.broadcast_to(row, (EDGE, row.shape[1])).T


def keeper(place, blocks, span):
    frames = span - EDGE

    def keep(start, width):
        lane = lax.broadcasted_iota(jnp.int32, (1, width), 1) + start
        frame = jnp.where(lane < span - HALF, lane, lane - span) + place[0] * frames
        return (frame >= 0) & (frame < blocks * frames)

    return keep


def own_kernel(
    layer, blocks, last, dilations, side, place, mine, theirs, weights, biases, *refs
):
    outs, taps, col = refs[:-2], refs[-2], refs[-1]
    out = outs[0]
    rows, span = mine.shape
    shift = dilations[layer]
    lane = lax.broadcasted_iota(jnp.int32, (rows, EDGE), 1)
    count = span // EDGE
    for part, source in ((side[0], mine), (1 - side[0], theirs)):
        here = pl.ds(pl.multiple_of(part * rows, rows), rows)
        tiles = [source[:, n * EDGE : (n + 1) * EDGE] for n in range(count)]
        later = [pltpu.roll(tile, shift, 1) for tile in tiles]
        sooner = [pltpu.roll(tile, EDGE - shift, 1) for tile in tiles]
        for n in range(count):
            cols = slice(n * EDGE, (n + 1) * EDGE)
            taps[1, here, cols] = tiles[n]
            taps[0, here, cols] = jnp.where(lane < shift, later[n - 1], later[n])
            taps[2, here, cols] = jnp.where(
                lane < EDGE - shift, sooner[n], sooner[(n + 1) % count]
            )
    column(biases[layer : layer + 1, :], col)

    def store(here, value):
        for target in outs:
            target[:, here] = value

    conv_rows(
        taps, lambda here: mine[:, here], weights, col[:, 0:1],
        None if last else keeper(place, blocks, span), store, out.shape[1], 256 if last else 384,
    )


def other_rows(layer, core, theirs, taps, near_w, far_w, biases, col, keep, target, cols, step):
    half = near_w.shape[1]
    column(biases[layer : layer + 1, :], col)
    for weights, part in ((near_w, core[0]), (far_w, 1 - core[0])):
        rows = pl.ds(pl.multiple_of(part * half, half), half)

        def store(here, value, rows=rows):
            target(rows, here, value)

        conv_rows(
            taps, lambda here, rows=rows: theirs[rows, here], weights, col[rows, 0:1], keep,
            store, cols, step,
        )


def other_kernel(layer, blocks, core, place, theirs, taps, near_w, far_w, biases, out, col):
    span = theirs.shape[1]

    def target(rows, here, value):
        out[rows, here] = value

    other_rows(
        layer, core, theirs, taps, near_w, far_w, biases, col, keeper(place, blocks, span), target,
        span, 384,
    )


def last_kernel(
    layer, side, core, features, theirs, taps, near_w, far_w, biases, key_w, value_w,
    key_keep, key_send, value_keep, value_send, col, full,
):
    rows, frames = features.shape
    base = (1 - side[0]) * rows
    full[pl.ds(pl.multiple_of(side[0] * rows, rows), rows), :] = features[...]
    half = rows // 2

    def target(part, here, value):
        full[pl.ds(pl.multiple_of(base + part.start, half), half), here] = value

    other_rows(
        layer, core, theirs, taps, near_w, far_w, biases, col, None, target, frames, 256
    )
    for key_out, value_out, part in (
        (key_send, value_send, 1 - core[0]), (key_keep, value_keep, core[0])
    ):
        here = pl.ds(pl.multiple_of(part * half, half), half)
        key_out[...] = dot(key_w[here, :], full[...]).astype(jnp.bfloat16)
        value_out[...] = dot(value_w[here, :], full[...]).T.astype(jnp.bfloat16)


def thirds(value):
    first = value.astype(jnp.bfloat16)
    rest = value - first.astype(jnp.float32)
    second = rest.astype(jnp.bfloat16)
    third = (rest - second.astype(jnp.float32)).astype(jnp.bfloat16)
    return first, second, third


def pack(out, peak, total, weighted):
    out[0:HD, :] = weighted.astype(jnp.bfloat16)
    lines = [line.astype(jnp.float32) for line in thirds(peak) + thirds(total)]
    lines.append(jnp.zeros_like(lines[0]))
    lines.append(jnp.zeros_like(lines[0]))
    out[HD : HD + 8, :] = jnp.concatenate(lines, axis=0).astype(jnp.bfloat16)


def unpack(packed):
    lines = packed[HD : HD + 8, :].astype(jnp.float32)
    peak = lines[0:1] + (lines[1:2] + lines[2:3])
    total = lines[3:4] + (lines[4:5] + lines[5:6])
    return peak, total, packed[0:HD, :].astype(jnp.float32)


SCALE = LOG2E / math.sqrt(HD)


def join(one, two):
    peak = jnp.maximum(one[0], two[0])
    left = jnp.exp2((one[0] - peak) * SCALE)
    right = jnp.exp2((two[0] - peak) * SCALE)
    return peak, one[1] * left + two[1] * right, one[2] * left + two[2] * right


def ordered(info, mine, theirs):
    swap = info[0] == 1
    one = tuple(jnp.where(swap, t, m) for m, t in zip(mine, theirs))
    two = tuple(jnp.where(swap, m, t) for m, t in zip(mine, theirs))
    return one, two


def meet_kernel(peak, total, weighted, *refs):
    state = (peak[...], total[...], weighted[...])
    for theirs in refs[:-1]:
        state = join(state, unpack(theirs))
    pack(refs[-1], *state)


def merge_kernel(info, mine, theirs, out):
    pack(out, *join(*ordered(info, unpack(mine), unpack(theirs))))


def finish_kernel(info, mine, theirs, out):
    _, total, weighted = join(*ordered(info, unpack(mine), unpack(theirs)))
    out[...] = (weighted / total).astype(out.dtype)


def ask_kernel(core, queries, out):
    rows = 2 * HD
    wide = queries[pl.ds(pl.multiple_of(core[0] * rows, rows), rows), :].astype(jnp.float32)
    out[...] = wide.T.astype(out.dtype)


def attend_kernel(
    packed, which, half, valid_own, valid_rec, key_own, key_rec, value_own, value_rec, queries,
    *refs
):
    outs = refs[:-6]
    asked, keyed, values, score_a, score_b, probs_ref = refs[-6:]
    frames = key_own.shape[1]
    latents = asked.shape[0]
    rows = score_a.shape[0]
    chunk = frames // 2
    slot = which[0]
    spare = (1 - slot) * HD
    row = lax.broadcasted_iota(jnp.int32, (2 * HD, frames), 0)
    frame = lax.broadcasted_iota(jnp.int32, (2 * HD, frames), 1)
    for part, (source, valid) in enumerate(((key_own, valid_own), (key_rec, valid_rec))):
        bias = jnp.where(frame < valid[0], 0.0, MASKED).astype(jnp.bfloat16)
        keyed[:, part * frames : (part + 1) * frames] = jnp.where(row == spare, bias, source[...])
    values[0:frames, :] = value_own[...]
    values[frames:, :] = value_rec[...]
    lane = lax.broadcasted_iota(jnp.int32, (latents, 2 * HD), 1)
    fill = jnp.where(lane == spare, 1.0, 0.0).astype(jnp.bfloat16)
    mine = queries[pl.ds(pl.multiple_of(half[0] * latents, latents), latents), :]
    asked[...] = jnp.where(lane // HD == slot, mine, fill)
    lane = lax.broadcasted_iota(jnp.int32, (rows, 2 * HD), 1)
    count = latents // rows
    peak = None
    for step in range(count + 1):
        now, before = ((score_a, score_b), (score_b, score_a))[step % 2]
        top = None
        total = None
        for start in range(0, 2 * frames, chunk):
            here = slice(start, start + chunk)
            if step < count:
                value = dot(asked[step * rows : (step + 1) * rows, :], keyed[:, here])
                now[:, here] = value
                for n in range(0, chunk, EDGE):
                    part = value[:, n : n + EDGE]
                    top = part if top is None else jnp.maximum(top, part)
            if step > 0:
                probs = jnp.exp2((before[:, here] - peak) * SCALE)
                for n in range(0, chunk, EDGE):
                    part = probs[:, n : n + EDGE]
                    total = part if total is None else total + part
                probs_ref[:, here] = probs.astype(jnp.bfloat16)
        if step > 0:
            weighted = dot(probs_ref[...], values[...])
            total = jnp.sum(total, axis=1, keepdims=True)
            both = jnp.where(
                lane == spare, peak, jnp.where(lane == spare + 1, total, weighted)
            ).T
            kept = jnp.where(slot == 0, both[0:HD, :], both[HD:, :])
            rest = jnp.where(slot == 0, both[HD : HD + 8, :], both[0:8, :])
            done = slice((step - 1) * rows, step * rows)
            if packed:
                pack(outs[0].at[:, done], rest[0:1], rest[1:2], kept)
            else:
                outs[0][:, done] = rest[0:1]
                outs[1][:, done] = rest[1:2]
                outs[2][:, done] = kept
        if step < count:
            peak = jnp.max(top, axis=1, keepdims=True)


def attend(packed, scalars, keys, values, queries):
    latents = queries.shape[0] // 2
    frames = keys[0].shape[1]
    rows = min(EDGE, latents)
    if packed:
        out_shape = jax.ShapeDtypeStruct((HD + 8, latents), jnp.bfloat16)
        out_specs = pl.BlockSpec(memory_space=pltpu.VMEM)
    else:
        out_shape = [
            jax.ShapeDtypeStruct((1, latents), jnp.float32),
            jax.ShapeDtypeStruct((1, latents), jnp.float32),
            jax.ShapeDtypeStruct((HD, latents), jnp.float32),
        ]
        out_specs = whole(3)
    return pl.pallas_call(
        functools.partial(attend_kernel, packed),
        out_shape=out_shape,
        in_specs=smem(4) + whole(5),
        out_specs=out_specs,
        scratch_shapes=[
            VMEM((latents, 2 * HD), jnp.bfloat16),
            VMEM((2 * HD, 2 * frames), jnp.bfloat16),
            VMEM((2 * frames, 2 * HD), jnp.bfloat16),
            VMEM((rows, 2 * frames), jnp.float32),
            VMEM((rows, 2 * frames), jnp.float32),
            VMEM((rows, 2 * frames), jnp.bfloat16),
        ],
        compiler_params=params(20),
        name="attend_send" if packed else "attend_keep",
    )(*scalars, *keys, *values, queries)


def assemble_kernel(core, cross, lower, *refs):
    out = refs[-1]
    latents = refs[0].shape[1]
    mine, theirs = 2 * core[0], 2 - 2 * core[0]
    heads = (mine + cross[0], mine + 1 - cross[0], theirs + cross[0], theirs + 1 - cross[0])
    for index, piece in enumerate(refs[:-1]):
        part = lower[0] if index % 2 == 0 else 1 - lower[0]
        out[
            pl.ds(pl.multiple_of(heads[index // 2] * HD, HD), HD),
            pl.ds(pl.multiple_of(part * latents, latents), latents),
        ] = piece[...]


def simple(kernel, out_shape, scalars, arrays, scratch=(), mib=16, specs=None):
    many = isinstance(out_shape, (list, tuple))
    return pl.pallas_call(
        kernel,
        grid=(1,),
        out_shape=out_shape,
        in_specs=smem(len(scalars)) + (specs or whole(len(arrays))),
        out_specs=whole(len(out_shape)) if many else pl.BlockSpec(memory_space=pltpu.VMEM),
        scratch_shapes=list(scratch),
        compiler_params=params(mib),
    )(*scalars, *arrays)


def pair_device(
    recording, spatial_w, conv_w, conv_b, dilations, valid_frames, key_w, value_w, queries
):
    frames = recording.shape[1]
    ch_loc = conv_w.shape[2]
    ch = conv_w.shape[3]
    half = ch_loc // 2
    latents = queries.shape[1]
    blocks = lax.axis_size("tm")
    side = lax.axis_index("sensor").astype(jnp.int32).reshape(1)
    place = lax.axis_index("tm").astype(jnp.int32).reshape(1)
    core = place & 1
    cross = (place >> 1) & 1
    span = frames + EDGE
    bf16 = jnp.bfloat16
    across = [(0, 1), (1, 0)]
    twins = [(i, i ^ 1) for i in range(blocks)]

    other_rec = lax.ppermute(recording, "sensor", across)
    other_w = lax.ppermute(spatial_w, "sensor", across)
    ends = blocks - 1
    last_part, first_part = recording[:, frames - EDGE :], recording[:, :EDGE]
    tail = lax.ppermute(last_part, "tm", [(i, i + 1) for i in range(ends)])
    head = lax.ppermute(first_part, "tm", [(i + 1, i) for i in range(ends)])
    planes = ("sensor", "tm")
    other_tail = lax.ppermute(
        last_part, planes,
        [(s * blocks + i, (1 - s) * blocks + i + 1) for s in range(2) for i in range(ends)],
    )
    other_head = lax.ppermute(
        first_part, planes,
        [(s * blocks + i + 1, (1 - s) * blocks + i) for s in range(2) for i in range(ends)],
    )
    other_b = lax.ppermute(conv_b, "sensor", across)
    later_w = lax.optimization_barrier((conv_w, other_head))[0]
    mine = [
        lax.dynamic_slice(
            later_w if layer else conv_w, (layer, 0, core[0] * half, 0), (1, 3, half, ch)
        )[0]
        for layer in range(LAYERS)
    ]
    near = [lax.ppermute(mine[n], "sensor", across) for n in range(LAYERS)]
    far = [lax.ppermute(near[n], "tm", twins) for n in range(LAYERS)]
    asked = simple(ask_kernel, jax.ShapeDtypeStruct((latents, half), bf16), (core,), (queries,))
    half_shape = jax.ShapeDtypeStruct((ch_loc, span), bf16)
    parts = (spatial_w, other_w, recording, other_rec, head, tail, other_head, other_tail)
    own_h, other_h = simple(
        first_kernel, [half_shape, half_shape], (side,), parts,
        [VMEM(part.shape, bf16) for part in parts] + [pltpu.SemaphoreType.DMA((len(parts),))],
        specs=[pl.BlockSpec(memory_space=pltpu.HBM)] * len(parts),
    )
    taps_shape = jax.ShapeDtypeStruct((3, ch, span), bf16)
    col = [VMEM((ch_loc, EDGE), jnp.float32)]
    for layer in range(LAYERS):
        last = layer == LAYERS - 1
        specs = whole(4)
        specs[2] = pl.BlockSpec((None, 3, ch_loc, ch), lambda _, layer=layer: (layer, 0, 0, 0))
        made = [jax.ShapeDtypeStruct((ch_loc, frames), bf16)] * 2 if last else [half_shape]
        *own_next, taps = simple(
            functools.partial(own_kernel, layer, blocks, last), made + [taps_shape],
            (dilations, side, place), (own_h, other_h, conv_w, conv_b), col,
            mib=24, specs=specs,
        )
        arrays = (other_h, taps, near[layer], far[layer], other_b)
        if last:
            features, kept_features = own_next
            shapes = [
                jax.ShapeDtypeStruct((half, frames), bf16),
                jax.ShapeDtypeStruct((half, frames), bf16),
                jax.ShapeDtypeStruct((frames, half), bf16),
                jax.ShapeDtypeStruct((frames, half), bf16),
            ]
            key_keep, key_send, value_keep, value_send = simple(
                functools.partial(last_kernel, layer), shapes, (side, core),
                (kept_features,) + arrays + (key_w, value_w), col + [VMEM((ch, frames), bf16)],
                mib=24,
            )
        else:
            other_h = simple(
                functools.partial(other_kernel, layer, blocks), half_shape, (core, place), arrays,
                col, mib=24,
            )
            own_h = own_next[0]
    keys = (key_keep, lax.ppermute(key_send, "tm", twins))
    values = (value_keep, lax.ppermute(value_send, "tm", twins))
    other_valid = lax.ppermute(valid_frames, "tm", twins)

    def flip(value, bit):
        return lax.ppermute(value, "tm", [(i, i ^ bit) for i in range(blocks)])

    lower = (place >> 2) & 1

    def run(packed, slot, part):
        scalars = (slot, part, valid_frames, other_valid)
        return attend(packed, scalars, keys, values, asked)

    sent = flip(run(True, 1 - cross, 1 - lower), 2)
    kept = flip(run(True, 1 - cross, lower), 2)
    packed_shape = jax.ShapeDtypeStruct((HD + 8, latents // 2), bf16)
    final_shape = jax.ShapeDtypeStruct((HD, latents // 2), bf16)
    given = run(False, cross, 1 - lower)
    given = simple(meet_kernel, packed_shape, (), (*given, sent))
    given = flip(given, 4)
    held = run(False, cross, lower)
    packed = simple(meet_kernel, packed_shape, (), (*held, kept, given))
    bit = 8
    while bit < blocks:
        theirs = flip(packed, bit)
        which = ((place & bit) != 0).astype(jnp.int32)
        if bit * 2 < blocks:
            packed = simple(merge_kernel, packed_shape, (which,), (packed, theirs))
        else:
            done = simple(finish_kernel, final_shape, (which,), (packed, theirs))
        bit *= 2
    above = flip(done, 4)
    beside = flip(done, 2)
    corner = flip(done, 6)
    pieces = [done, above, beside, corner]
    pieces += [flip(piece, 1) for piece in pieces]
    attended = simple(
        assemble_kernel, jax.ShapeDtypeStruct((ch_loc, latents), bf16), (core, cross, lower),
        pieces,
    )
    return (features, attended)


def fits(mesh):
    sensors, blocks = mesh.shape["sensor"], mesh.shape["tm"]
    return sensors == 2 and blocks >= 16 and blocks & (blocks - 1) == 0


def on_device(*arrays):
    if arrays[6].shape[0] // HD != 4:
        return generic_device(*arrays)
    return pair_device(*arrays)


def solution(mesh):
    quick = fits(mesh)
    return jax.shard_map(
        on_device if quick else generic_device,
        mesh=mesh,
        in_specs=(
            P("sensor", "tm"),
            P(None, "sensor"),
            P(None, None, "sensor", None),
            P(None, "sensor"),
            P(),
            P("tm"),
            P("sensor", None),
            P("sensor", None),
            P("sensor", None),
        ),
        out_specs=(P("sensor", "tm"), P("sensor", None)),
        check_vma=False,
    )
```

```python
import functools
import math

import jax
import jax.numpy as jnp
from jax import lax
from jax.experimental import pallas as pl
from jax.experimental.pallas import tpu as pltpu
from jax.sharding import PartitionSpec as P


HD = 64
LATENTS = 2048
LAYERS = 3
DMAX = 16


def padded(cells, sides, width):
    for axis, dim in sides:
        count = lax.axis_size(axis)
        ends = count - 1
        head = lax.slice_in_dim(cells, 0, width, axis=dim)
        tail = lax.slice_in_dim(cells, cells.shape[dim] - width, cells.shape[dim], axis=dim)
        cells = jnp.concatenate(
            [
                lax.ppermute(tail, axis, [(i, (i + 1) % count) for i in range(ends)]),
                cells,
                lax.ppermute(head, axis, [((i + 1) % count, i) for i in range(ends)]),
            ],
            axis=dim,
        )
    return cells


def tap_folder(kernels, dilation, frames, margin):

    def add_taps(running, portion, first_row):
        portion = jnp.pad(portion, ((0, 0), (margin, margin)))
        for tap_index in range(3):
            kernel = kernels[tap_index]
            offset = DMAX + (tap_index - 1) * dilation
            shifted = lax.dynamic_slice_in_dim(portion, offset, frames, 1)
            running = running + jnp.dot(kernel, shifted, preferred_element_type=jnp.float32)
        return running

    return add_taps


def generic_device(
    recording, spatial_w, conv_w, conv_b, dilations, valid_frames, key_w, value_w, queries
):
    frames = recording.shape[1]
    ch_loc = conv_w.shape[2]
    hidden = lax.psum_scatter(
        jnp.dot(spatial_w, recording, preferred_element_type=jnp.float32),
        "sensor",
        scatter_dimension=0,
        tiled=True,
    ).astype(jnp.bfloat16)
    reach = 3 * DMAX
    extended = padded(hidden, (("tm", 1),), reach)
    span = frames + 2 * reach
    position = lax.axis_index("tm") * frames - reach + jnp.arange(span, dtype=jnp.int32)
    inside = (position >= 0) & (position < frames * lax.axis_size("tm"))
    for layer in range(LAYERS):
        initial = jnp.broadcast_to(conv_b[layer][:, None], (ch_loc, span))
        folder = tap_folder(conv_w[layer], dilations[layer], span, DMAX)
        preact = folder(
            initial, lax.all_gather(extended, "sensor", axis=0, tiled=True), jnp.int32(0)
        )
        updated = extended.astype(jnp.float32) + jax.nn.gelu(preact, approximate=False)
        extended = jnp.where(inside[None, :], updated, 0.0).astype(jnp.bfloat16)
    hidden = extended[:, reach : reach + frames]
    portion = lax.all_gather(hidden, "sensor", axis=0, tiled=True)
    key_rows = jnp.dot(key_w, portion, preferred_element_type=jnp.float32)
    value_rows = jnp.dot(value_w, portion, preferred_element_type=jnp.float32)
    head_count = key_w.shape[0] // HD
    key_heads = key_rows.astype(jnp.bfloat16).reshape(head_count, HD, frames)
    value_heads = value_rows.astype(jnp.bfloat16).reshape(head_count, HD, frames)
    frame_mask = jnp.arange(frames, dtype=jnp.int32) < valid_frames[0]
    block_rows = min(LATENTS, 512)
    block_count = LATENTS // block_rows
    query_blocks = queries.reshape(head_count, HD, block_count, block_rows).transpose(2, 0, 1, 3)
    scale = 1.0 / math.sqrt(HD)

    def attend(query_block):
        scores = (
            jnp.einsum("hdq,hdt->hqt", query_block, key_heads, preferred_element_type=jnp.float32)
            * scale
        )
        scores = jnp.where(frame_mask[None, None, :], scores, -jnp.inf)
        peaks = jnp.max(scores, axis=2)
        probs = jnp.where(frame_mask[None, None, :], jnp.exp(scores - peaks[:, :, None]), 0.0)
        totals = jnp.sum(probs, axis=2)
        weighted = jnp.einsum(
            "hqt,hdt->hdq",
            probs.astype(jnp.bfloat16),
            value_heads,
            preferred_element_type=jnp.float32,
        )
        return (peaks, totals, weighted)

    peaks, totals, weighted = lax.map(attend, query_blocks)
    peaks = peaks.transpose(1, 0, 2).reshape(head_count, LATENTS)
    totals = totals.transpose(1, 0, 2).reshape(head_count, LATENTS)
    weighted = weighted.transpose(1, 2, 0, 3).reshape(head_count, HD, LATENTS)
    global_peaks = lax.pmax(peaks, "tm")
    rescale = jnp.exp(peaks - global_peaks)
    totals, weighted = lax.psum((totals * rescale, weighted * rescale[:, None, :]), "tm")
    attended = (
        (weighted / totals[:, None, :]).reshape(head_count * HD, LATENTS).astype(jnp.bfloat16)
    )
    return (hidden, attended)


VMEM = pltpu.VMEM
EDGE = 128
HALF = EDGE // 2
LOG2E = 1.4426950408889634
MASKED = -1e30


def whole(count):
    return [pl.BlockSpec(memory_space=pltpu.VMEM)] * count


def smem(count):
    return [pl.BlockSpec(memory_space=pltpu.SMEM)] * count


def params(mib):
    return pltpu.CompilerParams(vmem_limit_bytes=mib * 1024 * 1024)


def dot(left, right):
    return jnp.dot(left, right, preferred_element_type=jnp.float32)


def move_all(pairs, done):
    copies = [
        pltpu.make_async_copy(source, target, done.at[n])
        for n, (source, target) in enumerate(pairs)
    ]
    for copy in copies:
        copy.start()
    for copy in copies:
        copy.wait()


def rows_of(part, count):
    return pl.ds(pl.multiple_of(part * count, count), count)


def early_kernel(core, recording, spatial, weights, outer, inner, slab, near, done):
    width = outer.shape[1]
    far = recording.shape[1] - width
    here = pl.ds(pl.multiple_of(core[0] * far, width), width)
    there = pl.ds(pl.multiple_of((1 - core[0]) * far, width), width)
    move_all(
        (
            (recording.at[:, here], outer),
            (recording.at[:, there], inner),
            (spatial.at[rows_of(core[0], slab.shape[0]), :], slab),
            (weights.at[0, :, rows_of(core[0], near.shape[1]), :], near),
        ),
        done,
    )


def later_kernel(core, weights, *refs):
    pairs = []
    for layer, near in enumerate(refs[:-1]):
        pairs.append((weights.at[layer + 1, :, rows_of(core[0], near.shape[1]), :], near))
    move_all(pairs, refs[-1])


def first_kernel(side, core, *refs):
    sources, (mine, theirs), kept, done = refs[:7], refs[7:9], refs[9:15], refs[15]
    near_w, far_w = sources[:2]
    own_w, own, own_edge, held_w, held, held_edge = kept
    slab = near_w.shape[0]
    move_all(
        (
            (near_w, held_w.at[rows_of(core[0], slab), :]),
            (far_w, held_w.at[rows_of(1 - core[0], slab), :]),
            *zip(sources[2:], (own_w, own, own_edge, held, held_edge)),
        ),
        done,
    )
    frames = own.shape[1]
    rows = mine.shape[0]
    for out, part in ((mine, side[0]), (theirs, 1 - side[0])):
        here = rows_of(part, rows)
        left, right = own_w[here, :], held_w[here, :]
        out[:, :frames] = (dot(left, own[...]) + dot(right, held[...])).astype(out.dtype)
        out[:, frames:] = (dot(left, own_edge[...]) + dot(right, held_edge[...])).astype(out.dtype)


def gelu(value):
    return 0.5 * value * (1.0 + lax.erf(value * (1.0 / math.sqrt(2.0))))


def conv_rows(taps, old, kernel, bias, keep, store, cols, step):
    for start in range(0, cols, step):
        width = min(step, cols - start)
        here = pl.ds(start, width)
        total = dot(kernel[0], taps[0, :, here])
        total = total + dot(kernel[1], taps[1, :, here])
        total = total + dot(kernel[2], taps[2, :, here])
        new = old(here).astype(jnp.float32) + gelu(total + bias)
        if keep is not None and start + width > cols - EDGE:
            new = jnp.where(keep(start, width), new, 0.0)
        store(here, new.astype(jnp.bfloat16))


def column(row, out):
    out[...] = jnp.broadcast_to(row, (EDGE, row.shape[1])).T


def keeper(place, blocks, span):
    frames = span - EDGE

    def keep(start, width):
        lane = lax.broadcasted_iota(jnp.int32, (1, width), 1) + start
        frame = jnp.where(lane < span - HALF, lane, lane - span) + place[0] * frames
        return (frame >= 0) & (frame < blocks * frames)

    return keep


def own_kernel(
    layer, blocks, last, dilations, side, place, mine, theirs, weights, biases, *refs
):
    outs, taps, col = refs[:-2], refs[-2], refs[-1]
    out = outs[0]
    rows, span = mine.shape
    shift = dilations[layer]
    lane = lax.broadcasted_iota(jnp.int32, (rows, EDGE), 1)
    count = span // EDGE
    for part, source in ((side[0], mine), (1 - side[0], theirs)):
        here = pl.ds(pl.multiple_of(part * rows, rows), rows)
        tiles = [source[:, n * EDGE : (n + 1) * EDGE] for n in range(count)]
        later = [pltpu.roll(tile, shift, 1) for tile in tiles]
        sooner = [pltpu.roll(tile, EDGE - shift, 1) for tile in tiles]
        for n in range(count):
            cols = slice(n * EDGE, (n + 1) * EDGE)
            taps[1, here, cols] = tiles[n]
            taps[0, here, cols] = jnp.where(lane < shift, later[n - 1], later[n])
            taps[2, here, cols] = jnp.where(
                lane < EDGE - shift, sooner[n], sooner[(n + 1) % count]
            )
    column(biases[layer : layer + 1, :], col)

    def store(here, value):
        for target in outs:
            target[:, here] = value

    conv_rows(
        taps, lambda here: mine[:, here], weights, col[:, 0:1],
        None if last else keeper(place, blocks, span), store, out.shape[1], 256 if last else 384,
    )


def other_rows(layer, core, theirs, taps, near_w, far_w, biases, col, keep, target, cols, step):
    half = near_w.shape[1]
    column(biases[layer : layer + 1, :], col)
    for weights, part in ((near_w, core[0]), (far_w, 1 - core[0])):
        rows = pl.ds(pl.multiple_of(part * half, half), half)

        def store(here, value, rows=rows):
            target(rows, here, value)

        conv_rows(
            taps, lambda here, rows=rows: theirs[rows, here], weights, col[rows, 0:1], keep,
            store, cols, step,
        )


def other_kernel(layer, blocks, core, place, theirs, taps, near_w, far_w, biases, out, col):
    span = theirs.shape[1]

    def target(rows, here, value):
        out[rows, here] = value

    other_rows(
        layer, core, theirs, taps, near_w, far_w, biases, col, keeper(place, blocks, span), target,
        span, 384,
    )


def last_kernel(
    layer, side, core, features, theirs, taps, near_w, far_w, biases, key_w, value_w,
    key_keep, key_send, value_keep, value_send, col, full,
):
    rows, frames = features.shape
    base = (1 - side[0]) * rows
    full[pl.ds(pl.multiple_of(side[0] * rows, rows), rows), :] = features[...]
    half = rows // 2

    def target(part, here, value):
        full[pl.ds(pl.multiple_of(base + part.start, half), half), here] = value

    other_rows(
        layer, core, theirs, taps, near_w, far_w, biases, col, None, target, frames, 256
    )
    for key_out, value_out, part in (
        (key_send, value_send, 1 - core[0]), (key_keep, value_keep, core[0])
    ):
        here = pl.ds(pl.multiple_of(part * half, half), half)
        key_out[...] = dot(key_w[here, :], full[...]).astype(jnp.bfloat16)
        value_out[...] = dot(value_w[here, :], full[...]).T.astype(jnp.bfloat16)


def thirds(value):
    first = value.astype(jnp.bfloat16)
    rest = value - first.astype(jnp.float32)
    second = rest.astype(jnp.bfloat16)
    third = (rest - second.astype(jnp.float32)).astype(jnp.bfloat16)
    return first, second, third


def pack(out, peak, total, weighted):
    out[0:HD, :] = weighted.astype(jnp.bfloat16)
    lines = [line.astype(jnp.float32) for line in thirds(peak) + thirds(total)]
    lines.append(jnp.zeros_like(lines[0]))
    lines.append(jnp.zeros_like(lines[0]))
    out[HD : HD + 8, :] = jnp.concatenate(lines, axis=0).astype(jnp.bfloat16)


def unpack(packed):
    lines = packed[HD : HD + 8, :].astype(jnp.float32)
    peak = lines[0:1] + (lines[1:2] + lines[2:3])
    total = lines[3:4] + (lines[4:5] + lines[5:6])
    return peak, total, packed[0:HD, :].astype(jnp.float32)


SCALE = LOG2E / math.sqrt(HD)


def join(one, two):
    peak = jnp.maximum(one[0], two[0])
    left = jnp.exp2((one[0] - peak) * SCALE)
    right = jnp.exp2((two[0] - peak) * SCALE)
    return peak, one[1] * left + two[1] * right, one[2] * left + two[2] * right


def ordered(info, mine, theirs):
    swap = info[0] == 1
    one = tuple(jnp.where(swap, t, m) for m, t in zip(mine, theirs))
    two = tuple(jnp.where(swap, m, t) for m, t in zip(mine, theirs))
    return one, two


def meet_kernel(peak, total, weighted, *refs):
    state = (peak[...], total[...], weighted[...])
    for theirs in refs[:-1]:
        state = join(state, unpack(theirs))
    pack(refs[-1], *state)


def merge_kernel(info, mine, theirs, out):
    pack(out, *join(*ordered(info, unpack(mine), unpack(theirs))))


def finish_kernel(info, mine, theirs, out):
    _, total, weighted = join(*ordered(info, unpack(mine), unpack(theirs)))
    out[...] = (weighted / total).astype(out.dtype)


def ask_kernel(core, queries, out):
    rows = 2 * HD
    wide = queries[pl.ds(pl.multiple_of(core[0] * rows, rows), rows), :].astype(jnp.float32)
    out[...] = wide.T.astype(out.dtype)


def attend_kernel(
    packed, which, half, valid_own, valid_rec, key_own, key_rec, value_own, value_rec, queries,
    *refs
):
    outs = refs[:-6]
    asked, keyed, values, score_a, score_b, probs_ref = refs[-6:]
    frames = key_own.shape[1]
    latents = asked.shape[0]
    rows = score_a.shape[0]
    chunk = frames // 2
    slot = which[0]
    spare = (1 - slot) * HD
    row = lax.broadcasted_iota(jnp.int32, (2 * HD, frames), 0)
    frame = lax.broadcasted_iota(jnp.int32, (2 * HD, frames), 1)
    for part, (source, valid) in enumerate(((key_own, valid_own), (key_rec, valid_rec))):
        bias = jnp.where(frame < valid[0], 0.0, MASKED).astype(jnp.bfloat16)
        keyed[:, part * frames : (part + 1) * frames] = jnp.where(row == spare, bias, source[...])
    values[0:frames, :] = value_own[...]
    values[frames:, :] = value_rec[...]
    lane = lax.broadcasted_iota(jnp.int32, (latents, 2 * HD), 1)
    fill = jnp.where(lane == spare, 1.0, 0.0).astype(jnp.bfloat16)
    mine = queries[pl.ds(pl.multiple_of(half[0] * latents, latents), latents), :]
    asked[...] = jnp.where(lane // HD == slot, mine, fill)
    lane = lax.broadcasted_iota(jnp.int32, (rows, 2 * HD), 1)
    count = latents // rows
    peak = None
    for step in range(count + 1):
        now, before = ((score_a, score_b), (score_b, score_a))[step % 2]
        top = None
        total = None
        for start in range(0, 2 * frames, chunk):
            here = slice(start, start + chunk)
            if step < count:
                value = dot(asked[step * rows : (step + 1) * rows, :], keyed[:, here])
                now[:, here] = value
                for n in range(0, chunk, EDGE):
                    part = value[:, n : n + EDGE]
                    top = part if top is None else jnp.maximum(top, part)
            if step > 0:
                probs = jnp.exp2((before[:, here] - peak) * SCALE)
                for n in range(0, chunk, EDGE):
                    part = probs[:, n : n + EDGE]
                    total = part if total is None else total + part
                probs_ref[:, here] = probs.astype(jnp.bfloat16)
        if step > 0:
            weighted = dot(probs_ref[...], values[...])
            total = jnp.sum(total, axis=1, keepdims=True)
            both = jnp.where(
                lane == spare, peak, jnp.where(lane == spare + 1, total, weighted)
            ).T
            kept = jnp.where(slot == 0, both[0:HD, :], both[HD:, :])
            rest = jnp.where(slot == 0, both[HD : HD + 8, :], both[0:8, :])
            done = slice((step - 1) * rows, step * rows)
            if packed:
                pack(outs[0].at[:, done], rest[0:1], rest[1:2], kept)
            else:
                outs[0][:, done] = rest[0:1]
                outs[1][:, done] = rest[1:2]
                outs[2][:, done] = kept
        if step < count:
            peak = jnp.max(top, axis=1, keepdims=True)


def attend(packed, scalars, keys, values, queries):
    latents = queries.shape[0] // 2
    frames = keys[0].shape[1]
    rows = min(EDGE, latents)
    if packed:
        out_shape = jax.ShapeDtypeStruct((HD + 8, latents), jnp.bfloat16)
        out_specs = pl.BlockSpec(memory_space=pltpu.VMEM)
    else:
        out_shape = [
            jax.ShapeDtypeStruct((1, latents), jnp.float32),
            jax.ShapeDtypeStruct((1, latents), jnp.float32),
            jax.ShapeDtypeStruct((HD, latents), jnp.float32),
        ]
        out_specs = whole(3)
    return pl.pallas_call(
        functools.partial(attend_kernel, packed),
        out_shape=out_shape,
        in_specs=smem(4) + whole(5),
        out_specs=out_specs,
        scratch_shapes=[
            VMEM((latents, 2 * HD), jnp.bfloat16),
            VMEM((2 * HD, 2 * frames), jnp.bfloat16),
            VMEM((2 * frames, 2 * HD), jnp.bfloat16),
            VMEM((rows, 2 * frames), jnp.float32),
            VMEM((rows, 2 * frames), jnp.float32),
            VMEM((rows, 2 * frames), jnp.bfloat16),
        ],
        compiler_params=params(20),
        name="attend_send" if packed else "attend_keep",
    )(*scalars, *keys, *values, queries)


def assemble_kernel(core, cross, lower, *refs):
    pieces, out, done = refs[:-2], refs[-2], refs[-1]
    latents = pieces[0].shape[1]
    mine, theirs = 2 * core[0], 2 - 2 * core[0]
    heads = (mine + cross[0], mine + 1 - cross[0], theirs + cross[0], theirs + 1 - cross[0])
    pairs = []
    for index, piece in enumerate(pieces):
        part = lower[0] if index % 2 == 0 else 1 - lower[0]
        cols = pl.ds(pl.multiple_of(part * latents, latents), latents)
        pairs.append((piece, out.at[rows_of(heads[index // 2], HD), cols]))
    move_all(pairs, done)


def simple(
    kernel, out_shape, scalars, arrays, scratch=(), mib=16, specs=None, out_space=pltpu.VMEM
):
    many = isinstance(out_shape, (list, tuple))
    return pl.pallas_call(
        kernel,
        grid=(1,),
        out_shape=out_shape,
        in_specs=smem(len(scalars)) + (specs or whole(len(arrays))),
        out_specs=whole(len(out_shape)) if many else pl.BlockSpec(memory_space=out_space),
        scratch_shapes=list(scratch),
        compiler_params=params(mib),
    )(*scalars, *arrays)


def pair_device(
    recording, spatial_w, conv_w, conv_b, dilations, valid_frames, key_w, value_w, queries
):
    frames = recording.shape[1]
    ch_loc = conv_w.shape[2]
    ch = conv_w.shape[3]
    half = ch_loc // 2
    latents = queries.shape[1]
    blocks = lax.axis_size("tm")
    side = lax.axis_index("sensor").astype(jnp.int32).reshape(1)
    place = lax.axis_index("tm").astype(jnp.int32).reshape(1)
    core = place & 1
    cross = (place >> 1) & 1
    span = frames + EDGE
    bf16 = jnp.bfloat16
    across = [(0, 1), (1, 0)]
    twins = [(i, i ^ 1) for i in range(blocks)]

    other_rec = lax.ppermute(recording, "sensor", across)
    even = core[0] == 0
    slab = ch // 2
    params_in = (recording, spatial_w, conv_w)
    hbm = [pl.BlockSpec(memory_space=pltpu.HBM)]
    near_shape = jax.ShapeDtypeStruct((3, half, ch), bf16)
    edge_shape = jax.ShapeDtypeStruct((recording.shape[0], EDGE), bf16)
    outer, inner, slab_w, *mine = simple(
        early_kernel,
        [edge_shape, edge_shape, jax.ShapeDtypeStruct((slab, spatial_w.shape[1]), bf16), near_shape],
        (core,), params_in, [pltpu.SemaphoreType.DMA((4,))], mib=62, specs=hbm * 3,
    )
    mine += simple(
        later_kernel, [near_shape] * (LAYERS - 1), (core,), (conv_w,),
        [pltpu.SemaphoreType.DMA((LAYERS - 1,))], mib=62, specs=hbm,
    )
    near_sp = lax.ppermute(slab_w, "sensor", across)
    far_sp = lax.ppermute(near_sp, "tm", twins)
    links = [(i, i + 1) for i in range(1, blocks - 1, 2)]
    outer = lax.ppermute(outer, "tm", links + [(j, i) for i, j in links])
    inner = lax.ppermute(inner, "tm", twins)
    lane = jnp.arange(EDGE, dtype=jnp.int32)[None, :]
    edge = jnp.where((lane < HALF) == even, inner, outer)
    other_edge = lax.ppermute(edge, "sensor", across)
    other_b = lax.ppermute(conv_b, "sensor", across)
    near = [lax.ppermute(mine[n], "sensor", across) for n in range(LAYERS)]
    far = [lax.ppermute(near[n], "tm", twins) for n in range(LAYERS)]
    asked = simple(ask_kernel, jax.ShapeDtypeStruct((latents, half), bf16), (core,), (queries,))
    half_shape = jax.ShapeDtypeStruct((ch_loc, span), bf16)
    own_h, other_h = simple(
        first_kernel, [half_shape, half_shape], (side, core),
        (near_sp, far_sp, spatial_w, recording, edge, other_rec, other_edge),
        [VMEM(part.shape, bf16) for part in (spatial_w, recording, edge) * 2]
        + [pltpu.SemaphoreType.DMA((7,))],
        specs=hbm * 7,
    )
    taps_shape = jax.ShapeDtypeStruct((3, ch, span), bf16)
    col = [VMEM((ch_loc, EDGE), jnp.float32)]
    for layer in range(LAYERS):
        last = layer == LAYERS - 1
        specs = whole(4)
        specs[2] = pl.BlockSpec((None, 3, ch_loc, ch), lambda _, layer=layer: (layer, 0, 0, 0))
        made = [jax.ShapeDtypeStruct((ch_loc, frames), bf16)] * 2 if last else [half_shape]
        *own_next, taps = simple(
            functools.partial(own_kernel, layer, blocks, last), made + [taps_shape],
            (dilations, side, place), (own_h, other_h, conv_w, conv_b), col,
            mib=24, specs=specs,
        )
        arrays = (other_h, taps, near[layer], far[layer], other_b)
        if last:
            features, kept_features = own_next
            shapes = [
                jax.ShapeDtypeStruct((half, frames), bf16),
                jax.ShapeDtypeStruct((half, frames), bf16),
                jax.ShapeDtypeStruct((frames, half), bf16),
                jax.ShapeDtypeStruct((frames, half), bf16),
            ]
            key_keep, key_send, value_keep, value_send = simple(
                functools.partial(last_kernel, layer), shapes, (side, core),
                (kept_features,) + arrays + (key_w, value_w), col + [VMEM((ch, frames), bf16)],
                mib=24,
            )
        else:
            other_h = simple(
                functools.partial(other_kernel, layer, blocks), half_shape, (core, place), arrays,
                col, mib=24,
            )
            own_h = own_next[0]
    keys = (key_keep, lax.ppermute(key_send, "tm", twins))
    values = (value_keep, lax.ppermute(value_send, "tm", twins))
    other_valid = lax.ppermute(valid_frames, "tm", twins)

    def flip(value, bit):
        return lax.ppermute(value, "tm", [(i, i ^ bit) for i in range(blocks)])

    lower = (place >> 2) & 1

    def run(packed, slot, part):
        scalars = (slot, part, valid_frames, other_valid)
        return attend(packed, scalars, keys, values, asked)

    sent = flip(run(True, 1 - cross, 1 - lower), 2)
    kept = flip(run(True, 1 - cross, lower), 2)
    packed_shape = jax.ShapeDtypeStruct((HD + 8, latents // 2), bf16)
    final_shape = jax.ShapeDtypeStruct((HD, latents // 2), bf16)
    given = run(False, cross, 1 - lower)
    given = simple(meet_kernel, packed_shape, (), (*given, sent))
    given = flip(given, 4)
    held = run(False, cross, lower)
    packed = simple(meet_kernel, packed_shape, (), (*held, kept, given))
    bit = 8
    while bit < blocks:
        theirs = flip(packed, bit)
        which = ((place & bit) != 0).astype(jnp.int32)
        if bit * 2 < blocks:
            packed = simple(merge_kernel, packed_shape, (which,), (packed, theirs))
        else:
            done = simple(finish_kernel, final_shape, (which,), (packed, theirs))
        bit *= 2
    above = flip(done, 4)
    beside = flip(done, 2)
    corner = flip(done, 6)
    pieces = [done, above, beside, corner]
    pieces += [flip(piece, 1) for piece in pieces]
    attended = simple(
        assemble_kernel, jax.ShapeDtypeStruct((ch_loc, latents), bf16), (core, cross, lower),
        pieces, [pltpu.SemaphoreType.DMA((len(pieces),))], out_space=pltpu.HBM,
    )
    return (features, attended)


def fits(mesh):
    sensors, blocks = mesh.shape["sensor"], mesh.shape["tm"]
    return sensors == 2 and blocks >= 16 and blocks & (blocks - 1) == 0


def on_device(*arrays):
    if arrays[6].shape[0] // HD != 4:
        return generic_device(*arrays)
    return pair_device(*arrays)


def solution(mesh):
    quick = fits(mesh)
    return jax.shard_map(
        on_device if quick else generic_device,
        mesh=mesh,
        in_specs=(
            P("sensor", "tm"),
            P(None, "sensor"),
            P(None, None, "sensor", None),
            P(None, "sensor"),
            P(),
            P("tm"),
            P("sensor", None),
            P("sensor", None),
            P("sensor", None),
        ),
        out_specs=(P("sensor", "tm"), P("sensor", None)),
        check_vma=False,
    )
```

```python
import functools
import math

import jax
import jax.numpy as jnp
from jax import lax
from jax.experimental import pallas as pl
from jax.experimental.pallas import tpu as pltpu
from jax.sharding import PartitionSpec as P


HD = 64
LATENTS = 2048
LAYERS = 3
DMAX = 16


def padded(cells, sides, width):
    for axis, dim in sides:
        count = lax.axis_size(axis)
        ends = count - 1
        head = lax.slice_in_dim(cells, 0, width, axis=dim)
        tail = lax.slice_in_dim(cells, cells.shape[dim] - width, cells.shape[dim], axis=dim)
        cells = jnp.concatenate(
            [
                lax.ppermute(tail, axis, [(i, (i + 1) % count) for i in range(ends)]),
                cells,
                lax.ppermute(head, axis, [((i + 1) % count, i) for i in range(ends)]),
            ],
            axis=dim,
        )
    return cells


def tap_folder(kernels, dilation, frames, margin):

    def add_taps(running, portion, first_row):
        portion = jnp.pad(portion, ((0, 0), (margin, margin)))
        for tap_index in range(3):
            kernel = kernels[tap_index]
            offset = DMAX + (tap_index - 1) * dilation
            shifted = lax.dynamic_slice_in_dim(portion, offset, frames, 1)
            running = running + jnp.dot(kernel, shifted, preferred_element_type=jnp.float32)
        return running

    return add_taps


def generic_device(
    recording, spatial_w, conv_w, conv_b, dilations, valid_frames, key_w, value_w, queries
):
    frames = recording.shape[1]
    ch_loc = conv_w.shape[2]
    hidden = lax.psum_scatter(
        jnp.dot(spatial_w, recording, preferred_element_type=jnp.float32),
        "sensor",
        scatter_dimension=0,
        tiled=True,
    ).astype(jnp.bfloat16)
    reach = 3 * DMAX
    extended = padded(hidden, (("tm", 1),), reach)
    span = frames + 2 * reach
    position = lax.axis_index("tm") * frames - reach + jnp.arange(span, dtype=jnp.int32)
    inside = (position >= 0) & (position < frames * lax.axis_size("tm"))
    for layer in range(LAYERS):
        initial = jnp.broadcast_to(conv_b[layer][:, None], (ch_loc, span))
        folder = tap_folder(conv_w[layer], dilations[layer], span, DMAX)
        preact = folder(
            initial, lax.all_gather(extended, "sensor", axis=0, tiled=True), jnp.int32(0)
        )
        updated = extended.astype(jnp.float32) + jax.nn.gelu(preact, approximate=False)
        extended = jnp.where(inside[None, :], updated, 0.0).astype(jnp.bfloat16)
    hidden = extended[:, reach : reach + frames]
    portion = lax.all_gather(hidden, "sensor", axis=0, tiled=True)
    key_rows = jnp.dot(key_w, portion, preferred_element_type=jnp.float32)
    value_rows = jnp.dot(value_w, portion, preferred_element_type=jnp.float32)
    head_count = key_w.shape[0] // HD
    key_heads = key_rows.astype(jnp.bfloat16).reshape(head_count, HD, frames)
    value_heads = value_rows.astype(jnp.bfloat16).reshape(head_count, HD, frames)
    frame_mask = jnp.arange(frames, dtype=jnp.int32) < valid_frames[0]
    block_rows = min(LATENTS, 512)
    block_count = LATENTS // block_rows
    query_blocks = queries.reshape(head_count, HD, block_count, block_rows).transpose(2, 0, 1, 3)
    scale = 1.0 / math.sqrt(HD)

    def attend(query_block):
        scores = (
            jnp.einsum("hdq,hdt->hqt", query_block, key_heads, preferred_element_type=jnp.float32)
            * scale
        )
        scores = jnp.where(frame_mask[None, None, :], scores, -jnp.inf)
        peaks = jnp.max(scores, axis=2)
        probs = jnp.where(frame_mask[None, None, :], jnp.exp(scores - peaks[:, :, None]), 0.0)
        totals = jnp.sum(probs, axis=2)
        weighted = jnp.einsum(
            "hqt,hdt->hdq",
            probs.astype(jnp.bfloat16),
            value_heads,
            preferred_element_type=jnp.float32,
        )
        return (peaks, totals, weighted)

    peaks, totals, weighted = lax.map(attend, query_blocks)
    peaks = peaks.transpose(1, 0, 2).reshape(head_count, LATENTS)
    totals = totals.transpose(1, 0, 2).reshape(head_count, LATENTS)
    weighted = weighted.transpose(1, 2, 0, 3).reshape(head_count, HD, LATENTS)
    global_peaks = lax.pmax(peaks, "tm")
    rescale = jnp.exp(peaks - global_peaks)
    totals, weighted = lax.psum((totals * rescale, weighted * rescale[:, None, :]), "tm")
    attended = (
        (weighted / totals[:, None, :]).reshape(head_count * HD, LATENTS).astype(jnp.bfloat16)
    )
    return (hidden, attended)


VMEM = pltpu.VMEM
EDGE = 128
HALF = EDGE // 2
LOG2E = 1.4426950408889634
MASKED = -1e30


def whole(count):
    return [pl.BlockSpec(memory_space=pltpu.VMEM)] * count


def smem(count):
    return [pl.BlockSpec(memory_space=pltpu.SMEM)] * count


def params(mib):
    return pltpu.CompilerParams(vmem_limit_bytes=mib * 1024 * 1024)


def dot(left, right):
    return jnp.dot(left, right, preferred_element_type=jnp.float32)


def rows_of(part, count):
    return pl.ds(pl.multiple_of(part * count, count), count)


def first_kernel(side, core, *refs):
    sources, (mine, theirs), held, done = refs[:7], refs[7:9], refs[9:15], refs[15]
    slab = sources[0].shape[0]
    own_w, own, own_edge, other_w, other, other_edge = held
    targets = (
        other_w.at[rows_of(core[0], slab), :], other_w.at[rows_of(1 - core[0], slab), :],
        own_w, own, own_edge, other, other_edge,
    )
    copies = [
        pltpu.make_async_copy(source, target, done.at[n])
        for n, (source, target) in enumerate(zip(sources, targets))
    ]
    for copy in copies:
        copy.start()
    for copy in copies:
        copy.wait()
    frames = own.shape[1]
    rows = mine.shape[0]
    for out, part in ((mine, side[0]), (theirs, 1 - side[0])):
        here = rows_of(part, rows)
        left, right = own_w[here, :], other_w[here, :]
        out[:, :frames] = (dot(left, own[...]) + dot(right, other[...])).astype(out.dtype)
        out[:, frames:] = (dot(left, own_edge[...]) + dot(right, other_edge[...])).astype(out.dtype)


def gelu(value):
    return 0.5 * value * (1.0 + lax.erf(value * (1.0 / math.sqrt(2.0))))


def conv_rows(taps, old, kernel, bias, keep, store, cols, step):
    for start in range(0, cols, step):
        width = min(step, cols - start)
        here = pl.ds(start, width)
        total = dot(kernel[0], taps[0, :, here])
        total = total + dot(kernel[1], taps[1, :, here])
        total = total + dot(kernel[2], taps[2, :, here])
        new = old(here).astype(jnp.float32) + gelu(total + bias)
        if keep is not None and start + width > cols - EDGE:
            new = jnp.where(keep(start, width), new, 0.0)
        store(here, new.astype(jnp.bfloat16))


def column(row, out):
    out[...] = jnp.broadcast_to(row, (EDGE, row.shape[1])).T


def keeper(place, blocks, span):
    frames = span - EDGE

    def keep(start, width):
        lane = lax.broadcasted_iota(jnp.int32, (1, width), 1) + start
        frame = jnp.where(lane < span - HALF, lane, lane - span) + place[0] * frames
        return (frame >= 0) & (frame < blocks * frames)

    return keep


def own_kernel(
    layer, blocks, last, dilations, side, place, mine, theirs, weights, biases, *refs
):
    outs, taps, col = refs[:-2], refs[-2], refs[-1]
    out = outs[0]
    rows, span = mine.shape
    shift = dilations[layer]
    lane = lax.broadcasted_iota(jnp.int32, (rows, EDGE), 1)
    count = span // EDGE
    for part, source in ((side[0], mine), (1 - side[0], theirs)):
        here = pl.ds(pl.multiple_of(part * rows, rows), rows)
        tiles = [source[:, n * EDGE : (n + 1) * EDGE] for n in range(count)]
        later = [pltpu.roll(tile, shift, 1) for tile in tiles]
        sooner = [pltpu.roll(tile, EDGE - shift, 1) for tile in tiles]
        for n in range(count):
            cols = slice(n * EDGE, (n + 1) * EDGE)
            taps[1, here, cols] = tiles[n]
            taps[0, here, cols] = jnp.where(lane < shift, later[n - 1], later[n])
            taps[2, here, cols] = jnp.where(
                lane < EDGE - shift, sooner[n], sooner[(n + 1) % count]
            )
    column(biases[layer : layer + 1, :], col)

    def store(here, value):
        for target in outs:
            target[:, here] = value

    conv_rows(
        taps, lambda here: mine[:, here], weights, col[:, 0:1],
        None if last else keeper(place, blocks, span), store, out.shape[1], 256 if last else 384,
    )


def other_rows(layer, core, theirs, taps, near_w, far_w, biases, col, keep, target, cols, step):
    half = near_w.shape[1]
    column(biases[layer : layer + 1, :], col)
    for weights, part in ((near_w, core[0]), (far_w, 1 - core[0])):
        rows = pl.ds(pl.multiple_of(part * half, half), half)

        def store(here, value, rows=rows):
            target(rows, here, value)

        conv_rows(
            taps, lambda here, rows=rows: theirs[rows, here], weights, col[rows, 0:1], keep,
            store, cols, step,
        )


def other_kernel(layer, blocks, core, place, theirs, taps, near_w, far_w, biases, out, col):
    span = theirs.shape[1]

    def target(rows, here, value):
        out[rows, here] = value

    other_rows(
        layer, core, theirs, taps, near_w, far_w, biases, col, keeper(place, blocks, span), target,
        span, 384,
    )


def last_kernel(
    layer, side, core, features, theirs, taps, near_w, far_w, biases, key_w, value_w,
    key_keep, key_send, value_keep, value_send, col, full,
):
    rows, frames = features.shape
    base = (1 - side[0]) * rows
    full[pl.ds(pl.multiple_of(side[0] * rows, rows), rows), :] = features[...]
    half = rows // 2

    def target(part, here, value):
        full[pl.ds(pl.multiple_of(base + part.start, half), half), here] = value

    other_rows(
        layer, core, theirs, taps, near_w, far_w, biases, col, None, target, frames, 256
    )
    for key_out, value_out, part in (
        (key_send, value_send, 1 - core[0]), (key_keep, value_keep, core[0])
    ):
        here = pl.ds(pl.multiple_of(part * half, half), half)
        key_out[...] = dot(key_w[here, :], full[...]).astype(jnp.bfloat16)
        value_out[...] = dot(value_w[here, :], full[...]).T.astype(jnp.bfloat16)


def thirds(value):
    first = value.astype(jnp.bfloat16)
    rest = value - first.astype(jnp.float32)
    second = rest.astype(jnp.bfloat16)
    third = (rest - second.astype(jnp.float32)).astype(jnp.bfloat16)
    return first, second, third


def pack(out, peak, total, weighted):
    out[0:HD, :] = weighted.astype(jnp.bfloat16)
    lines = [line.astype(jnp.float32) for line in thirds(peak) + thirds(total)]
    lines.append(jnp.zeros_like(lines[0]))
    lines.append(jnp.zeros_like(lines[0]))
    out[HD : HD + 8, :] = jnp.concatenate(lines, axis=0).astype(jnp.bfloat16)


def unpack(packed):
    lines = packed[HD : HD + 8, :].astype(jnp.float32)
    peak = lines[0:1] + (lines[1:2] + lines[2:3])
    total = lines[3:4] + (lines[4:5] + lines[5:6])
    return peak, total, packed[0:HD, :].astype(jnp.float32)


SCALE = LOG2E / math.sqrt(HD)


def join(one, two):
    peak = jnp.maximum(one[0], two[0])
    left = jnp.exp2((one[0] - peak) * SCALE)
    right = jnp.exp2((two[0] - peak) * SCALE)
    return peak, one[1] * left + two[1] * right, one[2] * left + two[2] * right


def ordered(info, mine, theirs):
    swap = info[0] == 1
    one = tuple(jnp.where(swap, t, m) for m, t in zip(mine, theirs))
    two = tuple(jnp.where(swap, m, t) for m, t in zip(mine, theirs))
    return one, two


def meet_kernel(peak, total, weighted, *refs):
    state = (peak[...], total[...], weighted[...])
    for theirs in refs[:-1]:
        state = join(state, unpack(theirs))
    pack(refs[-1], *state)


def merge_kernel(info, mine, theirs, out):
    pack(out, *join(*ordered(info, unpack(mine), unpack(theirs))))


def finish_kernel(info, mine, theirs, out):
    _, total, weighted = join(*ordered(info, unpack(mine), unpack(theirs)))
    out[...] = (weighted / total).astype(out.dtype)


def ask_kernel(core, queries, out):
    rows = 2 * HD
    wide = queries[pl.ds(pl.multiple_of(core[0] * rows, rows), rows), :].astype(jnp.float32)
    out[...] = wide.T.astype(out.dtype)


def attend_kernel(
    packed, which, half, valid_own, valid_rec, key_own, key_rec, value_own, value_rec, queries,
    *refs
):
    outs = refs[:-6]
    asked, keyed, values, score_a, score_b, probs_ref = refs[-6:]
    frames = key_own.shape[1]
    latents = asked.shape[0]
    rows = score_a.shape[0]
    chunk = frames // 2
    slot = which[0]
    spare = (1 - slot) * HD
    row = lax.broadcasted_iota(jnp.int32, (2 * HD, frames), 0)
    frame = lax.broadcasted_iota(jnp.int32, (2 * HD, frames), 1)
    for part, (source, valid) in enumerate(((key_own, valid_own), (key_rec, valid_rec))):
        bias = jnp.where(frame < valid[0], 0.0, MASKED).astype(jnp.bfloat16)
        keyed[:, part * frames : (part + 1) * frames] = jnp.where(row == spare, bias, source[...])
    values[0:frames, :] = value_own[...]
    values[frames:, :] = value_rec[...]
    lane = lax.broadcasted_iota(jnp.int32, (latents, 2 * HD), 1)
    fill = jnp.where(lane == spare, 1.0, 0.0).astype(jnp.bfloat16)
    mine = queries[pl.ds(pl.multiple_of(half[0] * latents, latents), latents), :]
    asked[...] = jnp.where(lane // HD == slot, mine, fill)
    lane = lax.broadcasted_iota(jnp.int32, (rows, 2 * HD), 1)
    count = latents // rows
    peak = None
    for step in range(count + 1):
        now, before = ((score_a, score_b), (score_b, score_a))[step % 2]
        top = None
        total = None
        for start in range(0, 2 * frames, chunk):
            here = slice(start, start + chunk)
            if step < count:
                value = dot(asked[step * rows : (step + 1) * rows, :], keyed[:, here])
                now[:, here] = value
                for n in range(0, chunk, EDGE):
                    part = value[:, n : n + EDGE]
                    top = part if top is None else jnp.maximum(top, part)
            if step > 0:
                probs = jnp.exp2((before[:, here] - peak) * SCALE)
                for n in range(0, chunk, EDGE):
                    part = probs[:, n : n + EDGE]
                    total = part if total is None else total + part
                probs_ref[:, here] = probs.astype(jnp.bfloat16)
        if step > 0:
            weighted = dot(probs_ref[...], values[...])
            total = jnp.sum(total, axis=1, keepdims=True)
            both = jnp.where(
                lane == spare, peak, jnp.where(lane == spare + 1, total, weighted)
            ).T
            kept = jnp.where(slot == 0, both[0:HD, :], both[HD:, :])
            rest = jnp.where(slot == 0, both[HD : HD + 8, :], both[0:8, :])
            done = slice((step - 1) * rows, step * rows)
            if packed:
                pack(outs[0].at[:, done], rest[0:1], rest[1:2], kept)
            else:
                outs[0][:, done] = rest[0:1]
                outs[1][:, done] = rest[1:2]
                outs[2][:, done] = kept
        if step < count:
            peak = jnp.max(top, axis=1, keepdims=True)


def attend(packed, scalars, keys, values, queries):
    latents = queries.shape[0] // 2
    frames = keys[0].shape[1]
    rows = min(EDGE, latents)
    if packed:
        out_shape = jax.ShapeDtypeStruct((HD + 8, latents), jnp.bfloat16)
        out_specs = pl.BlockSpec(memory_space=pltpu.VMEM)
    else:
        out_shape = [
            jax.ShapeDtypeStruct((1, latents), jnp.float32),
            jax.ShapeDtypeStruct((1, latents), jnp.float32),
            jax.ShapeDtypeStruct((HD, latents), jnp.float32),
        ]
        out_specs = whole(3)
    return pl.pallas_call(
        functools.partial(attend_kernel, packed),
        out_shape=out_shape,
        in_specs=smem(4) + whole(5),
        out_specs=out_specs,
        scratch_shapes=[
            VMEM((latents, 2 * HD), jnp.bfloat16),
            VMEM((2 * HD, 2 * frames), jnp.bfloat16),
            VMEM((2 * frames, 2 * HD), jnp.bfloat16),
            VMEM((rows, 2 * frames), jnp.float32),
            VMEM((rows, 2 * frames), jnp.float32),
            VMEM((rows, 2 * frames), jnp.bfloat16),
        ],
        compiler_params=params(20),
        name="attend_send" if packed else "attend_keep",
    )(*scalars, *keys, *values, queries)


def assemble_kernel(core, cross, lower, *refs):
    out = refs[-1]
    latents = refs[0].shape[1]
    mine, theirs = 2 * core[0], 2 - 2 * core[0]
    heads = (mine + cross[0], mine + 1 - cross[0], theirs + cross[0], theirs + 1 - cross[0])
    for index, piece in enumerate(refs[:-1]):
        part = lower[0] if index % 2 == 0 else 1 - lower[0]
        out[
            pl.ds(pl.multiple_of(heads[index // 2] * HD, HD), HD),
            pl.ds(pl.multiple_of(part * latents, latents), latents),
        ] = piece[...]


def simple(kernel, out_shape, scalars, arrays, scratch=(), mib=16, specs=None):
    many = isinstance(out_shape, (list, tuple))
    return pl.pallas_call(
        kernel,
        grid=(1,),
        out_shape=out_shape,
        in_specs=smem(len(scalars)) + (specs or whole(len(arrays))),
        out_specs=whole(len(out_shape)) if many else pl.BlockSpec(memory_space=pltpu.VMEM),
        scratch_shapes=list(scratch),
        compiler_params=params(mib),
    )(*scalars, *arrays)


def pair_device(
    recording, spatial_w, conv_w, conv_b, dilations, valid_frames, key_w, value_w, queries
):
    frames = recording.shape[1]
    ch_loc = conv_w.shape[2]
    ch = conv_w.shape[3]
    half = ch_loc // 2
    latents = queries.shape[1]
    blocks = lax.axis_size("tm")
    side = lax.axis_index("sensor").astype(jnp.int32).reshape(1)
    place = lax.axis_index("tm").astype(jnp.int32).reshape(1)
    core = place & 1
    cross = (place >> 1) & 1
    span = frames + EDGE
    bf16 = jnp.bfloat16
    across = [(0, 1), (1, 0)]
    twins = [(i, i ^ 1) for i in range(blocks)]

    other_rec = lax.ppermute(recording, "sensor", across)
    even = core[0] == 0
    slab = ch // 2
    near_sp = lax.ppermute(jnp.where(even, spatial_w[:slab], spatial_w[slab:]), "sensor", across)
    far_sp = lax.ppermute(near_sp, "tm", twins)
    last_part, first_part = recording[:, frames - EDGE :], recording[:, :EDGE]
    links = [(i, i + 1) for i in range(1, blocks - 1, 2)]
    outer = lax.ppermute(
        jnp.where(even, first_part, last_part), "tm",
        links + [(j, i) for i, j in links],
    )
    inner = lax.ppermute(jnp.where(even, last_part, first_part), "tm", twins)
    lane = jnp.arange(EDGE, dtype=jnp.int32)[None, :]
    edge = jnp.where((lane < HALF) == even, inner, outer)
    other_edge = lax.ppermute(edge, "sensor", across)
    other_b = lax.ppermute(conv_b, "sensor", across)
    later_w = lax.optimization_barrier((conv_w, edge))[0]
    mine = [
        lax.dynamic_slice(
            later_w if layer else conv_w, (layer, 0, core[0] * half, 0), (1, 3, half, ch)
        )[0]
        for layer in range(LAYERS)
    ]
    near = [lax.ppermute(mine[n], "sensor", across) for n in range(LAYERS)]
    far = [lax.ppermute(near[n], "tm", twins) for n in range(LAYERS)]
    asked = simple(ask_kernel, jax.ShapeDtypeStruct((latents, half), bf16), (core,), (queries,))
    half_shape = jax.ShapeDtypeStruct((ch_loc, span), bf16)
    fixed = [pltpu.with_memory_space_constraint(v, pltpu.HBM) for v in (spatial_w, recording)]
    own_h, other_h = simple(
        first_kernel, [half_shape, half_shape], (side, core),
        (near_sp, far_sp, *fixed, edge, other_rec, other_edge),
        [VMEM(part.shape, bf16) for part in (spatial_w, recording, edge) * 2]
        + [pltpu.SemaphoreType.DMA((7,))],
        specs=[pl.BlockSpec(memory_space=pltpu.HBM)] * 7,
    )
    taps_shape = jax.ShapeDtypeStruct((3, ch, span), bf16)
    col = [VMEM((ch_loc, EDGE), jnp.float32)]
    for layer in range(LAYERS):
        last = layer == LAYERS - 1
        specs = whole(4)
        specs[2] = pl.BlockSpec((None, 3, ch_loc, ch), lambda _, layer=layer: (layer, 0, 0, 0))
        made = [jax.ShapeDtypeStruct((ch_loc, frames), bf16)] * 2 if last else [half_shape]
        *own_next, taps = simple(
            functools.partial(own_kernel, layer, blocks, last), made + [taps_shape],
            (dilations, side, place), (own_h, other_h, conv_w, conv_b), col,
            mib=24, specs=specs,
        )
        arrays = (other_h, taps, near[layer], far[layer], other_b)
        if last:
            features, kept_features = own_next
            shapes = [
                jax.ShapeDtypeStruct((half, frames), bf16),
                jax.ShapeDtypeStruct((half, frames), bf16),
                jax.ShapeDtypeStruct((frames, half), bf16),
                jax.ShapeDtypeStruct((frames, half), bf16),
            ]
            key_keep, key_send, value_keep, value_send = simple(
                functools.partial(last_kernel, layer), shapes, (side, core),
                (kept_features,) + arrays + (key_w, value_w), col + [VMEM((ch, frames), bf16)],
                mib=24,
            )
        else:
            other_h = simple(
                functools.partial(other_kernel, layer, blocks), half_shape, (core, place), arrays,
                col, mib=24,
            )
            own_h = own_next[0]
    keys = (key_keep, lax.ppermute(key_send, "tm", twins))
    values = (value_keep, lax.ppermute(value_send, "tm", twins))
    other_valid = lax.ppermute(valid_frames, "tm", twins)

    def flip(value, bit):
        return lax.ppermute(value, "tm", [(i, i ^ bit) for i in range(blocks)])

    lower = (place >> 2) & 1

    def run(packed, slot, part):
        scalars = (slot, part, valid_frames, other_valid)
        return attend(packed, scalars, keys, values, asked)

    sent = flip(run(True, 1 - cross, 1 - lower), 2)
    kept = flip(run(True, 1 - cross, lower), 2)
    packed_shape = jax.ShapeDtypeStruct((HD + 8, latents // 2), bf16)
    final_shape = jax.ShapeDtypeStruct((HD, latents // 2), bf16)
    given = run(False, cross, 1 - lower)
    given = simple(meet_kernel, packed_shape, (), (*given, sent))
    given = flip(given, 4)
    held = run(False, cross, lower)
    packed = simple(meet_kernel, packed_shape, (), (*held, kept, given))
    bit = 8
    while bit < blocks:
        theirs = flip(packed, bit)
        which = ((place & bit) != 0).astype(jnp.int32)
        if bit * 2 < blocks:
            packed = simple(merge_kernel, packed_shape, (which,), (packed, theirs))
        else:
            done = simple(finish_kernel, final_shape, (which,), (packed, theirs))
        bit *= 2
    above = flip(done, 4)
    beside = flip(done, 2)
    corner = flip(done, 6)
    pieces = [done, above, beside, corner]
    pieces += [flip(piece, 1) for piece in pieces]
    attended = simple(
        assemble_kernel, jax.ShapeDtypeStruct((ch_loc, latents), bf16), (core, cross, lower),
        pieces,
    )
    return (features, attended)


def fits(mesh):
    sensors, blocks = mesh.shape["sensor"], mesh.shape["tm"]
    return sensors == 2 and blocks >= 16 and blocks & (blocks - 1) == 0


def on_device(*arrays):
    if arrays[6].shape[0] // HD != 4:
        return generic_device(*arrays)
    return pair_device(*arrays)


def solution(mesh):
    quick = fits(mesh)
    return jax.shard_map(
        on_device if quick else generic_device,
        mesh=mesh,
        in_specs=(
            P("sensor", "tm"),
            P(None, "sensor"),
            P(None, None, "sensor", None),
            P(None, "sensor"),
            P(),
            P("tm"),
            P("sensor", None),
            P("sensor", None),
            P("sensor", None),
        ),
        out_specs=(P("sensor", "tm"), P("sensor", None)),
        check_vma=False,
    )
```

```python
import functools
import math

import jax
import jax.numpy as jnp
from jax import lax
from jax.experimental import pallas as pl
from jax.experimental.pallas import tpu as pltpu
from jax.sharding import PartitionSpec as P


HD = 64
LATENTS = 2048
LAYERS = 3
DMAX = 16


def padded(cells, sides, width):
    for axis, dim in sides:
        count = lax.axis_size(axis)
        ends = count - 1
        head = lax.slice_in_dim(cells, 0, width, axis=dim)
        tail = lax.slice_in_dim(cells, cells.shape[dim] - width, cells.shape[dim], axis=dim)
        cells = jnp.concatenate(
            [
                lax.ppermute(tail, axis, [(i, (i + 1) % count) for i in range(ends)]),
                cells,
                lax.ppermute(head, axis, [((i + 1) % count, i) for i in range(ends)]),
            ],
            axis=dim,
        )
    return cells


def tap_folder(kernels, dilation, frames, margin):

    def add_taps(running, portion, first_row):
        portion = jnp.pad(portion, ((0, 0), (margin, margin)))
        for tap_index in range(3):
            kernel = kernels[tap_index]
            offset = DMAX + (tap_index - 1) * dilation
            shifted = lax.dynamic_slice_in_dim(portion, offset, frames, 1)
            running = running + jnp.dot(kernel, shifted, preferred_element_type=jnp.float32)
        return running

    return add_taps


def generic_device(
    recording, spatial_w, conv_w, conv_b, dilations, valid_frames, key_w, value_w, queries
):
    frames = recording.shape[1]
    ch_loc = conv_w.shape[2]
    hidden = lax.psum_scatter(
        jnp.dot(spatial_w, recording, preferred_element_type=jnp.float32),
        "sensor",
        scatter_dimension=0,
        tiled=True,
    ).astype(jnp.bfloat16)
    reach = 3 * DMAX
    extended = padded(hidden, (("tm", 1),), reach)
    span = frames + 2 * reach
    position = lax.axis_index("tm") * frames - reach + jnp.arange(span, dtype=jnp.int32)
    inside = (position >= 0) & (position < frames * lax.axis_size("tm"))
    for layer in range(LAYERS):
        initial = jnp.broadcast_to(conv_b[layer][:, None], (ch_loc, span))
        folder = tap_folder(conv_w[layer], dilations[layer], span, DMAX)
        preact = folder(
            initial, lax.all_gather(extended, "sensor", axis=0, tiled=True), jnp.int32(0)
        )
        updated = extended.astype(jnp.float32) + jax.nn.gelu(preact, approximate=False)
        extended = jnp.where(inside[None, :], updated, 0.0).astype(jnp.bfloat16)
    hidden = extended[:, reach : reach + frames]
    portion = lax.all_gather(hidden, "sensor", axis=0, tiled=True)
    key_rows = jnp.dot(key_w, portion, preferred_element_type=jnp.float32)
    value_rows = jnp.dot(value_w, portion, preferred_element_type=jnp.float32)
    head_count = key_w.shape[0] // HD
    key_heads = key_rows.astype(jnp.bfloat16).reshape(head_count, HD, frames)
    value_heads = value_rows.astype(jnp.bfloat16).reshape(head_count, HD, frames)
    frame_mask = jnp.arange(frames, dtype=jnp.int32) < valid_frames[0]
    block_rows = min(LATENTS, 512)
    block_count = LATENTS // block_rows
    query_blocks = queries.reshape(head_count, HD, block_count, block_rows).transpose(2, 0, 1, 3)
    scale = 1.0 / math.sqrt(HD)

    def attend(query_block):
        scores = (
            jnp.einsum("hdq,hdt->hqt", query_block, key_heads, preferred_element_type=jnp.float32)
            * scale
        )
        scores = jnp.where(frame_mask[None, None, :], scores, -jnp.inf)
        peaks = jnp.max(scores, axis=2)
        probs = jnp.where(frame_mask[None, None, :], jnp.exp(scores - peaks[:, :, None]), 0.0)
        totals = jnp.sum(probs, axis=2)
        weighted = jnp.einsum(
            "hqt,hdt->hdq",
            probs.astype(jnp.bfloat16),
            value_heads,
            preferred_element_type=jnp.float32,
        )
        return (peaks, totals, weighted)

    peaks, totals, weighted = lax.map(attend, query_blocks)
    peaks = peaks.transpose(1, 0, 2).reshape(head_count, LATENTS)
    totals = totals.transpose(1, 0, 2).reshape(head_count, LATENTS)
    weighted = weighted.transpose(1, 2, 0, 3).reshape(head_count, HD, LATENTS)
    global_peaks = lax.pmax(peaks, "tm")
    rescale = jnp.exp(peaks - global_peaks)
    totals, weighted = lax.psum((totals * rescale, weighted * rescale[:, None, :]), "tm")
    attended = (
        (weighted / totals[:, None, :]).reshape(head_count * HD, LATENTS).astype(jnp.bfloat16)
    )
    return (hidden, attended)


VMEM = pltpu.VMEM
EDGE = 128
HALF = EDGE // 2
LOG2E = 1.4426950408889634
MASKED = -1e30


def whole(count):
    return [pl.BlockSpec(memory_space=pltpu.VMEM)] * count


def smem(count):
    return [pl.BlockSpec(memory_space=pltpu.SMEM)] * count


def params(mib):
    return pltpu.CompilerParams(vmem_limit_bytes=mib * 1024 * 1024)


def dot(left, right):
    return jnp.dot(left, right, preferred_element_type=jnp.float32)


def first_kernel(side, *refs):
    sources, (mine, theirs), held, done = refs[:6], refs[6:8], refs[8:14], refs[14]
    copies = [
        pltpu.make_async_copy(source, target, done.at[n])
        for n, (source, target) in enumerate(zip(sources, held))
    ]
    for copy in copies:
        copy.start()
    for copy in copies:
        copy.wait()
    own_w, other_w, own, other, own_edge, other_edge = held
    frames = own.shape[1]
    rows = mine.shape[0]
    for out, part in ((mine, side[0]), (theirs, 1 - side[0])):
        here = pl.ds(pl.multiple_of(part * rows, rows), rows)
        left, right = own_w[here, :], other_w[here, :]
        out[:, :frames] = (dot(left, own[...]) + dot(right, other[...])).astype(out.dtype)
        out[:, frames:] = (dot(left, own_edge[...]) + dot(right, other_edge[...])).astype(out.dtype)


def gelu(value):
    return 0.5 * value * (1.0 + lax.erf(value * (1.0 / math.sqrt(2.0))))


def conv_rows(taps, old, kernel, bias, keep, store, cols, step):
    for start in range(0, cols, step):
        width = min(step, cols - start)
        here = pl.ds(start, width)
        total = dot(kernel[0], taps[0, :, here])
        total = total + dot(kernel[1], taps[1, :, here])
        total = total + dot(kernel[2], taps[2, :, here])
        new = old(here).astype(jnp.float32) + gelu(total + bias)
        if keep is not None and start + width > cols - EDGE:
            new = jnp.where(keep(start, width), new, 0.0)
        store(here, new.astype(jnp.bfloat16))


def column(row, out):
    out[...] = jnp.broadcast_to(row, (EDGE, row.shape[1])).T


def keeper(place, blocks, span):
    frames = span - EDGE

    def keep(start, width):
        lane = lax.broadcasted_iota(jnp.int32, (1, width), 1) + start
        frame = jnp.where(lane < span - HALF, lane, lane - span) + place[0] * frames
        return (frame >= 0) & (frame < blocks * frames)

    return keep


def own_kernel(
    layer, blocks, last, dilations, side, place, mine, theirs, weights, biases, *refs
):
    outs, taps, col = refs[:-2], refs[-2], refs[-1]
    out = outs[0]
    rows, span = mine.shape
    shift = dilations[layer]
    lane = lax.broadcasted_iota(jnp.int32, (rows, EDGE), 1)
    count = span // EDGE
    for part, source in ((side[0], mine), (1 - side[0], theirs)):
        here = pl.ds(pl.multiple_of(part * rows, rows), rows)
        tiles = [source[:, n * EDGE : (n + 1) * EDGE] for n in range(count)]
        later = [pltpu.roll(tile, shift, 1) for tile in tiles]
        sooner = [pltpu.roll(tile, EDGE - shift, 1) for tile in tiles]
        for n in range(count):
            cols = slice(n * EDGE, (n + 1) * EDGE)
            taps[1, here, cols] = tiles[n]
            taps[0, here, cols] = jnp.where(lane < shift, later[n - 1], later[n])
            taps[2, here, cols] = jnp.where(
                lane < EDGE - shift, sooner[n], sooner[(n + 1) % count]
            )
    column(biases[layer : layer + 1, :], col)

    def store(here, value):
        for target in outs:
            target[:, here] = value

    conv_rows(
        taps, lambda here: mine[:, here], weights, col[:, 0:1],
        None if last else keeper(place, blocks, span), store, out.shape[1], 256 if last else 384,
    )


def other_rows(layer, core, theirs, taps, near_w, far_w, biases, col, keep, target, cols, step):
    half = near_w.shape[1]
    column(biases[layer : layer + 1, :], col)
    for weights, part in ((near_w, core[0]), (far_w, 1 - core[0])):
        rows = pl.ds(pl.multiple_of(part * half, half), half)

        def store(here, value, rows=rows):
            target(rows, here, value)

        conv_rows(
            taps, lambda here, rows=rows: theirs[rows, here], weights, col[rows, 0:1], keep,
            store, cols, step,
        )


def other_kernel(layer, blocks, core, place, theirs, taps, near_w, far_w, biases, out, col):
    span = theirs.shape[1]

    def target(rows, here, value):
        out[rows, here] = value

    other_rows(
        layer, core, theirs, taps, near_w, far_w, biases, col, keeper(place, blocks, span), target,
        span, 384,
    )


def last_kernel(
    layer, side, core, features, theirs, taps, near_w, far_w, biases, key_w, value_w,
    key_keep, key_send, value_keep, value_send, col, full,
):
    rows, frames = features.shape
    base = (1 - side[0]) * rows
    full[pl.ds(pl.multiple_of(side[0] * rows, rows), rows), :] = features[...]
    half = rows // 2

    def target(part, here, value):
        full[pl.ds(pl.multiple_of(base + part.start, half), half), here] = value

    other_rows(
        layer, core, theirs, taps, near_w, far_w, biases, col, None, target, frames, 256
    )
    for key_out, value_out, part in (
        (key_send, value_send, 1 - core[0]), (key_keep, value_keep, core[0])
    ):
        here = pl.ds(pl.multiple_of(part * half, half), half)
        key_out[...] = dot(key_w[here, :], full[...]).astype(jnp.bfloat16)
        value_out[...] = dot(value_w[here, :], full[...]).T.astype(jnp.bfloat16)


def thirds(value):
    first = value.astype(jnp.bfloat16)
    rest = value - first.astype(jnp.float32)
    second = rest.astype(jnp.bfloat16)
    third = (rest - second.astype(jnp.float32)).astype(jnp.bfloat16)
    return first, second, third


def pack(out, peak, total, weighted):
    out[0:HD, :] = weighted.astype(jnp.bfloat16)
    lines = [line.astype(jnp.float32) for line in thirds(peak) + thirds(total)]
    lines.append(jnp.zeros_like(lines[0]))
    lines.append(jnp.zeros_like(lines[0]))
    out[HD : HD + 8, :] = jnp.concatenate(lines, axis=0).astype(jnp.bfloat16)


def unpack(packed):
    lines = packed[HD : HD + 8, :].astype(jnp.float32)
    peak = lines[0:1] + (lines[1:2] + lines[2:3])
    total = lines[3:4] + (lines[4:5] + lines[5:6])
    return peak, total, packed[0:HD, :].astype(jnp.float32)


SCALE = LOG2E / math.sqrt(HD)


def join(one, two):
    peak = jnp.maximum(one[0], two[0])
    left = jnp.exp2((one[0] - peak) * SCALE)
    right = jnp.exp2((two[0] - peak) * SCALE)
    return peak, one[1] * left + two[1] * right, one[2] * left + two[2] * right


def ordered(info, mine, theirs):
    swap = info[0] == 1
    one = tuple(jnp.where(swap, t, m) for m, t in zip(mine, theirs))
    two = tuple(jnp.where(swap, m, t) for m, t in zip(mine, theirs))
    return one, two


def meet_kernel(peak, total, weighted, *refs):
    state = (peak[...], total[...], weighted[...])
    for theirs in refs[:-1]:
        state = join(state, unpack(theirs))
    pack(refs[-1], *state)


def merge_kernel(info, mine, theirs, out):
    pack(out, *join(*ordered(info, unpack(mine), unpack(theirs))))


def finish_kernel(info, mine, theirs, out):
    _, total, weighted = join(*ordered(info, unpack(mine), unpack(theirs)))
    out[...] = (weighted / total).astype(out.dtype)


def ask_kernel(core, queries, out):
    rows = 2 * HD
    wide = queries[pl.ds(pl.multiple_of(core[0] * rows, rows), rows), :].astype(jnp.float32)
    out[...] = wide.T.astype(out.dtype)


def attend_kernel(
    packed, which, half, valid_own, valid_rec, key_own, key_rec, value_own, value_rec, queries,
    *refs
):
    outs = refs[:-6]
    asked, keyed, values, score_a, score_b, probs_ref = refs[-6:]
    frames = key_own.shape[1]
    latents = asked.shape[0]
    rows = score_a.shape[0]
    chunk = frames // 2
    slot = which[0]
    spare = (1 - slot) * HD
    row = lax.broadcasted_iota(jnp.int32, (2 * HD, frames), 0)
    frame = lax.broadcasted_iota(jnp.int32, (2 * HD, frames), 1)
    for part, (source, valid) in enumerate(((key_own, valid_own), (key_rec, valid_rec))):
        bias = jnp.where(frame < valid[0], 0.0, MASKED).astype(jnp.bfloat16)
        keyed[:, part * frames : (part + 1) * frames] = jnp.where(row == spare, bias, source[...])
    values[0:frames, :] = value_own[...]
    values[frames:, :] = value_rec[...]
    lane = lax.broadcasted_iota(jnp.int32, (latents, 2 * HD), 1)
    fill = jnp.where(lane == spare, 1.0, 0.0).astype(jnp.bfloat16)
    mine = queries[pl.ds(pl.multiple_of(half[0] * latents, latents), latents), :]
    asked[...] = jnp.where(lane // HD == slot, mine, fill)
    lane = lax.broadcasted_iota(jnp.int32, (rows, 2 * HD), 1)
    count = latents // rows
    peak = None
    for step in range(count + 1):
        now, before = ((score_a, score_b), (score_b, score_a))[step % 2]
        top = None
        total = None
        for start in range(0, 2 * frames, chunk):
            here = slice(start, start + chunk)
            if step < count:
                value = dot(asked[step * rows : (step + 1) * rows, :], keyed[:, here])
                now[:, here] = value
                for n in range(0, chunk, EDGE):
                    part = value[:, n : n + EDGE]
                    top = part if top is None else jnp.maximum(top, part)
            if step > 0:
                probs = jnp.exp2((before[:, here] - peak) * SCALE)
                for n in range(0, chunk, EDGE):
                    part = probs[:, n : n + EDGE]
                    total = part if total is None else total + part
                probs_ref[:, here] = probs.astype(jnp.bfloat16)
        if step > 0:
            weighted = dot(probs_ref[...], values[...])
            total = jnp.sum(total, axis=1, keepdims=True)
            both = jnp.where(
                lane == spare, peak, jnp.where(lane == spare + 1, total, weighted)
            ).T
            kept = jnp.where(slot == 0, both[0:HD, :], both[HD:, :])
            rest = jnp.where(slot == 0, both[HD : HD + 8, :], both[0:8, :])
            done = slice((step - 1) * rows, step * rows)
            if packed:
                pack(outs[0].at[:, done], rest[0:1], rest[1:2], kept)
            else:
                outs[0][:, done] = rest[0:1]
                outs[1][:, done] = rest[1:2]
                outs[2][:, done] = kept
        if step < count:
            peak = jnp.max(top, axis=1, keepdims=True)


def attend(packed, scalars, keys, values, queries):
    latents = queries.shape[0] // 2
    frames = keys[0].shape[1]
    rows = min(EDGE, latents)
    if packed:
        out_shape = jax.ShapeDtypeStruct((HD + 8, latents), jnp.bfloat16)
        out_specs = pl.BlockSpec(memory_space=pltpu.VMEM)
    else:
        out_shape = [
            jax.ShapeDtypeStruct((1, latents), jnp.float32),
            jax.ShapeDtypeStruct((1, latents), jnp.float32),
            jax.ShapeDtypeStruct((HD, latents), jnp.float32),
        ]
        out_specs = whole(3)
    return pl.pallas_call(
        functools.partial(attend_kernel, packed),
        out_shape=out_shape,
        in_specs=smem(4) + whole(5),
        out_specs=out_specs,
        scratch_shapes=[
            VMEM((latents, 2 * HD), jnp.bfloat16),
            VMEM((2 * HD, 2 * frames), jnp.bfloat16),
            VMEM((2 * frames, 2 * HD), jnp.bfloat16),
            VMEM((rows, 2 * frames), jnp.float32),
            VMEM((rows, 2 * frames), jnp.float32),
            VMEM((rows, 2 * frames), jnp.bfloat16),
        ],
        compiler_params=params(20),
        name="attend_send" if packed else "attend_keep",
    )(*scalars, *keys, *values, queries)


def assemble_kernel(core, cross, lower, *refs):
    out = refs[-1]
    latents = refs[0].shape[1]
    mine, theirs = 2 * core[0], 2 - 2 * core[0]
    heads = (mine + cross[0], mine + 1 - cross[0], theirs + cross[0], theirs + 1 - cross[0])
    for index, piece in enumerate(refs[:-1]):
        part = lower[0] if index % 2 == 0 else 1 - lower[0]
        out[
            pl.ds(pl.multiple_of(heads[index // 2] * HD, HD), HD),
            pl.ds(pl.multiple_of(part * latents, latents), latents),
        ] = piece[...]


def simple(kernel, out_shape, scalars, arrays, scratch=(), mib=16, specs=None):
    many = isinstance(out_shape, (list, tuple))
    return pl.pallas_call(
        kernel,
        grid=(1,),
        out_shape=out_shape,
        in_specs=smem(len(scalars)) + (specs or whole(len(arrays))),
        out_specs=whole(len(out_shape)) if many else pl.BlockSpec(memory_space=pltpu.VMEM),
        scratch_shapes=list(scratch),
        compiler_params=params(mib),
    )(*scalars, *arrays)


def pair_device(
    recording, spatial_w, conv_w, conv_b, dilations, valid_frames, key_w, value_w, queries
):
    frames = recording.shape[1]
    ch_loc = conv_w.shape[2]
    ch = conv_w.shape[3]
    half = ch_loc // 2
    latents = queries.shape[1]
    blocks = lax.axis_size("tm")
    side = lax.axis_index("sensor").astype(jnp.int32).reshape(1)
    place = lax.axis_index("tm").astype(jnp.int32).reshape(1)
    core = place & 1
    cross = (place >> 1) & 1
    span = frames + EDGE
    bf16 = jnp.bfloat16
    across = [(0, 1), (1, 0)]
    twins = [(i, i ^ 1) for i in range(blocks)]

    other_rec = lax.ppermute(recording, "sensor", across)
    other_w = lax.ppermute(spatial_w, "sensor", across)
    even = core[0] == 0
    last_part, first_part = recording[:, frames - EDGE :], recording[:, :EDGE]
    links = [(i, i + 1) for i in range(1, blocks - 1, 2)]
    outer = lax.ppermute(
        jnp.where(even, first_part, last_part), "tm",
        links + [(j, i) for i, j in links],
    )
    inner = lax.ppermute(jnp.where(even, last_part, first_part), "tm", twins)
    lane = jnp.arange(EDGE, dtype=jnp.int32)[None, :]
    edge = jnp.where((lane < HALF) == even, inner, outer)
    other_edge = lax.ppermute(edge, "sensor", across)
    other_b = lax.ppermute(conv_b, "sensor", across)
    later_w = lax.optimization_barrier((conv_w, edge))[0]
    mine = [
        lax.dynamic_slice(
            later_w if layer else conv_w, (layer, 0, core[0] * half, 0), (1, 3, half, ch)
        )[0]
        for layer in range(LAYERS)
    ]
    near = [lax.ppermute(mine[n], "sensor", across) for n in range(LAYERS)]
    far = [lax.ppermute(near[n], "tm", twins) for n in range(LAYERS)]
    asked = simple(ask_kernel, jax.ShapeDtypeStruct((latents, half), bf16), (core,), (queries,))
    half_shape = jax.ShapeDtypeStruct((ch_loc, span), bf16)
    fixed = [pltpu.with_memory_space_constraint(v, pltpu.HBM) for v in (spatial_w, recording)]
    parts = (fixed[0], other_w, fixed[1], other_rec, edge, other_edge)
    own_h, other_h = simple(
        first_kernel, [half_shape, half_shape], (side,), parts,
        [VMEM(part.shape, bf16) for part in parts] + [pltpu.SemaphoreType.DMA((len(parts),))],
        specs=[pl.BlockSpec(memory_space=pltpu.HBM)] * len(parts),
    )
    taps_shape = jax.ShapeDtypeStruct((3, ch, span), bf16)
    col = [VMEM((ch_loc, EDGE), jnp.float32)]
    for layer in range(LAYERS):
        last = layer == LAYERS - 1
        specs = whole(4)
        specs[2] = pl.BlockSpec((None, 3, ch_loc, ch), lambda _, layer=layer: (layer, 0, 0, 0))
        made = [jax.ShapeDtypeStruct((ch_loc, frames), bf16)] * 2 if last else [half_shape]
        *own_next, taps = simple(
            functools.partial(own_kernel, layer, blocks, last), made + [taps_shape],
            (dilations, side, place), (own_h, other_h, conv_w, conv_b), col,
            mib=24, specs=specs,
        )
        arrays = (other_h, taps, near[layer], far[layer], other_b)
        if last:
            features, kept_features = own_next
            shapes = [
                jax.ShapeDtypeStruct((half, frames), bf16),
                jax.ShapeDtypeStruct((half, frames), bf16),
                jax.ShapeDtypeStruct((frames, half), bf16),
                jax.ShapeDtypeStruct((frames, half), bf16),
            ]
            key_keep, key_send, value_keep, value_send = simple(
                functools.partial(last_kernel, layer), shapes, (side, core),
                (kept_features,) + arrays + (key_w, value_w), col + [VMEM((ch, frames), bf16)],
                mib=24,
            )
        else:
            other_h = simple(
                functools.partial(other_kernel, layer, blocks), half_shape, (core, place), arrays,
                col, mib=24,
            )
            own_h = own_next[0]
    keys = (key_keep, lax.ppermute(key_send, "tm", twins))
    values = (value_keep, lax.ppermute(value_send, "tm", twins))
    other_valid = lax.ppermute(valid_frames, "tm", twins)

    def flip(value, bit):
        return lax.ppermute(value, "tm", [(i, i ^ bit) for i in range(blocks)])

    lower = (place >> 2) & 1

    def run(packed, slot, part):
        scalars = (slot, part, valid_frames, other_valid)
        return attend(packed, scalars, keys, values, asked)

    sent = flip(run(True, 1 - cross, 1 - lower), 2)
    kept = flip(run(True, 1 - cross, lower), 2)
    packed_shape = jax.ShapeDtypeStruct((HD + 8, latents // 2), bf16)
    final_shape = jax.ShapeDtypeStruct((HD, latents // 2), bf16)
    given = run(False, cross, 1 - lower)
    given = simple(meet_kernel, packed_shape, (), (*given, sent))
    given = flip(given, 4)
    held = run(False, cross, lower)
    packed = simple(meet_kernel, packed_shape, (), (*held, kept, given))
    bit = 8
    while bit < blocks:
        theirs = flip(packed, bit)
        which = ((place & bit) != 0).astype(jnp.int32)
        if bit * 2 < blocks:
            packed = simple(merge_kernel, packed_shape, (which,), (packed, theirs))
        else:
            done = simple(finish_kernel, final_shape, (which,), (packed, theirs))
        bit *= 2
    above = flip(done, 4)
    beside = flip(done, 2)
    corner = flip(done, 6)
    pieces = [done, above, beside, corner]
    pieces += [flip(piece, 1) for piece in pieces]
    attended = simple(
        assemble_kernel, jax.ShapeDtypeStruct((ch_loc, latents), bf16), (core, cross, lower),
        pieces,
    )
    return (features, attended)


def fits(mesh):
    sensors, blocks = mesh.shape["sensor"], mesh.shape["tm"]
    return sensors == 2 and blocks >= 16 and blocks & (blocks - 1) == 0


def on_device(*arrays):
    if arrays[6].shape[0] // HD != 4:
        return generic_device(*arrays)
    return pair_device(*arrays)


def solution(mesh):
    quick = fits(mesh)
    return jax.shard_map(
        on_device if quick else generic_device,
        mesh=mesh,
        in_specs=(
            P("sensor", "tm"),
            P(None, "sensor"),
            P(None, None, "sensor", None),
            P(None, "sensor"),
            P(),
            P("tm"),
            P("sensor", None),
            P("sensor", None),
            P("sensor", None),
        ),
        out_specs=(P("sensor", "tm"), P("sensor", None)),
        check_vma=False,
    )
```

```python
import functools
import math

import jax
import jax.numpy as jnp
from jax import lax
from jax.experimental import pallas as pl
from jax.experimental.pallas import tpu as pltpu
from jax.sharding import PartitionSpec as P


HD = 64
LATENTS = 2048
LAYERS = 3
DMAX = 16


def padded(cells, sides, width):
    for axis, dim in sides:
        count = lax.axis_size(axis)
        ends = count - 1
        head = lax.slice_in_dim(cells, 0, width, axis=dim)
        tail = lax.slice_in_dim(cells, cells.shape[dim] - width, cells.shape[dim], axis=dim)
        cells = jnp.concatenate(
            [
                lax.ppermute(tail, axis, [(i, (i + 1) % count) for i in range(ends)]),
                cells,
                lax.ppermute(head, axis, [((i + 1) % count, i) for i in range(ends)]),
            ],
            axis=dim,
        )
    return cells


def tap_folder(kernels, dilation, frames, margin):

    def add_taps(running, portion, first_row):
        portion = jnp.pad(portion, ((0, 0), (margin, margin)))
        for tap_index in range(3):
            kernel = kernels[tap_index]
            offset = DMAX + (tap_index - 1) * dilation
            shifted = lax.dynamic_slice_in_dim(portion, offset, frames, 1)
            running = running + jnp.dot(kernel, shifted, preferred_element_type=jnp.float32)
        return running

    return add_taps


def generic_device(
    recording, spatial_w, conv_w, conv_b, dilations, valid_frames, key_w, value_w, queries
):
    frames = recording.shape[1]
    ch_loc = conv_w.shape[2]
    hidden = lax.psum_scatter(
        jnp.dot(spatial_w, recording, preferred_element_type=jnp.float32),
        "sensor",
        scatter_dimension=0,
        tiled=True,
    ).astype(jnp.bfloat16)
    reach = 3 * DMAX
    extended = padded(hidden, (("tm", 1),), reach)
    span = frames + 2 * reach
    position = lax.axis_index("tm") * frames - reach + jnp.arange(span, dtype=jnp.int32)
    inside = (position >= 0) & (position < frames * lax.axis_size("tm"))
    for layer in range(LAYERS):
        initial = jnp.broadcast_to(conv_b[layer][:, None], (ch_loc, span))
        folder = tap_folder(conv_w[layer], dilations[layer], span, DMAX)
        preact = folder(
            initial, lax.all_gather(extended, "sensor", axis=0, tiled=True), jnp.int32(0)
        )
        updated = extended.astype(jnp.float32) + jax.nn.gelu(preact, approximate=False)
        extended = jnp.where(inside[None, :], updated, 0.0).astype(jnp.bfloat16)
    hidden = extended[:, reach : reach + frames]
    portion = lax.all_gather(hidden, "sensor", axis=0, tiled=True)
    key_rows = jnp.dot(key_w, portion, preferred_element_type=jnp.float32)
    value_rows = jnp.dot(value_w, portion, preferred_element_type=jnp.float32)
    head_count = key_w.shape[0] // HD
    key_heads = key_rows.astype(jnp.bfloat16).reshape(head_count, HD, frames)
    value_heads = value_rows.astype(jnp.bfloat16).reshape(head_count, HD, frames)
    frame_mask = jnp.arange(frames, dtype=jnp.int32) < valid_frames[0]
    block_rows = min(LATENTS, 512)
    block_count = LATENTS // block_rows
    query_blocks = queries.reshape(head_count, HD, block_count, block_rows).transpose(2, 0, 1, 3)
    scale = 1.0 / math.sqrt(HD)

    def attend(query_block):
        scores = (
            jnp.einsum("hdq,hdt->hqt", query_block, key_heads, preferred_element_type=jnp.float32)
            * scale
        )
        scores = jnp.where(frame_mask[None, None, :], scores, -jnp.inf)
        peaks = jnp.max(scores, axis=2)
        probs = jnp.where(frame_mask[None, None, :], jnp.exp(scores - peaks[:, :, None]), 0.0)
        totals = jnp.sum(probs, axis=2)
        weighted = jnp.einsum(
            "hqt,hdt->hdq",
            probs.astype(jnp.bfloat16),
            value_heads,
            preferred_element_type=jnp.float32,
        )
        return (peaks, totals, weighted)

    peaks, totals, weighted = lax.map(attend, query_blocks)
    peaks = peaks.transpose(1, 0, 2).reshape(head_count, LATENTS)
    totals = totals.transpose(1, 0, 2).reshape(head_count, LATENTS)
    weighted = weighted.transpose(1, 2, 0, 3).reshape(head_count, HD, LATENTS)
    global_peaks = lax.pmax(peaks, "tm")
    rescale = jnp.exp(peaks - global_peaks)
    totals, weighted = lax.psum((totals * rescale, weighted * rescale[:, None, :]), "tm")
    attended = (
        (weighted / totals[:, None, :]).reshape(head_count * HD, LATENTS).astype(jnp.bfloat16)
    )
    return (hidden, attended)


VMEM = pltpu.VMEM
EDGE = 128
HALF = EDGE // 2
LOG2E = 1.4426950408889634
MASKED = -1e30


def whole(count):
    return [pl.BlockSpec(memory_space=pltpu.VMEM)] * count


def smem(count):
    return [pl.BlockSpec(memory_space=pltpu.SMEM)] * count


def params(mib):
    return pltpu.CompilerParams(vmem_limit_bytes=mib * 1024 * 1024)


def dot(left, right):
    return jnp.dot(left, right, preferred_element_type=jnp.float32)


def first_kernel(side, *refs):
    sources, (mine, theirs), held, done = refs[:6], refs[6:8], refs[8:14], refs[14]
    copies = [
        pltpu.make_async_copy(source, target, done.at[n])
        for n, (source, target) in enumerate(zip(sources, held))
    ]
    for copy in copies:
        copy.start()
    for copy in copies:
        copy.wait()
    own_w, other_w, own, other, own_edge, other_edge = held
    frames = own.shape[1]
    rows = mine.shape[0]
    for out, part in ((mine, side[0]), (theirs, 1 - side[0])):
        here = pl.ds(pl.multiple_of(part * rows, rows), rows)
        left, right = own_w[here, :], other_w[here, :]
        out[:, :frames] = (dot(left, own[...]) + dot(right, other[...])).astype(out.dtype)
        out[:, frames:] = (dot(left, own_edge[...]) + dot(right, other_edge[...])).astype(out.dtype)


def gelu(value):
    return 0.5 * value * (1.0 + lax.erf(value * (1.0 / math.sqrt(2.0))))


def conv_rows(taps, old, kernel, bias, keep, store, cols, step):
    for start in range(0, cols, step):
        width = min(step, cols - start)
        here = pl.ds(start, width)
        total = dot(kernel[0], taps[0, :, here])
        total = total + dot(kernel[1], taps[1, :, here])
        total = total + dot(kernel[2], taps[2, :, here])
        new = old(here).astype(jnp.float32) + gelu(total + bias)
        if keep is not None and start + width > cols - EDGE:
            new = jnp.where(keep(start, width), new, 0.0)
        store(here, new.astype(jnp.bfloat16))


def column(row, out):
    out[...] = jnp.broadcast_to(row, (EDGE, row.shape[1])).T


def keeper(place, blocks, span):
    frames = span - EDGE

    def keep(start, width):
        lane = lax.broadcasted_iota(jnp.int32, (1, width), 1) + start
        frame = jnp.where(lane < span - HALF, lane, lane - span) + place[0] * frames
        return (frame >= 0) & (frame < blocks * frames)

    return keep


def own_kernel(
    layer, blocks, last, dilations, side, place, mine, theirs, weights, biases, *refs
):
    outs, taps, col = refs[:-2], refs[-2], refs[-1]
    out = outs[0]
    rows, span = mine.shape
    shift = dilations[layer]
    lane = lax.broadcasted_iota(jnp.int32, (rows, EDGE), 1)
    count = span // EDGE
    for part, source in ((side[0], mine), (1 - side[0], theirs)):
        here = pl.ds(pl.multiple_of(part * rows, rows), rows)
        tiles = [source[:, n * EDGE : (n + 1) * EDGE] for n in range(count)]
        later = [pltpu.roll(tile, shift, 1) for tile in tiles]
        sooner = [pltpu.roll(tile, EDGE - shift, 1) for tile in tiles]
        for n in range(count):
            cols = slice(n * EDGE, (n + 1) * EDGE)
            taps[1, here, cols] = tiles[n]
            taps[0, here, cols] = jnp.where(lane < shift, later[n - 1], later[n])
            taps[2, here, cols] = jnp.where(
                lane < EDGE - shift, sooner[n], sooner[(n + 1) % count]
            )
    column(biases[layer : layer + 1, :], col)

    def store(here, value):
        for target in outs:
            target[:, here] = value

    conv_rows(
        taps, lambda here: mine[:, here], weights, col[:, 0:1],
        None if last else keeper(place, blocks, span), store, out.shape[1], 256 if last else 384,
    )


def other_rows(layer, core, theirs, taps, near_w, far_w, biases, col, keep, target, cols, step):
    half = near_w.shape[1]
    column(biases[layer : layer + 1, :], col)
    for weights, part in ((near_w, core[0]), (far_w, 1 - core[0])):
        rows = pl.ds(pl.multiple_of(part * half, half), half)

        def store(here, value, rows=rows):
            target(rows, here, value)

        conv_rows(
            taps, lambda here, rows=rows: theirs[rows, here], weights, col[rows, 0:1], keep,
            store, cols, step,
        )


def other_kernel(layer, blocks, core, place, theirs, taps, near_w, far_w, biases, out, col):
    span = theirs.shape[1]

    def target(rows, here, value):
        out[rows, here] = value

    other_rows(
        layer, core, theirs, taps, near_w, far_w, biases, col, keeper(place, blocks, span), target,
        span, 384,
    )


def near_kernel(layer, core, theirs, taps, weights, biases, out, col):
    rows, frames = out.shape
    column(biases[layer : layer + 1, :], col)
    here = pl.ds(pl.multiple_of(core[0] * rows, rows), rows)

    def store(cols, value):
        out[:, cols] = value

    conv_rows(
        taps, lambda cols: theirs[here, cols], weights, col[here, 0:1], None, store, frames, 256
    )


def last_kernel(
    layer, side, core, features, near_rows, theirs, taps, weights, biases, key_w, value_w,
    key_keep, key_send, value_keep, value_send, col, full,
):
    rows, frames = features.shape
    half = rows // 2
    base = (1 - side[0]) * rows
    full[pl.ds(pl.multiple_of(side[0] * rows, rows), rows), :] = features[...]
    full[pl.ds(pl.multiple_of(base + core[0] * half, half), half), :] = near_rows[...]
    column(biases[layer : layer + 1, :], col)
    here = pl.ds(pl.multiple_of((1 - core[0]) * half, half), half)
    there = pl.ds(pl.multiple_of(base + (1 - core[0]) * half, half), half)

    def store(cols, value):
        full[there, cols] = value

    conv_rows(
        taps, lambda cols: theirs[here, cols], weights, col[here, 0:1], None, store, frames, 256
    )
    for key_out, value_out, part in (
        (key_send, value_send, 1 - core[0]), (key_keep, value_keep, core[0])
    ):
        here = pl.ds(pl.multiple_of(part * half, half), half)
        key_out[...] = dot(key_w[here, :], full[...]).astype(jnp.bfloat16)
        value_out[...] = dot(value_w[here, :], full[...]).T.astype(jnp.bfloat16)


def thirds(value):
    first = value.astype(jnp.bfloat16)
    rest = value - first.astype(jnp.float32)
    second = rest.astype(jnp.bfloat16)
    third = (rest - second.astype(jnp.float32)).astype(jnp.bfloat16)
    return first, second, third


def pack(out, peak, total, weighted):
    out[0:HD, :] = weighted.astype(jnp.bfloat16)
    lines = [line.astype(jnp.float32) for line in thirds(peak) + thirds(total)]
    lines.append(jnp.zeros_like(lines[0]))
    lines.append(jnp.zeros_like(lines[0]))
    out[HD : HD + 8, :] = jnp.concatenate(lines, axis=0).astype(jnp.bfloat16)


def unpack(packed):
    lines = packed[HD : HD + 8, :].astype(jnp.float32)
    peak = lines[0:1] + (lines[1:2] + lines[2:3])
    total = lines[3:4] + (lines[4:5] + lines[5:6])
    return peak, total, packed[0:HD, :].astype(jnp.float32)


SCALE = LOG2E / math.sqrt(HD)


def join(one, two):
    peak = jnp.maximum(one[0], two[0])
    left = jnp.exp2((one[0] - peak) * SCALE)
    right = jnp.exp2((two[0] - peak) * SCALE)
    return peak, one[1] * left + two[1] * right, one[2] * left + two[2] * right


def ordered(info, mine, theirs):
    swap = info[0] == 1
    one = tuple(jnp.where(swap, t, m) for m, t in zip(mine, theirs))
    two = tuple(jnp.where(swap, m, t) for m, t in zip(mine, theirs))
    return one, two


def meet_kernel(peak, total, weighted, *refs):
    state = (peak[...], total[...], weighted[...])
    for theirs in refs[:-1]:
        state = join(state, unpack(theirs))
    pack(refs[-1], *state)


def merge_kernel(info, mine, theirs, out):
    pack(out, *join(*ordered(info, unpack(mine), unpack(theirs))))


def finish_kernel(info, mine, theirs, out):
    _, total, weighted = join(*ordered(info, unpack(mine), unpack(theirs)))
    out[...] = (weighted / total).astype(out.dtype)


def ask_kernel(core, queries, out):
    rows = 2 * HD
    wide = queries[pl.ds(pl.multiple_of(core[0] * rows, rows), rows), :].astype(jnp.float32)
    out[...] = wide.T.astype(out.dtype)


def attend_kernel(
    packed, which, half, valid_own, valid_rec, key_own, key_rec, value_own, value_rec, queries,
    *refs
):
    outs = refs[:-6]
    asked, keyed, values, score_a, score_b, probs_ref = refs[-6:]
    frames = key_own.shape[1]
    latents = asked.shape[0]
    rows = score_a.shape[0]
    chunk = frames // 2
    slot = which[0]
    spare = (1 - slot) * HD
    row = lax.broadcasted_iota(jnp.int32, (2 * HD, frames), 0)
    frame = lax.broadcasted_iota(jnp.int32, (2 * HD, frames), 1)
    for part, (source, valid) in enumerate(((key_own, valid_own), (key_rec, valid_rec))):
        bias = jnp.where(frame < valid[0], 0.0, MASKED).astype(jnp.bfloat16)
        keyed[:, part * frames : (part + 1) * frames] = jnp.where(row == spare, bias, source[...])
    values[0:frames, :] = value_own[...]
    values[frames:, :] = value_rec[...]
    lane = lax.broadcasted_iota(jnp.int32, (latents, 2 * HD), 1)
    fill = jnp.where(lane == spare, 1.0, 0.0).astype(jnp.bfloat16)
    mine = queries[pl.ds(pl.multiple_of(half[0] * latents, latents), latents), :]
    asked[...] = jnp.where(lane // HD == slot, mine, fill)
    lane = lax.broadcasted_iota(jnp.int32, (rows, 2 * HD), 1)
    count = latents // rows
    peak = None
    for step in range(count + 1):
        now, before = ((score_a, score_b), (score_b, score_a))[step % 2]
        top = None
        total = None
        for start in range(0, 2 * frames, chunk):
            here = slice(start, start + chunk)
            if step < count:
                value = dot(asked[step * rows : (step + 1) * rows, :], keyed[:, here])
                now[:, here] = value
                for n in range(0, chunk, EDGE):
                    part = value[:, n : n + EDGE]
                    top = part if top is None else jnp.maximum(top, part)
            if step > 0:
                probs = jnp.exp2((before[:, here] - peak) * SCALE)
                for n in range(0, chunk, EDGE):
                    part = probs[:, n : n + EDGE]
                    total = part if total is None else total + part
                probs_ref[:, here] = probs.astype(jnp.bfloat16)
        if step > 0:
            weighted = dot(probs_ref[...], values[...])
            total = jnp.sum(total, axis=1, keepdims=True)
            both = jnp.where(
                lane == spare, peak, jnp.where(lane == spare + 1, total, weighted)
            ).T
            kept = jnp.where(slot == 0, both[0:HD, :], both[HD:, :])
            rest = jnp.where(slot == 0, both[HD : HD + 8, :], both[0:8, :])
            done = slice((step - 1) * rows, step * rows)
            if packed:
                pack(outs[0].at[:, done], rest[0:1], rest[1:2], kept)
            else:
                outs[0][:, done] = rest[0:1]
                outs[1][:, done] = rest[1:2]
                outs[2][:, done] = kept
        if step < count:
            peak = jnp.max(top, axis=1, keepdims=True)


def attend(packed, scalars, keys, values, queries):
    latents = queries.shape[0] // 2
    frames = keys[0].shape[1]
    rows = min(EDGE, latents)
    if packed:
        out_shape = jax.ShapeDtypeStruct((HD + 8, latents), jnp.bfloat16)
        out_specs = pl.BlockSpec(memory_space=pltpu.VMEM)
    else:
        out_shape = [
            jax.ShapeDtypeStruct((1, latents), jnp.float32),
            jax.ShapeDtypeStruct((1, latents), jnp.float32),
            jax.ShapeDtypeStruct((HD, latents), jnp.float32),
        ]
        out_specs = whole(3)
    return pl.pallas_call(
        functools.partial(attend_kernel, packed),
        out_shape=out_shape,
        in_specs=smem(4) + whole(5),
        out_specs=out_specs,
        scratch_shapes=[
            VMEM((latents, 2 * HD), jnp.bfloat16),
            VMEM((2 * HD, 2 * frames), jnp.bfloat16),
            VMEM((2 * frames, 2 * HD), jnp.bfloat16),
            VMEM((rows, 2 * frames), jnp.float32),
            VMEM((rows, 2 * frames), jnp.float32),
            VMEM((rows, 2 * frames), jnp.bfloat16),
        ],
        compiler_params=params(20),
        name="attend_send" if packed else "attend_keep",
    )(*scalars, *keys, *values, queries)


def assemble_kernel(spots, core, cross, lower, *refs):
    pieces, out, done = refs[: len(spots)], refs[-2], refs[-1]
    latents = pieces[0].shape[1]
    mine, theirs = 2 * core[0], 2 - 2 * core[0]
    heads = (mine + cross[0], mine + 1 - cross[0], theirs + cross[0], theirs + 1 - cross[0])
    copies = []
    for n, (spot, piece) in enumerate(zip(spots, pieces)):
        part = lower[0] if spot % 2 == 0 else 1 - lower[0]
        target = out.at[
            pl.ds(pl.multiple_of(heads[spot // 2] * HD, HD), HD),
            pl.ds(pl.multiple_of(part * latents, latents), latents),
        ]
        copies.append(pltpu.make_async_copy(piece, target, done.at[n]))
    for copy in copies:
        copy.start()
    for copy in copies:
        copy.wait()


def assemble(spots, out_shape, scalars, pieces, into=None):
    extra = [] if into is None else [into]
    call = pl.pallas_call(
        functools.partial(assemble_kernel, spots),
        out_shape=out_shape,
        in_specs=smem(len(scalars)) + whole(len(pieces))
        + [pl.BlockSpec(memory_space=pltpu.HBM)] * len(extra),
        out_specs=pl.BlockSpec(memory_space=pltpu.HBM),
        scratch_shapes=[pltpu.SemaphoreType.DMA((len(spots),))],
        input_output_aliases={len(scalars) + len(pieces): 0} if extra else {},
        compiler_params=params(16),
        name="assemble_rest" if extra else "assemble",
    )
    return call(*scalars, *pieces, *extra)


def simple(kernel, out_shape, scalars, arrays, scratch=(), mib=16, specs=None):
    many = isinstance(out_shape, (list, tuple))
    return pl.pallas_call(
        kernel,
        grid=(1,),
        out_shape=out_shape,
        in_specs=smem(len(scalars)) + (specs or whole(len(arrays))),
        out_specs=whole(len(out_shape)) if many else pl.BlockSpec(memory_space=pltpu.VMEM),
        scratch_shapes=list(scratch),
        compiler_params=params(mib),
    )(*scalars, *arrays)


def pair_device(
    recording, spatial_w, conv_w, conv_b, dilations, valid_frames, key_w, value_w, queries
):
    frames = recording.shape[1]
    ch_loc = conv_w.shape[2]
    ch = conv_w.shape[3]
    half = ch_loc // 2
    latents = queries.shape[1]
    blocks = lax.axis_size("tm")
    side = lax.axis_index("sensor").astype(jnp.int32).reshape(1)
    place = lax.axis_index("tm").astype(jnp.int32).reshape(1)
    core = place & 1
    cross = (place >> 1) & 1
    span = frames + EDGE
    bf16 = jnp.bfloat16
    across = [(0, 1), (1, 0)]
    twins = [(i, i ^ 1) for i in range(blocks)]

    other_rec = lax.ppermute(recording, "sensor", across)
    other_w = lax.ppermute(spatial_w, "sensor", across)
    even = core[0] == 0
    last_part, first_part = recording[:, frames - EDGE :], recording[:, :EDGE]
    links = [(i, i + 1) for i in range(1, blocks - 1, 2)]
    outer = lax.ppermute(
        jnp.where(even, first_part, last_part), "tm",
        links + [(j, i) for i, j in links],
    )
    inner = lax.ppermute(jnp.where(even, last_part, first_part), "tm", twins)
    lane = jnp.arange(EDGE, dtype=jnp.int32)[None, :]
    edge = jnp.where((lane < HALF) == even, inner, outer)
    other_edge = lax.ppermute(edge, "sensor", across)
    other_b = lax.ppermute(conv_b, "sensor", across)
    later_w = lax.optimization_barrier((conv_w, edge))[0]
    mine = [
        lax.dynamic_slice(
            later_w if layer else conv_w, (layer, 0, core[0] * half, 0), (1, 3, half, ch)
        )[0]
        for layer in range(LAYERS)
    ]
    near = [lax.ppermute(mine[n], "sensor", across) for n in range(LAYERS)]
    far = [lax.ppermute(near[n], "tm", twins) for n in range(LAYERS)]
    asked = simple(ask_kernel, jax.ShapeDtypeStruct((latents, half), bf16), (core,), (queries,))
    half_shape = jax.ShapeDtypeStruct((ch_loc, span), bf16)
    fixed = [pltpu.with_memory_space_constraint(v, pltpu.HBM) for v in (spatial_w, recording)]
    parts = (fixed[0], other_w, fixed[1], other_rec, edge, other_edge)
    own_h, other_h = simple(
        first_kernel, [half_shape, half_shape], (side,), parts,
        [VMEM(part.shape, bf16) for part in parts] + [pltpu.SemaphoreType.DMA((len(parts),))],
        specs=[pl.BlockSpec(memory_space=pltpu.HBM)] * len(parts),
    )
    taps_shape = jax.ShapeDtypeStruct((3, ch, span), bf16)
    col = [VMEM((ch_loc, EDGE), jnp.float32)]
    for layer in range(LAYERS):
        last = layer == LAYERS - 1
        specs = whole(4)
        specs[2] = pl.BlockSpec((None, 3, ch_loc, ch), lambda _, layer=layer: (layer, 0, 0, 0))
        made = [jax.ShapeDtypeStruct((ch_loc, frames), bf16)] * 2 if last else [half_shape]
        *own_next, taps = simple(
            functools.partial(own_kernel, layer, blocks, last), made + [taps_shape],
            (dilations, side, place), (own_h, other_h, conv_w, conv_b), col,
            mib=24, specs=specs,
        )
        arrays = (other_h, taps, near[layer], far[layer], other_b)
        if last:
            features, kept_features = own_next
            shapes = [
                jax.ShapeDtypeStruct((half, frames), bf16),
                jax.ShapeDtypeStruct((half, frames), bf16),
                jax.ShapeDtypeStruct((frames, half), bf16),
                jax.ShapeDtypeStruct((frames, half), bf16),
            ]
            near_rows = simple(
                functools.partial(near_kernel, layer), jax.ShapeDtypeStruct((half, frames), bf16),
                (core,), (other_h, taps, near[layer], other_b), col, mib=24,
            )
            key_keep, key_send, value_keep, value_send = simple(
                functools.partial(last_kernel, layer), shapes, (side, core),
                (kept_features, near_rows, other_h, taps, far[layer], other_b, key_w, value_w),
                col + [VMEM((ch, frames), bf16)],
                mib=24,
            )
        else:
            other_h = simple(
                functools.partial(other_kernel, layer, blocks), half_shape, (core, place), arrays,
                col, mib=24,
            )
            own_h = own_next[0]
    keys = (key_keep, lax.ppermute(key_send, "tm", twins))
    values = (value_keep, lax.ppermute(value_send, "tm", twins))
    other_valid = lax.ppermute(valid_frames, "tm", twins)

    def flip(value, bit):
        return lax.ppermute(value, "tm", [(i, i ^ bit) for i in range(blocks)])

    lower = (place >> 2) & 1

    def run(packed, slot, part):
        scalars = (slot, part, valid_frames, other_valid)
        return attend(packed, scalars, keys, values, asked)

    sent = flip(run(True, 1 - cross, 1 - lower), 2)
    kept = flip(run(True, 1 - cross, lower), 2)
    packed_shape = jax.ShapeDtypeStruct((HD + 8, latents // 2), bf16)
    final_shape = jax.ShapeDtypeStruct((HD, latents // 2), bf16)
    given = run(False, cross, 1 - lower)
    given = simple(meet_kernel, packed_shape, (), (*given, sent))
    given = flip(given, 4)
    held = run(False, cross, lower)
    packed = simple(meet_kernel, packed_shape, (), (*held, kept, given))
    bit = 8
    while bit < blocks:
        theirs = flip(packed, bit)
        which = ((place & bit) != 0).astype(jnp.int32)
        if bit * 2 < blocks:
            packed = simple(merge_kernel, packed_shape, (which,), (packed, theirs))
        else:
            done = simple(finish_kernel, final_shape, (which,), (packed, theirs))
        bit *= 2
    above = flip(done, 4)
    beside = flip(done, 2)
    corner = flip(done, 6)
    pieces = [done, above, beside, corner]
    pieces += [flip(piece, 1) for piece in pieces]
    shape = jax.ShapeDtypeStruct((ch_loc, latents), bf16)
    scalars = (core, cross, lower)
    attended = assemble((0, 1, 3, 4, 5, 7), shape, scalars, pieces[:2] + pieces[3:6] + pieces[7:])
    attended = assemble((2, 6), shape, scalars, [pieces[2], pieces[6]], attended)
    return (features, attended)


def fits(mesh):
    sensors, blocks = mesh.shape["sensor"], mesh.shape["tm"]
    return sensors == 2 and blocks >= 16 and blocks & (blocks - 1) == 0


def on_device(*arrays):
    if arrays[6].shape[0] // HD != 4:
        return generic_device(*arrays)
    return pair_device(*arrays)


def solution(mesh):
    quick = fits(mesh)
    return jax.shard_map(
        on_device if quick else generic_device,
        mesh=mesh,
        in_specs=(
            P("sensor", "tm"),
            P(None, "sensor"),
            P(None, None, "sensor", None),
            P(None, "sensor"),
            P(),
            P("tm"),
            P("sensor", None),
            P("sensor", None),
            P("sensor", None),
        ),
        out_specs=(P("sensor", "tm"), P("sensor", None)),
        check_vma=False,
    )
```

```python
import functools
import math

import jax
import jax.numpy as jnp
from jax import lax
from jax.experimental import pallas as pl
from jax.experimental.pallas import tpu as pltpu
from jax.sharding import PartitionSpec as P


HD = 64
LATENTS = 2048
LAYERS = 3
DMAX = 16


def padded(cells, sides, width):
    for axis, dim in sides:
        count = lax.axis_size(axis)
        ends = count - 1
        head = lax.slice_in_dim(cells, 0, width, axis=dim)
        tail = lax.slice_in_dim(cells, cells.shape[dim] - width, cells.shape[dim], axis=dim)
        cells = jnp.concatenate(
            [
                lax.ppermute(tail, axis, [(i, (i + 1) % count) for i in range(ends)]),
                cells,
                lax.ppermute(head, axis, [((i + 1) % count, i) for i in range(ends)]),
            ],
            axis=dim,
        )
    return cells


def tap_folder(kernels, dilation, frames, margin):

    def add_taps(running, portion, first_row):
        portion = jnp.pad(portion, ((0, 0), (margin, margin)))
        for tap_index in range(3):
            kernel = kernels[tap_index]
            offset = DMAX + (tap_index - 1) * dilation
            shifted = lax.dynamic_slice_in_dim(portion, offset, frames, 1)
            running = running + jnp.dot(kernel, shifted, preferred_element_type=jnp.float32)
        return running

    return add_taps


def generic_device(
    recording, spatial_w, conv_w, conv_b, dilations, valid_frames, key_w, value_w, queries
):
    frames = recording.shape[1]
    ch_loc = conv_w.shape[2]
    hidden = lax.psum_scatter(
        jnp.dot(spatial_w, recording, preferred_element_type=jnp.float32),
        "sensor",
        scatter_dimension=0,
        tiled=True,
    ).astype(jnp.bfloat16)
    reach = 3 * DMAX
    extended = padded(hidden, (("tm", 1),), reach)
    span = frames + 2 * reach
    position = lax.axis_index("tm") * frames - reach + jnp.arange(span, dtype=jnp.int32)
    inside = (position >= 0) & (position < frames * lax.axis_size("tm"))
    for layer in range(LAYERS):
        initial = jnp.broadcast_to(conv_b[layer][:, None], (ch_loc, span))
        folder = tap_folder(conv_w[layer], dilations[layer], span, DMAX)
        preact = folder(
            initial, lax.all_gather(extended, "sensor", axis=0, tiled=True), jnp.int32(0)
        )
        updated = extended.astype(jnp.float32) + jax.nn.gelu(preact, approximate=False)
        extended = jnp.where(inside[None, :], updated, 0.0).astype(jnp.bfloat16)
    hidden = extended[:, reach : reach + frames]
    portion = lax.all_gather(hidden, "sensor", axis=0, tiled=True)
    key_rows = jnp.dot(key_w, portion, preferred_element_type=jnp.float32)
    value_rows = jnp.dot(value_w, portion, preferred_element_type=jnp.float32)
    head_count = key_w.shape[0] // HD
    key_heads = key_rows.astype(jnp.bfloat16).reshape(head_count, HD, frames)
    value_heads = value_rows.astype(jnp.bfloat16).reshape(head_count, HD, frames)
    frame_mask = jnp.arange(frames, dtype=jnp.int32) < valid_frames[0]
    block_rows = min(LATENTS, 512)
    block_count = LATENTS // block_rows
    query_blocks = queries.reshape(head_count, HD, block_count, block_rows).transpose(2, 0, 1, 3)
    scale = 1.0 / math.sqrt(HD)

    def attend(query_block):
        scores = (
            jnp.einsum("hdq,hdt->hqt", query_block, key_heads, preferred_element_type=jnp.float32)
            * scale
        )
        scores = jnp.where(frame_mask[None, None, :], scores, -jnp.inf)
        peaks = jnp.max(scores, axis=2)
        probs = jnp.where(frame_mask[None, None, :], jnp.exp(scores - peaks[:, :, None]), 0.0)
        totals = jnp.sum(probs, axis=2)
        weighted = jnp.einsum(
            "hqt,hdt->hdq",
            probs.astype(jnp.bfloat16),
            value_heads,
            preferred_element_type=jnp.float32,
        )
        return (peaks, totals, weighted)

    peaks, totals, weighted = lax.map(attend, query_blocks)
    peaks = peaks.transpose(1, 0, 2).reshape(head_count, LATENTS)
    totals = totals.transpose(1, 0, 2).reshape(head_count, LATENTS)
    weighted = weighted.transpose(1, 2, 0, 3).reshape(head_count, HD, LATENTS)
    global_peaks = lax.pmax(peaks, "tm")
    rescale = jnp.exp(peaks - global_peaks)
    totals, weighted = lax.psum((totals * rescale, weighted * rescale[:, None, :]), "tm")
    attended = (
        (weighted / totals[:, None, :]).reshape(head_count * HD, LATENTS).astype(jnp.bfloat16)
    )
    return (hidden, attended)


VMEM = pltpu.VMEM
EDGE = 128
HALF = EDGE // 2
LOG2E = 1.4426950408889634
MASKED = -1e30


def whole(count):
    return [pl.BlockSpec(memory_space=pltpu.VMEM)] * count


def smem(count):
    return [pl.BlockSpec(memory_space=pltpu.SMEM)] * count


def params(mib):
    return pltpu.CompilerParams(vmem_limit_bytes=mib * 1024 * 1024)


def dot(left, right):
    return jnp.dot(left, right, preferred_element_type=jnp.float32)


def first_kernel(side, *refs):
    sources, (mine, theirs), held, done = refs[:6], refs[6:8], refs[8:14], refs[14]
    copies = [
        pltpu.make_async_copy(source, target, done.at[n])
        for n, (source, target) in enumerate(zip(sources, held))
    ]
    for copy in copies:
        copy.start()
    for copy in copies:
        copy.wait()
    own_w, other_w, own, other, own_edge, other_edge = held
    frames = own.shape[1]
    rows = mine.shape[0]
    for out, part in ((mine, side[0]), (theirs, 1 - side[0])):
        here = pl.ds(pl.multiple_of(part * rows, rows), rows)
        left, right = own_w[here, :], other_w[here, :]
        out[:, :frames] = (dot(left, own[...]) + dot(right, other[...])).astype(out.dtype)
        out[:, frames:] = (dot(left, own_edge[...]) + dot(right, other_edge[...])).astype(out.dtype)


def gelu(value):
    return 0.5 * value * (1.0 + lax.erf(value * (1.0 / math.sqrt(2.0))))


def conv_rows(taps, old, kernel, bias, keep, store, cols, step):
    for start in range(0, cols, step):
        width = min(step, cols - start)
        here = pl.ds(start, width)
        total = dot(kernel[0], taps[0, :, here])
        total = total + dot(kernel[1], taps[1, :, here])
        total = total + dot(kernel[2], taps[2, :, here])
        new = old(here).astype(jnp.float32) + gelu(total + bias)
        if keep is not None and start + width > cols - EDGE:
            new = jnp.where(keep(start, width), new, 0.0)
        store(here, new.astype(jnp.bfloat16))


def column(row, out):
    out[...] = jnp.broadcast_to(row, (EDGE, row.shape[1])).T


def keeper(place, blocks, span):
    frames = span - EDGE

    def keep(start, width):
        lane = lax.broadcasted_iota(jnp.int32, (1, width), 1) + start
        frame = jnp.where(lane < span - HALF, lane, lane - span) + place[0] * frames
        return (frame >= 0) & (frame < blocks * frames)

    return keep


def own_kernel(
    layer, blocks, last, dilations, side, place, mine, theirs, weights, biases, *refs
):
    outs, taps, col = refs[:-2], refs[-2], refs[-1]
    out = outs[0]
    rows, span = mine.shape
    shift = dilations[layer]
    lane = lax.broadcasted_iota(jnp.int32, (rows, EDGE), 1)
    count = span // EDGE
    for part, source in ((side[0], mine), (1 - side[0], theirs)):
        here = pl.ds(pl.multiple_of(part * rows, rows), rows)
        tiles = [source[:, n * EDGE : (n + 1) * EDGE] for n in range(count)]
        later = [pltpu.roll(tile, shift, 1) for tile in tiles]
        sooner = [pltpu.roll(tile, EDGE - shift, 1) for tile in tiles]
        for n in range(count):
            cols = slice(n * EDGE, (n + 1) * EDGE)
            taps[1, here, cols] = tiles[n]
            taps[0, here, cols] = jnp.where(lane < shift, later[n - 1], later[n])
            taps[2, here, cols] = jnp.where(
                lane < EDGE - shift, sooner[n], sooner[(n + 1) % count]
            )
    column(biases[layer : layer + 1, :], col)

    def store(here, value):
        for target in outs:
            target[:, here] = value

    conv_rows(
        taps, lambda here: mine[:, here], weights, col[:, 0:1],
        None if last else keeper(place, blocks, span), store, out.shape[1], 256 if last else 384,
    )


def other_rows(layer, core, theirs, taps, near_w, far_w, biases, col, keep, target, cols, step):
    half = near_w.shape[1]
    column(biases[layer : layer + 1, :], col)
    for weights, part in ((near_w, core[0]), (far_w, 1 - core[0])):
        rows = pl.ds(pl.multiple_of(part * half, half), half)

        def store(here, value, rows=rows):
            target(rows, here, value)

        conv_rows(
            taps, lambda here, rows=rows: theirs[rows, here], weights, col[rows, 0:1], keep,
            store, cols, step,
        )


def other_kernel(layer, blocks, core, place, theirs, taps, near_w, far_w, biases, out, col):
    span = theirs.shape[1]

    def target(rows, here, value):
        out[rows, here] = value

    other_rows(
        layer, core, theirs, taps, near_w, far_w, biases, col, keeper(place, blocks, span), target,
        span, 384,
    )


def near_kernel(layer, core, theirs, taps, weights, biases, out, col):
    rows, frames = out.shape
    column(biases[layer : layer + 1, :], col)
    here = pl.ds(pl.multiple_of(core[0] * rows, rows), rows)

    def store(cols, value):
        out[:, cols] = value

    conv_rows(
        taps, lambda cols: theirs[here, cols], weights, col[here, 0:1], None, store, frames, 256
    )


def last_kernel(
    layer, side, core, features, near_rows, theirs, taps, weights, biases, key_w, value_w,
    key_keep, key_send, value_keep, value_send, col, full,
):
    rows, frames = features.shape
    half = rows // 2
    base = (1 - side[0]) * rows
    full[pl.ds(pl.multiple_of(side[0] * rows, rows), rows), :] = features[...]
    full[pl.ds(pl.multiple_of(base + core[0] * half, half), half), :] = near_rows[...]
    column(biases[layer : layer + 1, :], col)
    here = pl.ds(pl.multiple_of((1 - core[0]) * half, half), half)
    there = pl.ds(pl.multiple_of(base + (1 - core[0]) * half, half), half)

    def store(cols, value):
        full[there, cols] = value

    conv_rows(
        taps, lambda cols: theirs[here, cols], weights, col[here, 0:1], None, store, frames, 256
    )
    for key_out, value_out, part in (
        (key_send, value_send, 1 - core[0]), (key_keep, value_keep, core[0])
    ):
        here = pl.ds(pl.multiple_of(part * half, half), half)
        key_out[...] = dot(key_w[here, :], full[...]).astype(jnp.bfloat16)
        value_out[...] = dot(value_w[here, :], full[...]).T.astype(jnp.bfloat16)


def thirds(value):
    first = value.astype(jnp.bfloat16)
    rest = value - first.astype(jnp.float32)
    second = rest.astype(jnp.bfloat16)
    third = (rest - second.astype(jnp.float32)).astype(jnp.bfloat16)
    return first, second, third


def pack(out, peak, total, weighted):
    out[0:HD, :] = weighted.astype(jnp.bfloat16)
    lines = [line.astype(jnp.float32) for line in thirds(peak) + thirds(total)]
    lines.append(jnp.zeros_like(lines[0]))
    lines.append(jnp.zeros_like(lines[0]))
    out[HD : HD + 8, :] = jnp.concatenate(lines, axis=0).astype(jnp.bfloat16)


def unpack(packed):
    lines = packed[HD : HD + 8, :].astype(jnp.float32)
    peak = lines[0:1] + (lines[1:2] + lines[2:3])
    total = lines[3:4] + (lines[4:5] + lines[5:6])
    return peak, total, packed[0:HD, :].astype(jnp.float32)


SCALE = LOG2E / math.sqrt(HD)


def join(one, two):
    peak = jnp.maximum(one[0], two[0])
    left = jnp.exp2((one[0] - peak) * SCALE)
    right = jnp.exp2((two[0] - peak) * SCALE)
    return peak, one[1] * left + two[1] * right, one[2] * left + two[2] * right


def ordered(info, mine, theirs):
    swap = info[0] == 1
    one = tuple(jnp.where(swap, t, m) for m, t in zip(mine, theirs))
    two = tuple(jnp.where(swap, m, t) for m, t in zip(mine, theirs))
    return one, two


def meet_kernel(peak, total, weighted, *refs):
    state = (peak[...], total[...], weighted[...])
    for theirs in refs[:-1]:
        state = join(state, unpack(theirs))
    pack(refs[-1], *state)


def merge_kernel(info, mine, theirs, out):
    pack(out, *join(*ordered(info, unpack(mine), unpack(theirs))))


def finish_kernel(info, mine, theirs, out):
    _, total, weighted = join(*ordered(info, unpack(mine), unpack(theirs)))
    out[...] = (weighted / total).astype(out.dtype)


def ask_kernel(core, queries, out):
    rows = 2 * HD
    wide = queries[pl.ds(pl.multiple_of(core[0] * rows, rows), rows), :].astype(jnp.float32)
    out[...] = wide.T.astype(out.dtype)


def attend_kernel(
    packed, which, half, valid_own, valid_rec, key_own, key_rec, value_own, value_rec, queries,
    *refs
):
    outs = refs[:-6]
    asked, keyed, values, score_a, score_b, probs_ref = refs[-6:]
    frames = key_own.shape[1]
    latents = asked.shape[0]
    rows = score_a.shape[0]
    chunk = frames
    slot = which[0]
    spare = (1 - slot) * HD
    row = lax.broadcasted_iota(jnp.int32, (2 * HD, frames), 0)
    frame = lax.broadcasted_iota(jnp.int32, (2 * HD, frames), 1)
    for part, (source, valid) in enumerate(((key_own, valid_own), (key_rec, valid_rec))):
        bias = jnp.where(frame < valid[0], 0.0, MASKED).astype(jnp.bfloat16)
        keyed[:, part * frames : (part + 1) * frames] = jnp.where(row == spare, bias, source[...])
    values[0:frames, :] = value_own[...]
    values[frames:, :] = value_rec[...]
    lane = lax.broadcasted_iota(jnp.int32, (latents, 2 * HD), 1)
    fill = jnp.where(lane == spare, 1.0, 0.0).astype(jnp.bfloat16)
    mine = queries[pl.ds(pl.multiple_of(half[0] * latents, latents), latents), :]
    asked[...] = jnp.where(lane // HD == slot, mine, fill)
    lane = lax.broadcasted_iota(jnp.int32, (rows, 2 * HD), 1)
    count = latents // rows
    peak = None
    for step in range(count + 1):
        now, before = ((score_a, score_b), (score_b, score_a))[step % 2]
        top = None
        total = None
        for start in range(0, 2 * frames, chunk):
            here = slice(start, start + chunk)
            if step < count:
                value = dot(asked[step * rows : (step + 1) * rows, :], keyed[:, here])
                now[:, here] = value
                for n in range(0, chunk, EDGE):
                    part = value[:, n : n + EDGE]
                    top = part if top is None else jnp.maximum(top, part)
            if step > 0:
                probs = jnp.exp2((before[:, here] - peak) * SCALE)
                for n in range(0, chunk, EDGE):
                    part = probs[:, n : n + EDGE]
                    total = part if total is None else total + part
                probs_ref[:, here] = probs.astype(jnp.bfloat16)
        if step > 0:
            weighted = dot(probs_ref[...], values[...])
            total = jnp.sum(total, axis=1, keepdims=True)
            both = jnp.where(
                lane == spare, peak, jnp.where(lane == spare + 1, total, weighted)
            ).T
            kept = jnp.where(slot == 0, both[0:HD, :], both[HD:, :])
            rest = jnp.where(slot == 0, both[HD : HD + 8, :], both[0:8, :])
            done = slice((step - 1) * rows, step * rows)
            if packed:
                pack(outs[0].at[:, done], rest[0:1], rest[1:2], kept)
            else:
                outs[0][:, done] = rest[0:1]
                outs[1][:, done] = rest[1:2]
                outs[2][:, done] = kept
        if step < count:
            peak = jnp.max(top, axis=1, keepdims=True)


def attend(packed, scalars, keys, values, queries):
    latents = queries.shape[0] // 2
    frames = keys[0].shape[1]
    rows = min(EDGE, latents)
    if packed:
        out_shape = jax.ShapeDtypeStruct((HD + 8, latents), jnp.bfloat16)
        out_specs = pl.BlockSpec(memory_space=pltpu.VMEM)
    else:
        out_shape = [
            jax.ShapeDtypeStruct((1, latents), jnp.float32),
            jax.ShapeDtypeStruct((1, latents), jnp.float32),
            jax.ShapeDtypeStruct((HD, latents), jnp.float32),
        ]
        out_specs = whole(3)
    return pl.pallas_call(
        functools.partial(attend_kernel, packed),
        out_shape=out_shape,
        in_specs=smem(4) + whole(5),
        out_specs=out_specs,
        scratch_shapes=[
            VMEM((latents, 2 * HD), jnp.bfloat16),
            VMEM((2 * HD, 2 * frames), jnp.bfloat16),
            VMEM((2 * frames, 2 * HD), jnp.bfloat16),
            VMEM((rows, 2 * frames), jnp.float32),
            VMEM((rows, 2 * frames), jnp.float32),
            VMEM((rows, 2 * frames), jnp.bfloat16),
        ],
        compiler_params=params(20),
        name="attend_send" if packed else "attend_keep",
    )(*scalars, *keys, *values, queries)


def assemble_kernel(spots, core, cross, lower, *refs):
    pieces, out, done = refs[: len(spots)], refs[-2], refs[-1]
    latents = pieces[0].shape[1]
    mine, theirs = 2 * core[0], 2 - 2 * core[0]
    heads = (mine + cross[0], mine + 1 - cross[0], theirs + cross[0], theirs + 1 - cross[0])
    copies = []
    for n, (spot, piece) in enumerate(zip(spots, pieces)):
        part = lower[0] if spot % 2 == 0 else 1 - lower[0]
        target = out.at[
            pl.ds(pl.multiple_of(heads[spot // 2] * HD, HD), HD),
            pl.ds(pl.multiple_of(part * latents, latents), latents),
        ]
        copies.append(pltpu.make_async_copy(piece, target, done.at[n]))
    for copy in copies:
        copy.start()
    for copy in copies:
        copy.wait()


def assemble(spots, out_shape, scalars, pieces, into=None):
    extra = [] if into is None else [into]
    call = pl.pallas_call(
        functools.partial(assemble_kernel, spots),
        out_shape=out_shape,
        in_specs=smem(len(scalars)) + whole(len(pieces))
        + [pl.BlockSpec(memory_space=pltpu.HBM)] * len(extra),
        out_specs=pl.BlockSpec(memory_space=pltpu.HBM),
        scratch_shapes=[pltpu.SemaphoreType.DMA((len(spots),))],
        input_output_aliases={len(scalars) + len(pieces): 0} if extra else {},
        compiler_params=params(16),
        name="assemble_rest" if extra else "assemble",
    )
    return call(*scalars, *pieces, *extra)


def simple(kernel, out_shape, scalars, arrays, scratch=(), mib=16, specs=None):
    many = isinstance(out_shape, (list, tuple))
    return pl.pallas_call(
        kernel,
        grid=(1,),
        out_shape=out_shape,
        in_specs=smem(len(scalars)) + (specs or whole(len(arrays))),
        out_specs=whole(len(out_shape)) if many else pl.BlockSpec(memory_space=pltpu.VMEM),
        scratch_shapes=list(scratch),
        compiler_params=params(mib),
    )(*scalars, *arrays)


def pair_device(
    recording, spatial_w, conv_w, conv_b, dilations, valid_frames, key_w, value_w, queries
):
    frames = recording.shape[1]
    ch_loc = conv_w.shape[2]
    ch = conv_w.shape[3]
    half = ch_loc // 2
    latents = queries.shape[1]
    blocks = lax.axis_size("tm")
    side = lax.axis_index("sensor").astype(jnp.int32).reshape(1)
    place = lax.axis_index("tm").astype(jnp.int32).reshape(1)
    core = place & 1
    cross = (place >> 1) & 1
    span = frames + EDGE
    bf16 = jnp.bfloat16
    across = [(0, 1), (1, 0)]
    twins = [(i, i ^ 1) for i in range(blocks)]

    other_rec = lax.ppermute(recording, "sensor", across)
    other_w = lax.ppermute(spatial_w, "sensor", across)
    even = core[0] == 0
    last_part, first_part = recording[:, frames - EDGE :], recording[:, :EDGE]
    links = [(i, i + 1) for i in range(1, blocks - 1, 2)]
    outer = lax.ppermute(
        jnp.where(even, first_part, last_part), "tm",
        links + [(j, i) for i, j in links],
    )
    inner = lax.ppermute(jnp.where(even, last_part, first_part), "tm", twins)
    lane = jnp.arange(EDGE, dtype=jnp.int32)[None, :]
    edge = jnp.where((lane < HALF) == even, inner, outer)
    other_edge = lax.ppermute(edge, "sensor", across)
    other_b = lax.ppermute(conv_b, "sensor", across)
    later_w = lax.optimization_barrier((conv_w, edge))[0]
    mine = [
        lax.dynamic_slice(
            later_w if layer else conv_w, (layer, 0, core[0] * half, 0), (1, 3, half, ch)
        )[0]
        for layer in range(LAYERS)
    ]
    near = [lax.ppermute(mine[n], "sensor", across) for n in range(LAYERS)]
    far = [lax.ppermute(near[n], "tm", twins) for n in range(LAYERS)]
    asked = simple(ask_kernel, jax.ShapeDtypeStruct((latents, half), bf16), (core,), (queries,))
    half_shape = jax.ShapeDtypeStruct((ch_loc, span), bf16)
    fixed = [pltpu.with_memory_space_constraint(v, pltpu.HBM) for v in (spatial_w, recording)]
    parts = (fixed[0], other_w, fixed[1], other_rec, edge, other_edge)
    own_h, other_h = simple(
        first_kernel, [half_shape, half_shape], (side,), parts,
        [VMEM(part.shape, bf16) for part in parts] + [pltpu.SemaphoreType.DMA((len(parts),))],
        specs=[pl.BlockSpec(memory_space=pltpu.HBM)] * len(parts),
    )
    taps_shape = jax.ShapeDtypeStruct((3, ch, span), bf16)
    col = [VMEM((ch_loc, EDGE), jnp.float32)]
    for layer in range(LAYERS):
        last = layer == LAYERS - 1
        specs = whole(4)
        specs[2] = pl.BlockSpec((None, 3, ch_loc, ch), lambda _, layer=layer: (layer, 0, 0, 0))
        made = [jax.ShapeDtypeStruct((ch_loc, frames), bf16)] * 2 if last else [half_shape]
        *own_next, taps = simple(
            functools.partial(own_kernel, layer, blocks, last), made + [taps_shape],
            (dilations, side, place), (own_h, other_h, conv_w, conv_b), col,
            mib=24, specs=specs,
        )
        arrays = (other_h, taps, near[layer], far[layer], other_b)
        if last:
            features, kept_features = own_next
            shapes = [
                jax.ShapeDtypeStruct((half, frames), bf16),
                jax.ShapeDtypeStruct((half, frames), bf16),
                jax.ShapeDtypeStruct((frames, half), bf16),
                jax.ShapeDtypeStruct((frames, half), bf16),
            ]
            near_rows = simple(
                functools.partial(near_kernel, layer), jax.ShapeDtypeStruct((half, frames), bf16),
                (core,), (other_h, taps, near[layer], other_b), col, mib=24,
            )
            key_keep, key_send, value_keep, value_send = simple(
                functools.partial(last_kernel, layer), shapes, (side, core),
                (kept_features, near_rows, other_h, taps, far[layer], other_b, key_w, value_w),
                col + [VMEM((ch, frames), bf16)],
                mib=24,
            )
        else:
            other_h = simple(
                functools.partial(other_kernel, layer, blocks), half_shape, (core, place), arrays,
                col, mib=24,
            )
            own_h = own_next[0]
    keys = (key_keep, lax.ppermute(key_send, "tm", twins))
    values = (value_keep, lax.ppermute(value_send, "tm", twins))
    other_valid = lax.ppermute(valid_frames, "tm", twins)

    def flip(value, bit):
        return lax.ppermute(value, "tm", [(i, i ^ bit) for i in range(blocks)])

    lower = (place >> 2) & 1

    def run(packed, slot, part):
        scalars = (slot, part, valid_frames, other_valid)
        return attend(packed, scalars, keys, values, asked)

    sent = flip(run(True, 1 - cross, 1 - lower), 2)
    kept = flip(run(True, 1 - cross, lower), 2)
    packed_shape = jax.ShapeDtypeStruct((HD + 8, latents // 2), bf16)
    final_shape = jax.ShapeDtypeStruct((HD, latents // 2), bf16)
    given = run(False, cross, 1 - lower)
    given = simple(meet_kernel, packed_shape, (), (*given, sent))
    given = flip(given, 4)
    held = run(False, cross, lower)
    packed = simple(meet_kernel, packed_shape, (), (*held, kept, given))
    bit = 8
    while bit < blocks:
        theirs = flip(packed, bit)
        which = ((place & bit) != 0).astype(jnp.int32)
        if bit * 2 < blocks:
            packed = simple(merge_kernel, packed_shape, (which,), (packed, theirs))
        else:
            done = simple(finish_kernel, final_shape, (which,), (packed, theirs))
        bit *= 2
    above = flip(done, 4)
    beside = flip(done, 2)
    corner = flip(done, 6)
    pieces = [done, above, beside, corner]
    pieces += [flip(piece, 1) for piece in pieces]
    shape = jax.ShapeDtypeStruct((ch_loc, latents), bf16)
    scalars = (core, cross, lower)
    attended = assemble((0, 1, 2, 4, 5, 6), shape, scalars, pieces[:3] + pieces[4:7])
    attended = assemble((3, 7), shape, scalars, [pieces[3], pieces[7]], attended)
    return (features, attended)


def fits(mesh):
    sensors, blocks = mesh.shape["sensor"], mesh.shape["tm"]
    return sensors == 2 and blocks >= 16 and blocks & (blocks - 1) == 0


def on_device(*arrays):
    if arrays[6].shape[0] // HD != 4:
        return generic_device(*arrays)
    return pair_device(*arrays)


def solution(mesh):
    quick = fits(mesh)
    return jax.shard_map(
        on_device if quick else generic_device,
        mesh=mesh,
        in_specs=(
            P("sensor", "tm"),
            P(None, "sensor"),
            P(None, None, "sensor", None),
            P(None, "sensor"),
            P(),
            P("tm"),
            P("sensor", None),
            P("sensor", None),
            P("sensor", None),
        ),
        out_specs=(P("sensor", "tm"), P("sensor", None)),
        check_vma=False,
    )
```
